32 devices in a mesh: clips: 2 (over x), lon: 16 (over z, y, core).
Axes of the slice: x: 2, y: 2, z: 4, core: 2. Of those that a mesh axis runs over, the one named last changes fastest.
Arguments:
- video_span: bfloat16 [2, 180, 128, 192], P(None, 'clips', 'lon'), parts along dimension 1, may hold values from -6 to 6
- caches: bfloat16 [3, 2, 180, 128, 192], P(None, None, 'clips', 'lon'), parts along dimension 2, may hold values from -0.25 to 1.5
- norm_gains: float32 [3, 192], replicated, may hold values from 0.5 to 1.5
- shifts: float32 [3, 192], replicated, may hold values from -0.5 to 0.5
- weights: bfloat16 [3, 5184, 192], replicated, may hold values from -0.078125 to 0.078125
- biases: float32 [3, 192], replicated, may hold values from -0.5 to 0.5
Outputs:
- encoded: bfloat16 [2, 180, 128, 192], P(None, 'clips', 'lon'), parts along dimension 1
- carried_frames: bfloat16 [3, 2, 180, 128, 192], P(None, None, 'clips', 'lon'), parts along dimension 2
The draws below stay inside these ranges and needn't reach their ends.
There are 2 independent parts, one for each index of `clips`. The reference program is written for one: setup_inputs(seed, part) draws one part's arguments, and reference() takes and returns one part's arrays. A program takes and returns all parts, laid end to end along the dimension named above; an argument that names none is the same for every part. Nothing has to cross between parts.
All inputs are finite; a program needn't handle non-finite values.
Results may differ from the reference program's by a relative error of at most 0.0031.
Values may be sent and summed in bfloat16 or wider, within the bound.
No kernel may reach another device: no remote copies, remote signals or barrier semaphores. Data moves between devices by JAX's collectives and lax.ppermute only.
A program may use at most 192 MiB of HBM per device.

```python
import jax
import jax.numpy as jnp
from jax import lax

C = 192
GROUPS = 32
LAYERS = 3
FRAMES = 2
H_ROWS = 90
NLON = 128


def draw_video_span(key, part):
    key_base, key_offset = jax.random.split(key, 2)
    position = jnp.arange(NLON, dtype=jnp.float32) / max(NLON - 1, 1)
    base_noise = jax.random.normal(key_base, (FRAMES, H_ROWS, NLON, C), jnp.float32)
    spread = 0.6 + 0.6 * position
    offset = 0.5 * jax.random.normal(key_offset, (C,), jnp.float32)
    ramp_level = 0.3 + 0.7 * position
    tensor = base_noise * spread[None, None, :, None] + offset[None, None, None, :] * ramp_level[None, None, :, None]
    return jnp.clip(tensor, -6.0, 6.0).astype(jnp.bfloat16)


def shard_levels(own_key, extent, cuts, smallest, top_value):
    loudness = 1.0
    for dim, parts in cuts:
        heights = jax.random.uniform(jax.random.fold_in(jax.random.fold_in(own_key, 6), dim), (parts,), jnp.float32, smallest / len(cuts), top_value / len(cuts))
        loudness = loudness * jnp.repeat(jnp.exp(heights), extent[dim] // parts).reshape((-1,) + (1,) * (len(extent) - 1 - dim))
    return loudness


def scatter_about(stream_key, dims, scale, bound, held_as=jnp.bfloat16):
    values = jax.random.normal(stream_key, dims, jnp.float32) * scale
    return jnp.minimum(jnp.maximum(values, -bound), bound).astype(held_as)


def setup_inputs(seed: int = 0, part: int = 0) -> dict:
    key_of = jax.random.split(jax.random.key(seed), 7)
    part_keys = jax.random.split(jax.random.fold_in(key_of[6], part), 7)
    return {
        "video_span": draw_video_span(jax.random.fold_in(jax.random.fold_in(key_of[6], part), 71), part),
        "caches": jnp.clip(-0.25 + 1.75 * jax.random.uniform(part_keys[1], (LAYERS, 2, H_ROWS, NLON, C), jnp.float32) ** shard_levels(part_keys[1], (LAYERS, 2, H_ROWS, NLON, C), ((3, 16),), -0.2, 0.2), -0.25, 1.5).astype(jnp.bfloat16),
        "norm_gains": jnp.clip(jax.random.uniform(key_of[2], (LAYERS, C), jnp.float32, 0.5, 1.5), 0.5, 1.5),
        "shifts": jnp.clip(jax.random.uniform(key_of[3], (LAYERS, C), jnp.float32, -0.5, 0.5), -0.5, 0.5),
        "weights": scatter_about(key_of[4], (LAYERS, 27 * C, C), (27 * C) ** -0.5, 0.078125),
        "biases": jnp.clip(jax.random.uniform(key_of[5], (LAYERS, C), jnp.float32, -0.5, 0.5), -0.5, 0.5),
    }


epsilon = 1e-06

def activate(tensor, norm_gain, norm_shift):
    members = tensor.shape[-1] // GROUPS
    grouped = tensor.reshape(tensor.shape[:-1] + (GROUPS, members))
    average = lax.optimization_barrier(jnp.mean(grouped, axis=(0, 1, 2, 4), keepdims=True))
    centered = grouped - average
    variance = lax.optimization_barrier(jnp.mean(centered * centered, axis=(0, 1, 2, 4), keepdims=True))
    normed = (centered * lax.rsqrt(variance + epsilon)).reshape(tensor.shape)
    return jax.nn.silu(normed * norm_gain + norm_shift).astype(jnp.bfloat16)

def convolve(padded, kernel, offset):
    frames_out = padded.shape[0] - 2
    lat_rows = padded.shape[1] - 2
    columns = padded.shape[2] - 2
    channels = padded.shape[3]
    accumulated = jnp.zeros((frames_out, lat_rows, columns, channels), jnp.float32)
    for tap_index in range(27):
        step_t = tap_index // 9
        step_h = tap_index // 3 % 3
        step_w = tap_index % 3
        window = padded[step_t:step_t + frames_out, step_h:step_h + lat_rows, step_w:step_w + columns]
        product = jnp.dot(window.reshape(-1, channels), kernel[tap_index * channels:(tap_index + 1) * channels], preferred_element_type=jnp.float32)
        accumulated = accumulated + product.reshape(accumulated.shape)
    return accumulated + offset

def reference(video_span, caches, norm_gains, shifts, weights, biases):
    source = video_span.astype(jnp.float32)
    carried = []

    def apply_section(tensor, section_index):
        activation = activate(tensor, norm_gains[section_index], shifts[section_index])
        joined = jnp.concatenate([caches[section_index], activation], axis=0)
        carried.append(joined[-2:])
        padded = jnp.pad(joined, ((0, 0), (1, 1), (0, 0), (0, 0)))
        padded = jnp.concatenate([padded[:, :, -1:], padded, padded[:, :, :1]], axis=2)
        return convolve(padded, weights[section_index], biases[section_index])
    hidden_one = apply_section(source, 0)
    hidden_two = apply_section(hidden_one, 1)
    middle = source + hidden_two
    hidden_three = apply_section(middle, 2)
    return ((middle + hidden_three).astype(jnp.bfloat16), jnp.stack(carried))
```

```python
import functools

import jax
import jax.numpy as jnp
from jax import lax
from jax.experimental import pallas as pl
from jax.experimental.pallas import tpu as pltpu
from jax.sharding import PartitionSpec as P

GROUPS = 32
EPSILON = 1e-06
LANES = 128
COLS = 8
SLABS = 10
VMEM = pl.BlockSpec(memory_space=pltpu.VMEM)
ANY = pl.BlockSpec(memory_space=pl.ANY)


def silu(u):
    return u * (0.5 + 0.5 * jnp.tanh(0.5 * u))


def twice(v):
    return jnp.concatenate([v, v], axis=-1)


def pair(a, b):
    return jnp.concatenate([a, b], axis=0).astype(jnp.bfloat16)


def build_slabs(rows, row_of, edge_of, slab):
    lane = lax.broadcasted_iota(jnp.int32, (COLS, LANES), 1)
    low = lane < LANES // 2
    column = lax.broadcasted_iota(jnp.int32, (COLS, LANES), 0)
    first, last = column == 0, column == COLS - 1
    zero = jnp.zeros((COLS, LANES), jnp.float32)

    def shifted(h):
        out = []
        for part, value in enumerate(row_of(h)):
            left, right = edge_of(h, part)
            out.append(
                (
                    jnp.where(first, left, pltpu.roll(value, 1, 0)),
                    value,
                    jnp.where(last, right, pltpu.roll(value, COLS - 1, 0)),
                )
            )
        main, rest = out
        return main + (jnp.where(low, rest[0], rest[1]), rest[2])

    def put(index, k, value):
        start = k * 16 if isinstance(k, int) else pl.multiple_of(k * 16, 16)
        slab[index, pl.ds(start, 16), :] = value

    def step(k, carry):
        before, older, oldest = carry
        one, two = shifted(2 * k), shifted(2 * k + 1)
        for r in range(3):
            put(r, k, pair(one[r], two[r]))
            put(3 + r, k, pair(before[r], one[r]))
        put(6, k, pair(one[3], two[3]))
        put(7, k, pair(before[3], one[3]))
        put(9, k, pair(one[4], two[4]))

        if older is not None:
            put(8, k - 1, pair(jnp.where(low, oldest, before[4]), jnp.where(low, older, one[4])))

        return two, one[4], before[4]

    count = rows // 2
    begun = step(0, ((zero,) * 5, None, None))
    before, older, oldest = lax.fori_loop(1, count, step, begun, unroll=4)
    for r in range(3):
        put(3 + r, count, pair(before[r], zero))
    put(7, count, pair(before[3], zero))
    put(8, count - 1, pair(jnp.where(low, oldest, before[4]), jnp.where(low, older, zero)))


def slab_rows(slab, start, size):
    def at(index, step=0):
        return slab[index, pl.ds(start + step, size), :]

    tiles = [at(3 + r) for r in range(3)] + [at(r) for r in range(3)]
    tiles += [at(3 + r, 16) for r in range(3)]
    tiles += [at(7), at(6), at(7, 16), at(8), at(9)]
    return jnp.concatenate(tiles, axis=1)


def tap_rows(weight, layer, tap_t, channels):
    def at(q, r, start, size):
        return weight[layer, pl.ds(((tap_t * 3 + q) * 3 + r) * channels + start, size), :]

    half = LANES // 2
    tiles = [at(q, r, 0, LANES) for q in range(3) for r in range(3)]
    for q in range(3):
        tiles += [at(q, 0, LANES, half), at(q, 1, LANES, half)]
    tiles += [at(0, 2, LANES, half), at(2, 2, LANES, half), at(1, 2, LANES, half)]
    tiles.append(jnp.zeros((half, weight.shape[2]), weight.dtype))
    return jnp.concatenate(tiles, axis=0)


def product(slab, start, size, weight):
    return jnp.dot(slab_rows(slab, start, size), weight, preferred_element_type=jnp.float32)


def cached_kernel(chunk, cache, before, after, weight, bias, out, edges, slab):
    layers, frames, rows, cols, channels = cache.shape
    for layer in range(layers):
        for frame in range(frames):
            for side, ref in enumerate((before, after)):
                value = ref[layer, frame].astype(jnp.float32)
                edges[side, 0, frame] = value[:, :LANES]
                edges[side, 1, frame] = twice(value[:, LANES:])

            def row_of(h, frame=frame):
                value = cache[layer, frame, h].astype(jnp.float32)
                return value[:, :LANES], twice(value[:, LANES:])

            def edge_of(h, part, frame=frame):
                return [edges[side, part, frame, pl.ds(h, COLS, stride=0), :] for side in (0, 1)]

            build_slabs(rows, row_of, edge_of, slab.at[frame])
        taps = [tap_rows(weight, layer, p, channels) for p in range(2)]
        for i in range(rows * cols // chunk):
            start = i * chunk
            here = pl.ds(start, chunk)
            out[layer, 0, here, :] = (
                product(slab.at[0], start, chunk, taps[0])
                + product(slab.at[1], start, chunk, taps[1])
                + bias[layer : layer + 1, :]
            )
            out[layer, 1, here, :] = (
                product(slab.at[1], start, chunk, taps[0]) + bias[layer : layer + 1, :]
            )


def halves(value):
    return value[..., :LANES], value[..., LANES:]


def active_kernel(layer, chunk, entries, final, *refs):
    x, before, after, stats, gain, shift, weight, part = refs[:8]
    rest = refs[8:]
    residual = None
    if layer == 1:
        residual, *rest = rest
    if layer > 0:
        _, *rest = rest
    if final:
        y, carried, edges, slab, kept, sem = rest
    else:
        y, carried, sums, first, last, edges, slab, kept, sem = rest
    frames, rows, cols, channels = kept.shape
    places = rows * cols
    members = channels // GROUPS

    total = jnp.sum(stats[...], axis=0)
    own = lax.broadcasted_iota(jnp.int32, (channels, channels), 0) // members
    other = lax.broadcasted_iota(jnp.int32, (channels, channels), 1) // members
    same = jnp.where(own == other, 1.0, 0.0)
    means = (
        jnp.dot(
            total, same, precision=lax.Precision.HIGHEST, preferred_element_type=jnp.float32
        )
        / entries
    )
    average = means[0:1]
    variance = means[1:2] - average * average
    scale = lax.rsqrt(variance + EPSILON) * gain[layer : layer + 1, :]
    offset = shift[layer : layer + 1, :] - average * scale
    scales = (scale[:, :LANES], twice(scale[:, LANES:]))
    offsets = (offset[:, :LANES], twice(offset[:, LANES:]))

    def act(part, value):
        return silu(value * scales[part] + offsets[part])

    for frame in range(frames):
        for side, ref in enumerate((before, after)):
            for part_index in range(2):
                if layer:
                    value = ref[part_index, frame]
                else:
                    value = halves(ref[frame].astype(jnp.float32))[part_index]
                    value = twice(value) if part_index else value
                edges[side, part_index, frame] = act(part_index, value)

        def row_of(h, frame=frame):
            if layer:
                start = h * COLS if isinstance(h, int) else pl.multiple_of(h * COLS, COLS)
                main, other = (x[i, frame, pl.ds(start, COLS), :] for i in range(2))
            else:
                main, other = halves(x[frame, h].astype(jnp.float32))
                other = twice(other)
            main, other = act(0, main), act(1, other)
            whole = jnp.concatenate([main, other[:, : channels - LANES]], axis=1)
            kept[frame, h] = whole.astype(jnp.bfloat16)
            return main, other

        def edge_of(h, part, frame=frame):
            return [edges[side, part, frame, pl.ds(h, COLS, stride=0), :] for side in (0, 1)]

        build_slabs(rows, row_of, edge_of, slab.at[frame])
    copy = pltpu.make_async_copy(kept, carried.at[layer], sem)
    copy.start()
    taps = [tap_rows(weight, layer, p, channels) for p in (1, 2)]
    sum_rows = jnp.zeros((COLS, channels), jnp.float32)
    square_rows = jnp.zeros((COLS, channels), jnp.float32)
    for i in range(places // chunk):
        start = i * chunk
        here = pl.ds(start, chunk)
        span = pl.ds(start // COLS, chunk // COLS)
        values = (
            product(slab.at[0], start, chunk, taps[1]) + part[layer, 0, here, :],
            product(slab.at[0], start, chunk, taps[0])
            + product(slab.at[1], start, chunk, taps[1])
            + part[layer, 1, here, :],
        )
        for t, value in enumerate(values):
            if final:
                held = [x[0, t, here, :], x[1, t, here, : channels - LANES]]
                value = value + jnp.concatenate(held, axis=1)
                shape = (chunk // COLS, COLS, channels)
                y[t, span] = value.reshape(shape).astype(jnp.bfloat16)
                continue
            if residual is not None:
                value = value + residual[t, span].astype(jnp.float32).reshape(chunk, channels)
            main, other = halves(value)
            y[0, t, here, :] = main
            y[1, t, here, :] = twice(other)
            folded = value.reshape(chunk // COLS, COLS, channels)
            sum_rows = sum_rows + jnp.sum(folded, axis=0)
            square_rows = square_rows + jnp.sum(folded * folded, axis=0)
    if not final:
        both = jnp.concatenate(
            [
                jnp.sum(sum_rows, axis=0, keepdims=True),
                jnp.sum(square_rows, axis=0, keepdims=True),
            ],
            axis=0,
        )
        sums[...] = jnp.broadcast_to(both[None], sums.shape)
        for i in range(2):
            for t in range(frames):
                first[i, t] = y[i, t, pl.ds(0, rows, stride=COLS), :]
                last[i, t] = y[i, t, pl.ds(COLS - 1, rows, stride=COLS), :]
    copy.wait()


def scratch(frames, rows):
    return [
        pltpu.VMEM((2, 2, frames, rows, LANES), jnp.float32),
        pltpu.VMEM((frames, SLABS, rows * COLS + 16, LANES), jnp.bfloat16),
    ]


def local(video_span, caches, norm_gains, shifts, weights, biases):
    peers = lax.axis_size("lon")
    frames, rows, cols, channels = video_span.shape
    layers = caches.shape[0]
    places = rows * cols
    entries = frames * places * peers * (channels // GROUPS)
    up = [(i, (i + 1) % peers) for i in range(peers)]
    down = [(j, i) for i, j in up]
    chunk = 240

    def around(first, last):
        return lax.ppermute(last, "lon", up), lax.ppermute(first, "lon", down)

    def gathered(sums):
        return lax.all_to_all(sums, "lon", 0, 0)

    source = video_span.astype(jnp.float32)
    sums = jnp.stack([jnp.sum(source, axis=(0, 1, 2)), jnp.sum(source * source, axis=(0, 1, 2))])
    stats = gathered(jnp.broadcast_to(sums[None], (peers,) + sums.shape))
    before, after = around(video_span[:, :, 0], video_span[:, :, -1])
    cache_before, cache_after = around(caches[:, :, :, 0], caches[:, :, :, -1])
    part = pl.pallas_call(
        functools.partial(cached_kernel, chunk),
        out_shape=jax.ShapeDtypeStruct((layers, frames, places, channels), jnp.float32),
        in_specs=[VMEM] * 5,
        out_specs=VMEM,
        scratch_shapes=scratch(frames, rows),
        name="cached",
    )(caches, cache_before, cache_after, weights, biases)

    x = video_span
    carried = None
    for layer in range(layers):
        final = layer == layers - 1
        operands = [x, before, after, stats, norm_gains, shifts, weights, part]
        specs = [VMEM] * 8
        aliases = {}
        if layer == 1:
            operands.append(video_span)
            specs.append(VMEM)
        if layer > 0:
            aliases = {len(operands): 1}
            operands.append(carried)
            specs.append(ANY)
        state = jax.ShapeDtypeStruct((2, frames, places, LANES), jnp.float32)
        if final:
            state = jax.ShapeDtypeStruct(video_span.shape, jnp.bfloat16)
        outs = [state, jax.ShapeDtypeStruct(caches.shape, jnp.bfloat16)]
        out_specs = [VMEM, ANY]
        if not final:
            edge = jax.ShapeDtypeStruct((2, frames, rows, LANES), jnp.float32)
            outs += [jax.ShapeDtypeStruct((peers, 2, channels), jnp.float32), edge, edge]
            out_specs += [VMEM] * 3
        results = pl.pallas_call(
            functools.partial(active_kernel, layer, chunk, entries, final),
            out_shape=outs,
            in_specs=specs,
            out_specs=out_specs,
            scratch_shapes=scratch(frames, rows)
            + [pltpu.VMEM(video_span.shape, jnp.bfloat16), pltpu.SemaphoreType.DMA(())],
            input_output_aliases=aliases,
            name="active",
        )(*operands)
        x, carried = results[:2]
        if not final:
            stats = gathered(results[2])
            before, after = around(results[3], results[4])
    return x, carried


def solution(mesh):
    return jax.shard_map(
        local,
        mesh=mesh,
        in_specs=(
            P(None, "clips", "lon", None),
            P(None, None, "clips", "lon", None),
            P(),
            P(),
            P(),
            P(),
        ),
        out_specs=(P(None, "clips", "lon", None), P(None, None, "clips", "lon", None)),
        check_vma=False,
    )
```

```python
import functools

import jax
import jax.numpy as jnp
from jax import lax
from jax.experimental import pallas as pl
from jax.experimental.pallas import tpu as pltpu
from jax.sharding import PartitionSpec as P

GROUPS = 32
EPSILON = 1e-06
LANES = 128
COLS = 8
SLABS = 10
VMEM = pl.BlockSpec(memory_space=pltpu.VMEM)
ANY = pl.BlockSpec(memory_space=pl.ANY)


def silu(u):
    return u * (0.5 + 0.5 * jnp.tanh(0.5 * u))


def twice(v):
    return jnp.concatenate([v, v], axis=-1)


def pair(a, b):
    return jnp.concatenate([a, b], axis=0).astype(jnp.bfloat16)


def build_slabs(rows, row_of, edge_of, slab):
    lane = lax.broadcasted_iota(jnp.int32, (COLS, LANES), 1)
    low = lane < LANES // 2
    column = lax.broadcasted_iota(jnp.int32, (COLS, LANES), 0)
    first, last = column == 0, column == COLS - 1
    zero = jnp.zeros((COLS, LANES), jnp.float32)

    def shifted(h):
        out = []
        for part, value in enumerate(row_of(h)):
            left, right = edge_of(h, part)
            out.append(
                (
                    jnp.where(first, left, pltpu.roll(value, 1, 0)),
                    value,
                    jnp.where(last, right, pltpu.roll(value, COLS - 1, 0)),
                )
            )
        main, rest = out
        return main + (jnp.where(low, rest[0], rest[1]), rest[2])

    def put(index, k, value):
        start = k * 16 if isinstance(k, int) else pl.multiple_of(k * 16, 16)
        slab[index, pl.ds(start, 16), :] = value

    def step(k, carry):
        before, older, oldest = carry
        one, two = shifted(2 * k), shifted(2 * k + 1)
        for r in range(3):
            put(r, k, pair(one[r], two[r]))
            put(3 + r, k, pair(before[r], one[r]))
        put(6, k, pair(one[3], two[3]))
        put(7, k, pair(before[3], one[3]))
        put(9, k, pair(one[4], two[4]))

        if older is not None:
            put(8, k - 1, pair(jnp.where(low, oldest, before[4]), jnp.where(low, older, one[4])))

        return two, one[4], before[4]

    count = rows // 2
    begun = step(0, ((zero,) * 5, None, None))
    before, older, oldest = lax.fori_loop(1, count, step, begun, unroll=4)
    for r in range(3):
        put(3 + r, count, pair(before[r], zero))
    put(7, count, pair(before[3], zero))
    put(8, count - 1, pair(jnp.where(low, oldest, before[4]), jnp.where(low, older, zero)))


def slab_rows(slab, start, size):
    def at(index, step=0):
        return slab[index, pl.ds(start + step, size), :]

    tiles = [at(3 + r) for r in range(3)] + [at(r) for r in range(3)]
    tiles += [at(3 + r, 16) for r in range(3)]
    tiles += [at(7), at(6), at(7, 16), at(8), at(9)]
    return jnp.concatenate(tiles, axis=1)


def tap_lanes(weight, tap_t, channels):
    def at(q, r, start, size):
        return weight[:, pl.ds(((tap_t * 3 + q) * 3 + r) * channels + start, size)]

    half = LANES // 2
    tiles = [at(q, r, 0, LANES) for q in range(3) for r in range(3)]
    for q in range(3):
        tiles += [at(q, 0, LANES, half), at(q, 1, LANES, half)]
    tiles += [at(0, 2, LANES, half), at(2, 2, LANES, half), at(1, 2, LANES, half)]
    tiles.append(jnp.zeros((weight.shape[0], half), weight.dtype))
    return jnp.concatenate(tiles, axis=1)


def product(slab, start, size, weight):
    return lax.dot_general(
        slab_rows(slab, start, size),
        weight,
        (((1,), (1,)), ((), ())),
        preferred_element_type=jnp.float32,
    )


def cached_kernel(chunk, cache, before, after, weights, bias, out, edges, slab, weight, sem):
    layers, frames, rows, cols, channels = cache.shape
    fetch = [
        pltpu.make_async_copy(weights.at[layer], weight.at[layer % 2], sem.at[layer % 2])
        for layer in range(layers)
    ]
    fetch[0].start()
    for layer in range(layers):
        if layer + 1 < layers:
            fetch[layer + 1].start()
        for frame in range(frames):
            for side, ref in enumerate((before, after)):
                value = ref[layer, frame].astype(jnp.float32)
                edges[side, 0, frame] = value[:, :LANES]
                edges[side, 1, frame] = twice(value[:, LANES:])

            def row_of(h, frame=frame):
                value = cache[layer, frame, h].astype(jnp.float32)
                return value[:, :LANES], twice(value[:, LANES:])

            def edge_of(h, part, frame=frame):
                return [edges[side, part, frame, pl.ds(h, COLS, stride=0), :] for side in (0, 1)]

            build_slabs(rows, row_of, edge_of, slab.at[frame])
        fetch[layer].wait()
        taps = [tap_lanes(weight.at[layer % 2], p, channels) for p in range(2)]
        for i in range(rows * cols // chunk):
            start = i * chunk
            here = pl.ds(start, chunk)
            out[layer, 0, here, :] = (
                product(slab.at[0], start, chunk, taps[0])
                + product(slab.at[1], start, chunk, taps[1])
                + bias[layer : layer + 1, :]
            )
            out[layer, 1, here, :] = (
                product(slab.at[1], start, chunk, taps[0]) + bias[layer : layer + 1, :]
            )


def halves(value):
    return value[..., :LANES], value[..., LANES:]


def active_kernel(layer, chunk, entries, final, *refs):
    x, before, after, stats, gain, shift, weights, parts = refs[:8]
    rest = refs[8:]
    residual = None
    if layer == 1:
        residual, *rest = rest
    if layer > 0:
        _, *rest = rest
    if final:
        y, carried, edges, slab, weight, part, kept, sem = rest
    else:
        y, carried, sums, first, last, edges, slab, weight, part, kept, sem = rest
    frames, rows, cols, channels = kept.shape
    places = rows * cols
    members = channels // GROUPS
    fetch = [
        pltpu.make_async_copy(weights.at[layer], weight, sem.at[0]),
        pltpu.make_async_copy(parts.at[layer], part, sem.at[1]),
    ]
    for one in fetch:
        one.start()

    total = jnp.sum(stats[...], axis=0)
    own = lax.broadcasted_iota(jnp.int32, (channels, channels), 0) // members
    other = lax.broadcasted_iota(jnp.int32, (channels, channels), 1) // members
    same = jnp.where(own == other, 1.0, 0.0)
    means = (
        jnp.dot(
            total, same, precision=lax.Precision.HIGHEST, preferred_element_type=jnp.float32
        )
        / entries
    )
    average = means[0:1]
    variance = means[1:2] - average * average
    scale = lax.rsqrt(variance + EPSILON) * gain[layer : layer + 1, :]
    offset = shift[layer : layer + 1, :] - average * scale
    scales = (scale[:, :LANES], twice(scale[:, LANES:]))
    offsets = (offset[:, :LANES], twice(offset[:, LANES:]))

    def act(part, value):
        return silu(value * scales[part] + offsets[part])

    for frame in range(frames):
        for side, ref in enumerate((before, after)):
            for part_index in range(2):
                if layer:
                    value = ref[part_index, frame]
                else:
                    value = halves(ref[frame].astype(jnp.float32))[part_index]
                    value = twice(value) if part_index else value
                edges[side, part_index, frame] = act(part_index, value)

        def row_of(h, frame=frame):
            if layer:
                start = h * COLS if isinstance(h, int) else pl.multiple_of(h * COLS, COLS)
                main, other = (x[i, frame, pl.ds(start, COLS), :] for i in range(2))
            else:
                main, other = halves(x[frame, h].astype(jnp.float32))
                other = twice(other)
            main, other = act(0, main), act(1, other)
            whole = jnp.concatenate([main, other[:, : channels - LANES]], axis=1)
            kept[frame, h] = whole.astype(jnp.bfloat16)
            return main, other

        def edge_of(h, part, frame=frame):
            return [edges[side, part, frame, pl.ds(h, COLS, stride=0), :] for side in (0, 1)]

        build_slabs(rows, row_of, edge_of, slab.at[frame])
    copy = pltpu.make_async_copy(kept, carried.at[layer], sem.at[2])
    copy.start()
    for one in fetch:
        one.wait()
    taps = [tap_lanes(weight, p, channels) for p in (1, 2)]
    sum_rows = jnp.zeros((COLS, channels), jnp.float32)
    square_rows = jnp.zeros((COLS, channels), jnp.float32)
    for i in range(places // chunk):
        start = i * chunk
        here = pl.ds(start, chunk)
        span = pl.ds(start // COLS, chunk // COLS)
        values = (
            product(slab.at[0], start, chunk, taps[1]) + part[0, here, :],
            product(slab.at[0], start, chunk, taps[0])
            + product(slab.at[1], start, chunk, taps[1])
            + part[1, here, :],
        )
        for t, value in enumerate(values):
            if final:
                held = [x[0, t, here, :], x[1, t, here, : channels - LANES]]
                value = value + jnp.concatenate(held, axis=1)
                shape = (chunk // COLS, COLS, channels)
                y[t, span] = value.reshape(shape).astype(jnp.bfloat16)
                continue
            if residual is not None:
                value = value + residual[t, span].astype(jnp.float32).reshape(chunk, channels)
            main, other = halves(value)
            y[0, t, here, :] = main
            y[1, t, here, :] = twice(other)
            folded = value.reshape(chunk // COLS, COLS, channels)
            sum_rows = sum_rows + jnp.sum(folded, axis=0)
            square_rows = square_rows + jnp.sum(folded * folded, axis=0)
    if not final:
        both = jnp.concatenate(
            [
                jnp.sum(sum_rows, axis=0, keepdims=True),
                jnp.sum(square_rows, axis=0, keepdims=True),
            ],
            axis=0,
        )
        sums[...] = jnp.broadcast_to(both[None], sums.shape)
        for i in range(2):
            for t in range(frames):
                first[i, t] = y[i, t, pl.ds(0, rows, stride=COLS), :]
                last[i, t] = y[i, t, pl.ds(COLS - 1, rows, stride=COLS), :]
    copy.wait()


def scratch(frames, rows):
    return [
        pltpu.VMEM((2, 2, frames, rows, LANES), jnp.float32),
        pltpu.VMEM((frames, SLABS, rows * COLS + 16, LANES), jnp.bfloat16),
    ]


def local(video_span, caches, norm_gains, shifts, weights, biases):
    peers = lax.axis_size("lon")
    frames, rows, cols, channels = video_span.shape
    layers = caches.shape[0]
    places = rows * cols
    entries = frames * places * peers * (channels // GROUPS)
    up = [(i, (i + 1) % peers) for i in range(peers)]
    down = [(j, i) for i, j in up]
    chunk = 240

    def around(first, last):
        return lax.ppermute(last, "lon", up), lax.ppermute(first, "lon", down)

    def gathered(sums):
        return lax.all_to_all(sums, "lon", 0, 0)

    turned = jnp.swapaxes(weights, 1, 2)
    source = video_span.astype(jnp.float32)
    sums = jnp.stack([jnp.sum(source, axis=(0, 1, 2)), jnp.sum(source * source, axis=(0, 1, 2))])
    stats = gathered(jnp.broadcast_to(sums[None], (peers,) + sums.shape))
    before, after = around(video_span[:, :, 0], video_span[:, :, -1])
    cache_before, cache_after = around(caches[:, :, :, 0], caches[:, :, :, -1])
    part = pl.pallas_call(
        functools.partial(cached_kernel, chunk),
        out_shape=jax.ShapeDtypeStruct((layers, frames, places, channels), jnp.float32),
        in_specs=[VMEM, VMEM, VMEM, ANY, VMEM],
        out_specs=VMEM,
        scratch_shapes=scratch(frames, rows)
        + [
            pltpu.VMEM((2, channels, weights.shape[1]), weights.dtype),
            pltpu.SemaphoreType.DMA((2,)),
        ],
        compiler_params=pltpu.CompilerParams(vmem_limit_bytes=28 << 20),
        name="cached",
    )(caches, cache_before, cache_after, turned, biases)

    x = video_span
    carried = None
    for layer in range(layers):
        final = layer == layers - 1
        operands = [x, before, after, stats, norm_gains, shifts, turned, part]
        specs = [VMEM] * 6 + [ANY] * 2
        aliases = {}
        if layer == 1:
            operands.append(video_span)
            specs.append(VMEM)
        if layer > 0:
            aliases = {len(operands): 1}
            operands.append(carried)
            specs.append(ANY)
        state = jax.ShapeDtypeStruct((2, frames, places, LANES), jnp.float32)
        if final:
            state = jax.ShapeDtypeStruct(video_span.shape, jnp.bfloat16)
        outs = [state, jax.ShapeDtypeStruct(caches.shape, jnp.bfloat16)]
        out_specs = [VMEM, ANY]
        if not final:
            edge = jax.ShapeDtypeStruct((2, frames, rows, LANES), jnp.float32)
            outs += [jax.ShapeDtypeStruct((peers, 2, channels), jnp.float32), edge, edge]
            out_specs += [VMEM] * 3
        results = pl.pallas_call(
            functools.partial(active_kernel, layer, chunk, entries, final),
            out_shape=outs,
            in_specs=specs,
            out_specs=out_specs,
            scratch_shapes=scratch(frames, rows)
            + [
                pltpu.VMEM((channels, weights.shape[1]), weights.dtype),
                pltpu.VMEM(part.shape[1:], jnp.float32),
                pltpu.VMEM(video_span.shape, jnp.bfloat16),
                pltpu.SemaphoreType.DMA((3,)),
            ],
            compiler_params=pltpu.CompilerParams(vmem_limit_bytes=28 << 20),
            input_output_aliases=aliases,
            name="active",
        )(*operands)
        x, carried = results[:2]
        if not final:
            stats = gathered(results[2])
            before, after = around(results[3], results[4])
    return x, carried


def solution(mesh):
    return jax.shard_map(
        local,
        mesh=mesh,
        in_specs=(
            P(None, "clips", "lon", None),
            P(None, None, "clips", "lon", None),
            P(),
            P(),
            P(),
            P(),
        ),
        out_specs=(P(None, "clips", "lon", None), P(None, None, "clips", "lon", None)),
        check_vma=False,
    )
```

```python
import functools

import jax
import jax.numpy as jnp
from jax import lax
from jax.experimental import pallas as pl
from jax.experimental.pallas import tpu as pltpu
from jax.sharding import PartitionSpec as P

GROUPS = 32
EPSILON = 1e-06
LANES = 128
COLS = 8
SLABS = 10
VMEM = pl.BlockSpec(memory_space=pltpu.VMEM)
HBM = pl.BlockSpec(memory_space=pltpu.HBM)


def silu(u):
    return u * (0.5 + 0.5 * jnp.tanh(0.5 * u))


def twice(v):
    return jnp.concatenate([v, v], axis=-1)


def pair(a, b):
    return jnp.concatenate([a, b], axis=0).astype(jnp.bfloat16)


def build_slabs(rows, row_of, edge_of, slab):
    lane = lax.broadcasted_iota(jnp.int32, (COLS, LANES), 1)
    low = lane < LANES // 2
    column = lax.broadcasted_iota(jnp.int32, (COLS, LANES), 0)
    first, last = column == 0, column == COLS - 1
    zero = jnp.zeros((COLS, LANES), jnp.float32)

    def shifted(h):
        out = []
        for part, value in enumerate(row_of(h)):
            left, right = edge_of(h, part)
            out.append(
                (
                    jnp.where(first, left, pltpu.roll(value, 1, 0)),
                    value,
                    jnp.where(last, right, pltpu.roll(value, COLS - 1, 0)),
                )
            )
        main, rest = out
        return main + (jnp.where(low, rest[0], rest[1]), rest[2])

    def put(index, k, value):
        start = k * 16 if isinstance(k, int) else pl.multiple_of(k * 16, 16)
        slab[index, pl.ds(start, 16), :] = value

    def step(k, carry):
        before, older, oldest = carry
        one, two = shifted(2 * k), shifted(2 * k + 1)
        for r in range(3):
            put(r, k, pair(one[r], two[r]))
            put(3 + r, k, pair(before[r], one[r]))
        put(6, k, pair(one[3], two[3]))
        put(7, k, pair(before[3], one[3]))
        put(9, k, pair(one[4], two[4]))

        if older is not None:
            put(8, k - 1, pair(jnp.where(low, oldest, before[4]), jnp.where(low, older, one[4])))

        return two, one[4], before[4]

    count = rows // 2
    begun = step(0, ((zero,) * 5, None, None))
    before, older, oldest = lax.fori_loop(1, count, step, begun, unroll=4)
    for r in range(3):
        put(3 + r, count, pair(before[r], zero))
    put(7, count, pair(before[3], zero))
    put(8, count - 1, pair(jnp.where(low, oldest, before[4]), jnp.where(low, older, zero)))


def slab_rows(slab, start, size):
    def at(index, step=0):
        return slab[index, pl.ds(start + step, size), :]

    tiles = [at(3 + r) for r in range(3)] + [at(r) for r in range(3)]
    tiles += [at(3 + r, 16) for r in range(3)]
    tiles += [at(7), at(6), at(7, 16), at(8), at(9)]
    return jnp.concatenate(tiles, axis=1)


def tap_lanes(weight, origin, channels):
    def at(q, r, start, size):
        return weight[:, pl.ds(origin + (q * 3 + r) * channels + start, size)]

    half = LANES // 2
    tiles = [at(q, r, 0, LANES) for q in range(3) for r in range(3)]
    for q in range(3):
        tiles += [at(q, 0, LANES, half), at(q, 1, LANES, half)]
    tiles += [at(0, 2, LANES, half), at(2, 2, LANES, half), at(1, 2, LANES, half)]
    tiles.append(jnp.zeros((weight.shape[0], half), weight.dtype))
    return jnp.concatenate(tiles, axis=1)


def product(slab, start, size, weight):
    return lax.dot_general(
        slab_rows(slab, start, size),
        weight,
        (((1,), (1,)), ((), ())),
        preferred_element_type=jnp.float32,
    )


def begin_kernel(video, caches, sums, first, last, wide, held, sem):
    layers, frames, rows, cols, channels = caches.shape
    copies = [pltpu.make_async_copy(video, held.at[0], sem.at[0])]
    for layer in range(layers):
        copies.append(
            pltpu.make_async_copy(caches.at[layer], held.at[layer + 1], sem.at[layer + 1])
        )
    for copy in copies:
        copy.start()
    half = channels - LANES
    total = [jnp.zeros((COLS, LANES), jnp.float32), jnp.zeros((COLS, half), jnp.float32)]
    square = list(total)
    for group, copy in enumerate(copies):
        copy.wait()
        for frame in range(frames):
            value = held[group, frame].astype(jnp.float32)
            parts = halves(value)
            if group == 0:
                for i in range(2):
                    total[i] = total[i] + jnp.sum(parts[i], axis=0)
                    square[i] = square[i] + jnp.sum(parts[i] * parts[i], axis=0)
            wide[0] = parts[0].reshape(rows * cols, LANES)
            wide[1, :, :half] = parts[1].reshape(rows * cols, half)
            for out, column in ((first, 0), (last, cols - 1)):
                found = [wide[i, pl.ds(column, rows, stride=cols), :] for i in range(2)]
                edge = jnp.concatenate([found[0], found[1][:, :half]], axis=1)
                out[group * frames + frame] = edge.astype(jnp.bfloat16)
    both = [
        jnp.concatenate([jnp.sum(v, axis=0, keepdims=True) for v in pieces], axis=1)
        for pieces in (total, square)
    ]
    sums[...] = jnp.broadcast_to(jnp.concatenate(both, axis=0)[None], sums.shape)


def cached_kernel(layer, chunk, caches, before, after, weights, bias, out, *scratches):
    edges, slab, cache, brims, weight, sem = scratches
    _, frames, rows, cols, channels = caches.shape
    where = pl.ds((layer + 1) * frames, frames)
    begun = [pltpu.make_async_copy(caches.at[layer], cache, sem.at[0])]
    for side, ref in enumerate((before, after)):
        begun.append(pltpu.make_async_copy(ref.at[where], brims.at[side], sem.at[side + 1]))
    fetch = pltpu.make_async_copy(
        weights.at[layer, :, pl.ds(0, weight.shape[1])], weight, sem.at[3]
    )
    for copy in begun:
        copy.start()
    fetch.start()
    for copy in begun:
        copy.wait()
    for frame in range(frames):
        for side in range(2):
            value = brims[side, frame].astype(jnp.float32)
            edges[side, 0, frame] = value[:, :LANES]
            edges[side, 1, frame] = twice(value[:, LANES:])

        def row_of(h, frame=frame):
            value = cache[frame, h].astype(jnp.float32)
            return value[:, :LANES], twice(value[:, LANES:])

        def edge_of(h, part, frame=frame):
            return [edges[side, part, frame, pl.ds(h, COLS, stride=0), :] for side in (0, 1)]

        build_slabs(rows, row_of, edge_of, slab.at[frame])
    fetch.wait()
    taps = [tap_lanes(weight, p * 9 * channels, channels) for p in range(2)]
    constant = bias[layer : layer + 1, :]
    for i in range(rows * cols // chunk):
        start = i * chunk
        here = pl.ds(start, chunk)
        out[0, here, :] = (
            product(slab.at[0], start, chunk, taps[0])
            + product(slab.at[1], start, chunk, taps[1])
            + constant
        )
        out[1, here, :] = product(slab.at[1], start, chunk, taps[0]) + constant


def halves(value):
    return value[..., :LANES], value[..., LANES:]


def active_kernel(layer, chunk, entries, final, *refs):
    x, before, after, stats, gain, shift, weights, part = refs[:8]
    rest = refs[8:]
    residual = None
    if layer == 1:
        residual, *rest = rest
    if layer > 0:
        _, *rest = rest
    if final:
        y, carried, edges, slab, kept, held, weight, sem = rest
    else:
        y, carried, sums, first, last, edges, slab, kept, held, weight, sem = rest
    frames, rows, cols, channels = kept.shape
    places = rows * cols
    members = channels // GROUPS
    skipped = weights.shape[2] - weight.shape[1]
    fetch = pltpu.make_async_copy(
        weights.at[layer, :, pl.ds(skipped, weight.shape[1])], weight, sem.at[1]
    )
    fetch.start()
    if residual is not None:
        source = pltpu.make_async_copy(residual, held, sem.at[2])
        source.start()

    total = jnp.sum(stats[...], axis=0)
    own = lax.broadcasted_iota(jnp.int32, (channels, channels), 0) // members
    other = lax.broadcasted_iota(jnp.int32, (channels, channels), 1) // members
    same = jnp.where(own == other, 1.0, 0.0)
    means = (
        jnp.dot(
            total, same, precision=lax.Precision.HIGHEST, preferred_element_type=jnp.float32
        )
        / entries
    )
    average = means[0:1]
    variance = means[1:2] - average * average
    scale = lax.rsqrt(variance + EPSILON) * gain[layer : layer + 1, :]
    offset = shift[layer : layer + 1, :] - average * scale
    scales = (scale[:, :LANES], twice(scale[:, LANES:]))
    offsets = (offset[:, :LANES], twice(offset[:, LANES:]))

    def act(part, value):
        return silu(value * scales[part] + offsets[part])

    for frame in range(frames):
        for side, ref in enumerate((before, after)):
            for part_index in range(2):
                if layer:
                    value = ref[part_index, frame]
                else:
                    value = halves(ref[frame].astype(jnp.float32))[part_index]
                    value = twice(value) if part_index else value
                edges[side, part_index, frame] = act(part_index, value)

        def row_of(h, frame=frame):
            if layer:
                start = h * COLS if isinstance(h, int) else pl.multiple_of(h * COLS, COLS)
                main, other = (x[i, frame, pl.ds(start, COLS), :] for i in range(2))
            else:
                main, other = halves(x[frame, h].astype(jnp.float32))
                other = twice(other)
            main, other = act(0, main), act(1, other)
            whole = jnp.concatenate([main, other[:, : channels - LANES]], axis=1)
            kept[frame, h] = whole.astype(jnp.bfloat16)
            return main, other

        def edge_of(h, part, frame=frame):
            return [edges[side, part, frame, pl.ds(h, COLS, stride=0), :] for side in (0, 1)]

        build_slabs(rows, row_of, edge_of, slab.at[frame])
    copy = pltpu.make_async_copy(kept, carried.at[layer], sem.at[0])
    copy.start()
    fetch.wait()
    if residual is not None:
        source.wait()
    taps = [tap_lanes(weight, p * 9 * channels - skipped, channels) for p in (1, 2)]
    sum_rows = jnp.zeros((COLS, channels), jnp.float32)
    square_rows = jnp.zeros((COLS, channels), jnp.float32)
    for i in range(places // chunk):
        start = i * chunk
        here = pl.ds(start, chunk)
        span = pl.ds(start // COLS, chunk // COLS)
        values = (
            product(slab.at[0], start, chunk, taps[1]) + part[0, here, :],
            product(slab.at[0], start, chunk, taps[0])
            + product(slab.at[1], start, chunk, taps[1])
            + part[1, here, :],
        )
        for t, value in enumerate(values):
            if final:
                held = [x[0, t, here, :], x[1, t, here, : channels - LANES]]
                value = value + jnp.concatenate(held, axis=1)
                shape = (chunk // COLS, COLS, channels)
                y[t, span] = value.reshape(shape).astype(jnp.bfloat16)
                continue
            if residual is not None:
                value = value + held[t, span].astype(jnp.float32).reshape(chunk, channels)
            main, other = halves(value)
            y[0, t, here, :] = main
            y[1, t, here, :] = twice(other)
            folded = value.reshape(chunk // COLS, COLS, channels)
            sum_rows = sum_rows + jnp.sum(folded, axis=0)
            square_rows = square_rows + jnp.sum(folded * folded, axis=0)
    if not final:
        both = jnp.concatenate(
            [
                jnp.sum(sum_rows, axis=0, keepdims=True),
                jnp.sum(square_rows, axis=0, keepdims=True),
            ],
            axis=0,
        )
        sums[...] = jnp.broadcast_to(both[None], sums.shape)
        for i in range(2):
            for t in range(frames):
                first[i, t] = y[i, t, pl.ds(0, rows, stride=COLS), :]
                last[i, t] = y[i, t, pl.ds(COLS - 1, rows, stride=COLS), :]
    copy.wait()


def scratch(frames, rows):
    return [
        pltpu.VMEM((2, 2, frames, rows, LANES), jnp.float32),
        pltpu.VMEM((frames, SLABS, rows * COLS + 16, LANES), jnp.bfloat16),
    ]


def local(video_span, caches, norm_gains, shifts, weights, biases):
    peers = lax.axis_size("lon")
    frames, rows, cols, channels = video_span.shape
    layers = caches.shape[0]
    places = rows * cols
    entries = frames * places * peers * (channels // GROUPS)
    up = [(i, (i + 1) % peers) for i in range(peers)]
    down = [(j, i) for i, j in up]
    chunk = 240
    skipped = 9 * channels // LANES * LANES

    def around(first, last):
        return lax.ppermute(last, "lon", up), lax.ppermute(first, "lon", down)

    def gathered(sums):
        return lax.all_to_all(sums, "lon", 0, 0)

    def in_hbm(value):
        return pltpu.with_memory_space_constraint(value, pltpu.HBM)

    turned = in_hbm(jnp.swapaxes(weights, 1, 2))
    caches, video = in_hbm(caches), in_hbm(video_span)
    spread = jax.ShapeDtypeStruct((peers, 2, channels), jnp.float32)
    brim = jax.ShapeDtypeStruct(((layers + 1) * frames, rows, channels), jnp.bfloat16)
    sums, first, last = pl.pallas_call(
        begin_kernel,
        out_shape=[spread, brim, brim],
        in_specs=[HBM, HBM],
        out_specs=[VMEM] * 3,
        scratch_shapes=[
            pltpu.VMEM((2, places, LANES), jnp.float32),
            pltpu.VMEM((layers + 1,) + video_span.shape, jnp.bfloat16),
            pltpu.SemaphoreType.DMA((layers + 1,)),
        ],
        compiler_params=pltpu.CompilerParams(vmem_limit_bytes=24 << 20),
        name="begin",
    )(video, caches)
    before, after = around(first, last)
    brims = [in_hbm(before), in_hbm(after)]
    stats = gathered(sums)

    def cached_part(layer):
        return pl.pallas_call(
            functools.partial(cached_kernel, layer, chunk),
            out_shape=jax.ShapeDtypeStruct((frames, places, channels), jnp.float32),
            in_specs=[HBM, HBM, HBM, HBM, VMEM],
            out_specs=VMEM,
            scratch_shapes=scratch(frames, rows)
            + [
                pltpu.VMEM(video_span.shape, jnp.bfloat16),
                pltpu.VMEM((2, frames, rows, channels), jnp.bfloat16),
                pltpu.VMEM((channels, 18 * channels), weights.dtype),
                pltpu.SemaphoreType.DMA((4,)),
            ],
            compiler_params=pltpu.CompilerParams(vmem_limit_bytes=24 << 20),
            name="cached",
        )(caches, *brims, turned, biases)

    x = video_span
    carried = None
    for layer in range(layers):
        final = layer == layers - 1
        operands = [x, before, after, stats, norm_gains, shifts, turned]
        operands.append(cached_part(layer))
        specs = [VMEM] * 6 + [HBM, VMEM]
        aliases = {}
        if layer == 1:
            operands.append(video)
            specs.append(HBM)
        if layer > 0:
            aliases = {len(operands): 1}
            operands.append(carried)
            specs.append(HBM)
        state = jax.ShapeDtypeStruct((2, frames, places, LANES), jnp.float32)
        if final:
            state = jax.ShapeDtypeStruct(video_span.shape, jnp.bfloat16)
        outs = [state, jax.ShapeDtypeStruct(caches.shape, jnp.bfloat16)]
        out_specs = [VMEM, HBM]
        if not final:
            edge = jax.ShapeDtypeStruct((2, frames, rows, LANES), jnp.float32)
            outs += [spread, edge, edge]
            out_specs += [VMEM] * 3
        results = pl.pallas_call(
            functools.partial(active_kernel, layer, chunk, entries, final),
            out_shape=outs,
            in_specs=specs,
            out_specs=out_specs,
            scratch_shapes=scratch(frames, rows)
            + [
                pltpu.VMEM(video_span.shape, jnp.bfloat16),
                pltpu.VMEM(video_span.shape, jnp.bfloat16),
                pltpu.VMEM((channels, 27 * channels - skipped), weights.dtype),
                pltpu.SemaphoreType.DMA((3,)),
            ],
            compiler_params=pltpu.CompilerParams(vmem_limit_bytes=24 << 20),
            input_output_aliases=aliases,
            name="active",
        )(*operands)
        x, carried = results[:2]
        if not final:
            stats = gathered(results[2])
            before, after = around(results[3], results[4])
    return x, carried


def solution(mesh):
    return jax.shard_map(
        local,
        mesh=mesh,
        in_specs=(
            P(None, "clips", "lon", None),
            P(None, None, "clips", "lon", None),
            P(),
            P(),
            P(),
            P(),
        ),
        out_specs=(P(None, "clips", "lon", None), P(None, None, "clips", "lon", None)),
        check_vma=False,
    )
```

```python
import functools

import jax
import jax.numpy as jnp
import numpy as np
from jax import lax
from jax.experimental import pallas as pl
from jax.experimental.pallas import tpu as pltpu
from jax.sharding import PartitionSpec as P

GROUPS = 32
EPSILON = 1e-06
LANES = 128
COLS = 8
SLABS = 10
STEPS = 12
VMEM = pl.BlockSpec(memory_space=pltpu.VMEM)
HBM = pl.BlockSpec(memory_space=pltpu.HBM)


def silu_of_twice(u):
    return u + u * jnp.tanh(u)


def twice(v):
    return jnp.concatenate([v, v], axis=-1)


def pair(a, b):
    return jnp.concatenate([a, b], axis=0).astype(jnp.bfloat16)


def build_slabs(rows, row_of, edge_of, slab, steps):
    lane = lax.broadcasted_iota(jnp.int32, (COLS, LANES), 1)
    low = lane < LANES // 2
    column = lax.broadcasted_iota(jnp.int32, (COLS, LANES), 0)
    first, last = column == 0, column == COLS - 1
    zero = jnp.zeros((COLS, LANES), jnp.float32)

    def shifted(h):
        out = []
        for part, value in enumerate(row_of(h)):
            left, right = edge_of(h, part)
            out.append(
                (
                    jnp.where(first, left, pltpu.roll(value, 1, 0)),
                    value,
                    jnp.where(last, right, pltpu.roll(value, COLS - 1, 0)),
                )
            )
        main, rest = out
        return main + (jnp.where(low, rest[0], rest[1]), rest[2])

    def put(index, k, value):
        start = k * 16 if isinstance(k, int) else pl.multiple_of(k * 16, 16)
        slab[index, pl.ds(start, 16), :] = value

    def step(k, carry):
        before, older, oldest = carry
        one, two = shifted(2 * k), shifted(2 * k + 1)
        for r in range(3):
            put(r, k, pair(one[r], two[r]))
            put(3 + r, k, pair(before[r], one[r]))
        put(6, k, pair(one[3], two[3]))
        put(7, k, pair(before[3], one[3]))
        put(9, k, pair(one[4], two[4]))
        if older is not None:
            put(8, k - 1, pair(jnp.where(low, oldest, before[4]), jnp.where(low, older, one[4])))
        return two, one[4], before[4]

    count = rows // 2
    carry = step(0, ((zero,) * 5, None, None))
    if steps:
        for k in range(1, count):
            carry = step(k, carry)
            if k % steps == 0:
                yield
    else:
        carry = lax.fori_loop(1, count, step, carry, unroll=4)
    before, older, oldest = carry
    for r in range(3):
        put(3 + r, count, pair(before[r], zero))
    put(7, count, pair(before[3], zero))
    put(8, count - 1, pair(jnp.where(low, oldest, before[4]), jnp.where(low, older, zero)))


def drain(pieces):
    for _ in pieces:
        pass


def slab_rows(slab, start, size):
    def at(index, step=0):
        return slab[index, pl.ds(start + step, size), :]

    tiles = [at(3 + r) for r in range(3)] + [at(r) for r in range(3)]
    tiles += [at(3 + r, 16) for r in range(3)]
    tiles += [at(7), at(6), at(7, 16), at(8), at(9)]
    return jnp.concatenate(tiles, axis=1)


def tap_lanes(weight, origin, channels):
    def at(q, r, start, size):
        return weight[:, pl.ds(origin + (q * 3 + r) * channels + start, size)]

    half = LANES // 2
    tiles = [at(q, r, 0, LANES) for q in range(3) for r in range(3)]
    for q in range(3):
        tiles += [at(q, 0, LANES, half), at(q, 1, LANES, half)]
    tiles += [at(0, 2, LANES, half), at(2, 2, LANES, half), at(1, 2, LANES, half)]
    tiles.append(jnp.zeros((weight.shape[0], half), weight.dtype))
    return jnp.concatenate(tiles, axis=1)


def product(slab, start, size, weight):
    return lax.dot_general(
        slab_rows(slab, start, size),
        weight,
        (((1,), (1,)), ((), ())),
        preferred_element_type=jnp.float32,
    )


def begin_kernel(video, caches, sums, first, last, wide, held, sem):
    layers, frames, rows, cols, channels = caches.shape
    copies = [pltpu.make_async_copy(video, held.at[0], sem.at[0])]
    for layer in range(layers):
        copies.append(
            pltpu.make_async_copy(caches.at[layer], held.at[layer + 1], sem.at[layer + 1])
        )
    for copy in copies:
        copy.start()
    half = channels - LANES
    total = [jnp.zeros((COLS, LANES), jnp.float32), jnp.zeros((COLS, half), jnp.float32)]
    square = list(total)
    for group, copy in enumerate(copies):
        copy.wait()
        for frame in range(frames):
            value = held[group, frame].astype(jnp.float32)
            parts = halves(value)
            if group == 0:
                for i in range(2):
                    total[i] = total[i] + jnp.sum(parts[i], axis=0)
                    square[i] = square[i] + jnp.sum(parts[i] * parts[i], axis=0)
            wide[0] = parts[0].reshape(rows * cols, LANES)
            wide[1, :, :half] = parts[1].reshape(rows * cols, half)
            for out, column in ((first, 0), (last, cols - 1)):
                found = [wide[i, pl.ds(column, rows, stride=cols), :] for i in range(2)]
                edge = jnp.concatenate([found[0], found[1][:, :half]], axis=1)
                out[group * frames + frame] = edge.astype(jnp.bfloat16)
    both = [
        jnp.concatenate([jnp.sum(v, axis=0, keepdims=True) for v in pieces], axis=1)
        for pieces in (total, square)
    ]
    sums[...] = jnp.broadcast_to(jnp.concatenate(both, axis=0)[None], sums.shape)


def cached_kernel(layer, chunk, caches, before, after, weights, bias, out, *scratches):
    edges, *slabs, cache, brims, weight, sem = scratches
    _, frames, rows, cols, channels = caches.shape
    where = pl.ds((layer + 1) * frames, frames)
    begun = [pltpu.make_async_copy(caches.at[layer], cache, sem.at[0])]
    for side, ref in enumerate((before, after)):
        begun.append(pltpu.make_async_copy(ref.at[where], brims.at[side], sem.at[side + 1]))
    fetch = pltpu.make_async_copy(
        weights.at[layer, :, pl.ds(0, weight.shape[1])], weight, sem.at[3]
    )
    for copy in begun:
        copy.start()
    fetch.start()
    for copy in begun:
        copy.wait()
    pieces = []
    for frame in range(frames):
        for side in range(2):
            value = brims[side, frame].astype(jnp.float32)
            edges[side, 0, frame] = value[:, :LANES]
            edges[side, 1, frame] = twice(value[:, LANES:])

        def row_of(h, frame=frame):
            value = cache[frame, h].astype(jnp.float32)
            return value[:, :LANES], twice(value[:, LANES:])

        def edge_of(h, part, frame=frame):
            return [edges[side, part, frame, pl.ds(h, COLS, stride=0), :] for side in (0, 1)]

        steps = STEPS if frame else None
        pieces.append(build_slabs(rows, row_of, edge_of, slabs[frame], steps))
    drain(pieces[0])
    fetch.wait()
    taps = [tap_lanes(weight, p * 9 * channels, channels) for p in range(2)]
    constant = bias[layer : layer + 1, :]
    for start in range(0, rows * cols, chunk):
        here = pl.ds(start, chunk)
        out[0, here, :] = product(slabs[0], start, chunk, taps[0]) + constant
        next(pieces[1], None)
    drain(pieces[1])
    for start in range(0, rows * cols, chunk):
        here = pl.ds(start, chunk)
        out[0, here, :] += product(slabs[1], start, chunk, taps[1])
        out[1, here, :] = product(slabs[1], start, chunk, taps[0]) + constant


def halves(value):
    return value[..., :LANES], value[..., LANES:]


def group_means(stats, same, entries):
    total = jnp.sum(stats, axis=0)
    high = total.astype(jnp.bfloat16)
    left = total - high.astype(jnp.float32)
    middle = left.astype(jnp.bfloat16)
    low = (left - middle.astype(jnp.float32)).astype(jnp.bfloat16)
    split = jnp.concatenate([high, middle, low], axis=0)
    sums = jnp.dot(split, same, preferred_element_type=jnp.float32)
    return (sums[0:2] + sums[2:4] + sums[4:6]) / entries


def active_kernel(layer, chunk, entries, final, *refs):
    x, before, after, stats, gain, shift, weights, part, same = refs[:9]
    rest = refs[9:]
    residual = None
    if layer == 1:
        residual, *rest = rest
    if layer > 0:
        _, *rest = rest
    if final:
        y, carried, *rest = rest
    else:
        y, carried, sums, first, last, *rest = rest
    edges, *slabs, kept, held, brims, partial, weight, sem = rest
    frames, rows, cols, channels = kept.shape
    places = rows * cols
    half = channels - LANES
    skipped = weights.shape[2] - weight.shape[1]
    fetch = [
        pltpu.make_async_copy(
            weights.at[layer, :, pl.ds(skipped, weight.shape[1])], weight, sem.at[1]
        )
    ]
    brim = []
    if layer == 0:
        for side, ref in enumerate((before, after)):
            brim.append(
                pltpu.make_async_copy(ref.at[pl.ds(0, frames)], brims.at[side], sem.at[3 + side])
            )
    if residual is not None:
        fetch.append(pltpu.make_async_copy(residual, held, sem.at[2]))
    for copy in brim + fetch:
        copy.start()

    means = group_means(stats[...], same[...], entries)
    average = means[0:1]
    variance = means[1:2] - average * average
    scale = lax.rsqrt(variance + EPSILON) * gain[layer : layer + 1, :]
    offset = shift[layer : layer + 1, :] - average * scale
    scale, offset = 0.5 * scale, 0.5 * offset
    scales = (scale[:, :LANES], twice(scale[:, LANES:]))
    offsets = (offset[:, :LANES], twice(offset[:, LANES:]))

    def act(index, value):
        return silu_of_twice(value * scales[index] + offsets[index])

    for copy in brim:
        copy.wait()
    pieces = []
    for frame in range(frames):
        for side, ref in enumerate((before, after)):
            for index in range(2):
                if layer:
                    value = ref[index, frame].astype(jnp.float32)
                else:
                    value = halves(brims[side, frame].astype(jnp.float32))[index]
                    value = twice(value) if index else value
                edges[side, index, frame] = act(index, value)

        def row_of(h, frame=frame):
            if layer:
                start = h * COLS if isinstance(h, int) else pl.multiple_of(h * COLS, COLS)
                main, other = (x[i, frame, pl.ds(start, COLS), :] for i in range(2))
            else:
                main, other = halves(x[frame, h].astype(jnp.float32))
                other = twice(other)
            main, other = act(0, main), act(1, other)
            whole = jnp.concatenate([main, other[:, :half]], axis=1)
            kept[frame, h] = whole.astype(jnp.bfloat16)
            return main, other

        def edge_of(h, index, frame=frame):
            return [edges[side, index, frame, pl.ds(h, COLS, stride=0), :] for side in (0, 1)]

        steps = STEPS if frame else None
        pieces.append(build_slabs(rows, row_of, edge_of, slabs[frame], steps))
    drain(pieces[0])
    for copy in fetch:
        copy.wait()
    taps = [tap_lanes(weight, p * 9 * channels - skipped, channels) for p in (1, 2)]
    moments = [jnp.zeros((COLS, channels), jnp.float32)] * 2

    def finish(t, start, value, moments):
        here, span = pl.ds(start, chunk), pl.ds(start // COLS, chunk // COLS)
        shape = (chunk // COLS, COLS, channels)
        if final:
            own = jnp.concatenate([x[0, t, here, :], x[1, t, here, :half]], axis=1)
            y[t, span] = (value + own).reshape(shape).astype(jnp.bfloat16)
            return moments
        if residual is not None:
            value = value + held[t, span].astype(jnp.float32).reshape(chunk, channels)
        main, other = halves(value)
        y[0, t, here, :] = main
        y[1, t, here, :] = twice(other)
        folded = value.reshape(shape)
        return [
            moments[0] + jnp.sum(folded, axis=0),
            moments[1] + jnp.sum(folded * folded, axis=0),
        ]

    starts = range(0, places, chunk)
    for start in starts:
        here = pl.ds(start, chunk)
        partial[here, :] = part[1, here, :] + product(slabs[0], start, chunk, taps[0])
        next(pieces[1], None)
    for start in starts:
        value = product(slabs[0], start, chunk, taps[1]) + part[0, pl.ds(start, chunk), :]
        next(pieces[1], None)
        moments = finish(0, start, value, moments)
    drain(pieces[1])
    copy = pltpu.make_async_copy(kept, carried.at[layer], sem.at[0])
    copy.start()
    for start in starts:
        value = product(slabs[1], start, chunk, taps[1]) + partial[pl.ds(start, chunk), :]
        moments = finish(1, start, value, moments)
    if not final:
        both = [jnp.sum(v, axis=0, keepdims=True) for v in moments]
        sums[...] = jnp.broadcast_to(jnp.concatenate(both, axis=0)[None], sums.shape)
        for i in range(2):
            for t in range(frames):
                for out, column in ((first, 0), (last, cols - 1)):
                    edge = y[i, t, pl.ds(column, rows, stride=cols), :]
                    out[i, t] = edge.astype(jnp.bfloat16)
    copy.wait()


def scratch(frames, rows):
    return [
        pltpu.VMEM((2, 2, frames, rows, LANES), jnp.float32),
    ] + [pltpu.VMEM((SLABS, rows * COLS + 16, LANES), jnp.bfloat16)] * frames


def local(video_span, caches, norm_gains, shifts, weights, biases):
    peers = lax.axis_size("lon")
    frames, rows, cols, channels = video_span.shape
    layers = caches.shape[0]
    places = rows * cols
    entries = frames * places * peers * (channels // GROUPS)
    up = [(i, (i + 1) % peers) for i in range(peers)]
    down = [(j, i) for i, j in up]
    chunk = 360
    skipped = 9 * channels // LANES * LANES

    def around(first, last):
        return lax.ppermute(last, "lon", up), lax.ppermute(first, "lon", down)

    def gathered(sums):
        return lax.all_to_all(sums, "lon", 0, 0)

    def in_hbm(value):
        return pltpu.with_memory_space_constraint(value, pltpu.HBM)

    turned = in_hbm(jnp.swapaxes(weights, 1, 2))
    caches, video = in_hbm(caches), in_hbm(video_span)
    spread = jax.ShapeDtypeStruct((peers, 2, channels), jnp.float32)
    brim = jax.ShapeDtypeStruct(((layers + 1) * frames, rows, channels), jnp.bfloat16)
    sums, first, last = pl.pallas_call(
        begin_kernel,
        out_shape=[spread, brim, brim],
        in_specs=[HBM, HBM],
        out_specs=[VMEM] * 3,
        scratch_shapes=[
            pltpu.VMEM((2, places, LANES), jnp.float32),
            pltpu.VMEM((layers + 1,) + video_span.shape, jnp.bfloat16),
            pltpu.SemaphoreType.DMA((layers + 1,)),
        ],
        compiler_params=pltpu.CompilerParams(vmem_limit_bytes=24 << 20),
        name="begin",
    )(video, caches)
    brims = [in_hbm(brim) for brim in around(first, last)]
    before, after = brims
    members = channels // GROUPS
    same = jnp.asarray(np.kron(np.eye(GROUPS), np.ones((members, members))), jnp.bfloat16)
    stats = gathered(sums)

    def cached_part(layer):
        return pl.pallas_call(
            functools.partial(cached_kernel, layer, chunk),
            out_shape=jax.ShapeDtypeStruct((frames, places, channels), jnp.float32),
            in_specs=[HBM, HBM, HBM, HBM, VMEM],
            out_specs=VMEM,
            scratch_shapes=scratch(frames, rows)
            + [
                pltpu.VMEM(video_span.shape, jnp.bfloat16),
                pltpu.VMEM((2, frames, rows, channels), jnp.bfloat16),
                pltpu.VMEM((channels, 18 * channels), weights.dtype),
                pltpu.SemaphoreType.DMA((4,)),
            ],
            compiler_params=pltpu.CompilerParams(vmem_limit_bytes=24 << 20),
            name="cached",
        )(caches, *brims, turned, biases)

    x = video_span
    carried = None
    for layer in range(layers):
        final = layer == layers - 1
        operands = [x, before, after, stats, norm_gains, shifts, turned]
        operands += [cached_part(layer), same]
        specs = [VMEM] * 6 + [HBM, VMEM, VMEM]
        if layer == 0:
            specs[1:3] = [HBM, HBM]
        aliases = {}
        if layer == 1:
            operands.append(video)
            specs.append(HBM)
        if layer > 0:
            aliases = {len(operands): 1}
            operands.append(carried)
            specs.append(HBM)
        state = jax.ShapeDtypeStruct((2, frames, places, LANES), jnp.float32)
        if final:
            state = jax.ShapeDtypeStruct(video_span.shape, jnp.bfloat16)
        outs = [state, jax.ShapeDtypeStruct(caches.shape, jnp.bfloat16)]
        out_specs = [VMEM, HBM]
        if not final:
            edge = jax.ShapeDtypeStruct((2, frames, rows, LANES), jnp.bfloat16)
            outs += [spread, edge, edge]
            out_specs += [VMEM] * 3
        results = pl.pallas_call(
            functools.partial(active_kernel, layer, chunk, entries, final),
            out_shape=outs,
            in_specs=specs,
            out_specs=out_specs,
            scratch_shapes=scratch(frames, rows)
            + [
                pltpu.VMEM(video_span.shape, jnp.bfloat16),
                pltpu.VMEM(video_span.shape, jnp.bfloat16),
                pltpu.VMEM((2, frames, rows, channels), jnp.bfloat16),
                pltpu.VMEM((places, channels), jnp.float32),
                pltpu.VMEM((channels, 27 * channels - skipped), weights.dtype),
                pltpu.SemaphoreType.DMA((5,)),
            ],
            compiler_params=pltpu.CompilerParams(vmem_limit_bytes=24 << 20),
            input_output_aliases=aliases,
            name="active",
        )(*operands)
        x, carried = results[:2]
        if not final:
            stats = gathered(results[2])
            before, after = around(results[3], results[4])
    return x, carried


def solution(mesh):
    return jax.shard_map(
        local,
        mesh=mesh,
        in_specs=(
            P(None, "clips", "lon", None),
            P(None, None, "clips", "lon", None),
            P(),
            P(),
            P(),
            P(),
        ),
        out_specs=(P(None, "clips", "lon", None), P(None, None, "clips", "lon", None)),
        check_vma=False,
    )
```

```python
import functools

import jax
import jax.numpy as jnp
import numpy as np
from jax import lax
from jax.experimental import pallas as pl
from jax.experimental.pallas import tpu as pltpu
from jax.sharding import PartitionSpec as P

GROUPS = 32
EPSILON = 1e-06
LANES = 128
HALF = LANES // 2
COLS = 8
SLABS = 10
UNROLL = 2
PLANES = 3
VMEM = pl.BlockSpec(memory_space=pltpu.VMEM)
HBM = pl.BlockSpec(memory_space=pltpu.HBM)


def silu_of_twice(u):
    return u + u * jnp.tanh(u)


def twice(v):
    return jnp.concatenate([v, v], axis=-1)


def halves(value):
    return value[..., :LANES], value[..., LANES:]


def planes(first, second):
    (a, b), (c, d) = halves(first), halves(second)
    return a, c, jnp.concatenate([b, d], axis=-1)


def pair(a, b):
    return jnp.concatenate([a, b], axis=0).astype(jnp.bfloat16)


def build_slabs(rows, row_of, edge_of, slabs, keep=None):
    lane = lax.broadcasted_iota(jnp.int32, (COLS, LANES), 1)
    low = lane < HALF
    column = lax.broadcasted_iota(jnp.int32, (COLS, LANES), 0)
    first, last = column == 0, column == COLS - 1
    zero = jnp.zeros((COLS, LANES), jnp.float32)

    def shifted(h):
        out = []
        for plane, value in enumerate(row_of(h)):
            left, right = edge_of(h, plane)
            out.append(
                (
                    jnp.where(first, left, pltpu.roll(value, 1, 0)),
                    value,
                    jnp.where(last, right, pltpu.roll(value, COLS - 1, 0)),
                )
            )
        rest = out[2]
        swapped = [pltpu.roll(v, HALF, 1) for v in rest]
        if keep is not None:
            keep(h, out[0][1], rest[1], out[1][1], swapped[1])
        mains = out[0] + out[1]
        packed = (jnp.where(low, rest[0], swapped[1]), jnp.where(low, swapped[0], rest[1]))
        return mains, packed, (rest[2], swapped[2])

    def put(frame, index, k, value):
        start = k * 16 if isinstance(k, int) else pl.multiple_of(k * 16, 16)
        slabs[frame][index, pl.ds(start, 16), :] = value

    def around(frame, upper, lower):
        return jnp.where(low, upper[frame], lower[1 - frame])

    def step(k, carry):
        before, older, oldest = carry
        one, two = shifted(2 * k), shifted(2 * k + 1)
        for frame in range(2):
            for r in range(3):
                put(frame, r, k, pair(one[0][3 * frame + r], two[0][3 * frame + r]))
                put(frame, 3 + r, k, pair(before[0][3 * frame + r], one[0][3 * frame + r]))
            put(frame, 6, k, pair(one[1][frame], two[1][frame]))
            put(frame, 7, k, pair(before[1][frame], one[1][frame]))
            put(frame, 9, k, pair(one[2][frame], two[2][frame]))
            if older is not None:
                upper = around(frame, oldest, before[2])
                put(frame, 8, k - 1, pair(upper, around(frame, older, one[2])))
        return two, one[2], before[2]

    count = rows // 2
    carry = step(0, (((zero,) * 6, (zero,) * 2, (zero,) * 2), None, None))
    before, older, oldest = lax.fori_loop(1, count, step, carry, unroll=UNROLL)
    for frame in range(2):
        for r in range(3):
            put(frame, 3 + r, count, pair(before[0][3 * frame + r], zero))
        put(frame, 7, count, pair(before[1][frame], zero))
        upper = around(frame, oldest, before[2])
        put(frame, 8, count - 1, pair(upper, around(frame, older, (zero, zero))))


def slab_rows(slab, start, size):
    def at(index, step=0):
        return slab[index, pl.ds(start + step, size), :]

    tiles = [at(3 + r) for r in range(3)] + [at(r) for r in range(3)]
    tiles += [at(3 + r, 16) for r in range(3)]
    return tiles + [at(7), at(6), at(7, 16), at(8), at(9)]


def tap_lanes(weight, origin, channels):
    def at(q, r, start, size):
        return weight[:, pl.ds(origin + (q * 3 + r) * channels + start, size)]

    tiles = [at(q, r, 0, LANES) for q in range(3) for r in range(3)]
    for q in range(3):
        tiles += [at(q, 0, LANES, HALF), at(q, 1, LANES, HALF)]
    tiles += [at(0, 2, LANES, HALF), at(2, 2, LANES, HALF), at(1, 2, LANES, HALF)]
    tiles.append(jnp.zeros((weight.shape[0], HALF), weight.dtype))
    return jnp.concatenate(tiles, axis=1)


def product(pairs, start, size):
    left = [tile for slab, _ in pairs for tile in slab_rows(slab, start, size)]
    right = [taps for _, taps in pairs]
    return lax.dot_general(
        jnp.concatenate(left, axis=1),
        jnp.concatenate(right, axis=1),
        (((1,), (1,)), ((), ())),
        preferred_element_type=jnp.float32,
    )


def put_planes(out, t, here, value):
    main, rest = halves(value)
    out[t, here, :] = main
    out[2, here, HALF * t : HALF * (t + 1)] = rest


def get_planes(held, t, here):
    rest = held[2, here, HALF * t : HALF * (t + 1)]
    return jnp.concatenate([held[t, here, :], rest], axis=1)


def begin_kernel(video, caches, sums, first, last, wide, held, sem):
    layers, frames, rows, cols, channels = caches.shape
    copies = [pltpu.make_async_copy(video, held.at[0], sem.at[0])]
    for layer in range(layers):
        copies.append(
            pltpu.make_async_copy(caches.at[layer], held.at[layer + 1], sem.at[layer + 1])
        )
    for copy in copies:
        copy.start()
    half = channels - LANES
    total = [jnp.zeros((COLS, LANES), jnp.float32), jnp.zeros((COLS, half), jnp.float32)]
    square = list(total)
    for group, copy in enumerate(copies):
        copy.wait()
        for frame in range(frames):
            value = held[group, frame].astype(jnp.float32)
            parts = halves(value)
            if group == 0:
                for i in range(2):
                    total[i] = total[i] + jnp.sum(parts[i], axis=0)
                    square[i] = square[i] + jnp.sum(parts[i] * parts[i], axis=0)
            wide[0] = parts[0].reshape(rows * cols, LANES)
            wide[1, :, :half] = parts[1].reshape(rows * cols, half)
            for out, column in ((first, 0), (last, cols - 1)):
                found = [wide[i, pl.ds(column, rows, stride=cols), :] for i in range(2)]
                edge = jnp.concatenate([found[0], found[1][:, :half]], axis=1)
                out[group * frames + frame] = edge.astype(jnp.bfloat16)
    both = [
        jnp.concatenate([jnp.sum(v, axis=0, keepdims=True) for v in pieces], axis=1)
        for pieces in (total, square)
    ]
    sums[...] = jnp.broadcast_to(jnp.concatenate(both, axis=0)[None], sums.shape)


def cached_kernel(layer, chunk, caches, before, after, weights, bias, out, ordered, *scratches):
    edges, *slabs, cache, weight, taps, sem = scratches
    _, frames, rows, cols, channels = caches.shape
    places = rows * cols
    begun = pltpu.make_async_copy(caches.at[layer], cache, sem.at[0])
    fetch = pltpu.make_async_copy(weights.at[layer], weight, sem.at[1])
    begun.start()
    fetch.start()
    begun.wait()
    origin = (layer + 1) * frames
    for side, ref in enumerate((before, after)):
        found = planes(*(ref[origin + frame].astype(jnp.float32) for frame in range(2)))
        for plane in range(PLANES):
            edges[side, plane] = found[plane]

    def row_of(h):
        return planes(*(cache[frame, h].astype(jnp.float32) for frame in range(2)))

    def edge_of(h, plane):
        return [edges[side, plane, pl.ds(h, COLS, stride=0), :] for side in (0, 1)]

    build_slabs(rows, row_of, edge_of, slabs)
    fetch.wait()
    for p in (1, 2, 0):
        taps[p] = tap_lanes(weight, p * 9 * channels, channels)
    store = pltpu.make_async_copy(taps.at[pl.ds(1, 2)], ordered, sem.at[2])
    store.start()
    constant = bias[layer : layer + 1, :]
    tables = [taps[p] for p in range(2)]
    for start in range(0, places, chunk):
        value = product([(slabs[1], tables[0])], start, chunk)
        put_planes(out, 1, pl.ds(start, chunk), value + constant)
    for start in range(0, places, chunk):
        value = product([(slabs[0], tables[0]), (slabs[1], tables[1])], start, chunk)
        put_planes(out, 0, pl.ds(start, chunk), value + constant)
    store.wait()


def group_means(stats, same, entries):
    total = jnp.sum(stats, axis=0)
    high = total.astype(jnp.bfloat16)
    left = total - high.astype(jnp.float32)
    middle = left.astype(jnp.bfloat16)
    low = (left - middle.astype(jnp.float32)).astype(jnp.bfloat16)
    split = jnp.concatenate([high, middle, low], axis=0)
    sums = jnp.dot(split, same, preferred_element_type=jnp.float32)
    return (sums[0:2] + sums[2:4] + sums[4:6]) / entries


def active_kernel(layer, chunk, entries, final, *refs):
    x, before, after, stats, gain, shift, ordered, part, same = refs[:9]
    rest = refs[9:]
    residual = None
    if layer == 1:
        residual, *rest = rest
    if layer > 0:
        _, *rest = rest
    if final:
        y, carried, *rest = rest
    else:
        y, carried, sums, first, last, *rest = rest
    edges, *slabs, kept, held, taps, sem = rest
    frames, rows, cols, channels = kept.shape
    places = rows * cols
    fetch = [pltpu.make_async_copy(ordered, taps, sem.at[1])]
    if residual is not None:
        fetch.append(pltpu.make_async_copy(residual, held, sem.at[2]))
    for copy in fetch:
        copy.start()

    means = group_means(stats[...], same[...], entries)
    average = means[0:1]
    variance = means[1:2] - average * average
    scale = lax.rsqrt(variance + EPSILON) * gain[layer : layer + 1, :]
    offset = shift[layer : layer + 1, :] - average * scale
    scale, offset = 0.5 * scale, 0.5 * offset
    scales = [scale[:, :LANES]] * 2 + [twice(scale[:, LANES:])]
    offsets = [offset[:, :LANES]] * 2 + [twice(offset[:, LANES:])]

    def act(values):
        return [silu_of_twice(v * a + b) for v, a, b in zip(values, scales, offsets)]

    for side, ref in enumerate((before, after)):
        if layer:
            values = [ref[plane].astype(jnp.float32) for plane in range(PLANES)]
        else:
            values = planes(*(ref[frame].astype(jnp.float32) for frame in range(2)))
        for plane, value in enumerate(act(values)):
            edges[side, plane] = value

    def row_of(h):
        if layer:
            start = h * COLS if isinstance(h, int) else pl.multiple_of(h * COLS, COLS)
            return act([x[plane, pl.ds(start, COLS), :] for plane in range(PLANES)])
        return act(planes(*(x[frame, h].astype(jnp.float32) for frame in range(2))))

    def edge_of(h, plane):
        return [edges[side, plane, pl.ds(h, COLS, stride=0), :] for side in (0, 1)]

    def keep(h, *values):
        for frame in range(2):
            main, other = values[2 * frame : 2 * frame + 2]
            whole = jnp.concatenate([main, other[:, : channels - LANES]], axis=1)
            kept[frame, h] = whole.astype(jnp.bfloat16)

    build_slabs(rows, row_of, edge_of, slabs, keep)
    copy = pltpu.make_async_copy(kept, carried.at[layer], sem.at[0])
    copy.start()
    for one in fetch:
        one.wait()
    tables = [taps[p] for p in range(2)]
    moments = [jnp.zeros((COLS, channels), jnp.float32)] * 2

    def finish(t, start, value, moments):
        here, span = pl.ds(start, chunk), pl.ds(start // COLS, chunk // COLS)
        shape = (chunk // COLS, COLS, channels)
        value = value + get_planes(part, t, here)
        if final:
            value = value + get_planes(x, t, here)
            y[t, span] = value.reshape(shape).astype(jnp.bfloat16)
            return moments
        if residual is not None:
            value = value + held[t, span].astype(jnp.float32).reshape(chunk, channels)
        put_planes(y, t, here, value)
        folded = value.reshape(shape)
        return [
            moments[0] + jnp.sum(folded, axis=0),
            moments[1] + jnp.sum(folded * folded, axis=0),
        ]

    starts = range(0, places, chunk)
    for start in starts:
        value = product([(slabs[0], tables[1])], start, chunk)
        moments = finish(0, start, value, moments)
    for start in starts:
        value = product([(slabs[0], tables[0]), (slabs[1], tables[1])], start, chunk)
        moments = finish(1, start, value, moments)
    if not final:
        both = [jnp.sum(v, axis=0, keepdims=True) for v in moments]
        sums[...] = jnp.broadcast_to(jnp.concatenate(both, axis=0)[None], sums.shape)
        for plane in range(PLANES):
            for out, column in ((first, 0), (last, cols - 1)):
                edge = y[plane, pl.ds(column, rows, stride=cols), :]
                out[plane] = edge.astype(jnp.bfloat16)
    copy.wait()


def scratch(frames, rows):
    slab = pltpu.VMEM((SLABS, rows * COLS + 16, LANES), jnp.bfloat16)
    return [pltpu.VMEM((2, PLANES, rows, LANES), jnp.float32)] + [slab] * frames


def local(video_span, caches, norm_gains, shifts, weights, biases):
    peers = lax.axis_size("lon")
    frames, rows, cols, channels = video_span.shape
    layers = caches.shape[0]
    places = rows * cols
    entries = frames * places * peers * (channels // GROUPS)
    up = [(i, (i + 1) % peers) for i in range(peers)]
    down = [(j, i) for i, j in up]
    chunk = 720
    tiles = 14 * LANES

    def around(first, last):
        return lax.ppermute(last, "lon", up), lax.ppermute(first, "lon", down)

    def gathered(sums):
        return lax.all_to_all(sums, "lon", 0, 0)

    def in_hbm(value):
        return pltpu.with_memory_space_constraint(value, pltpu.HBM)

    turned = in_hbm(jnp.swapaxes(weights, 1, 2))
    caches, video = in_hbm(caches), in_hbm(video_span)
    spread = jax.ShapeDtypeStruct((peers, 2, channels), jnp.float32)
    brim = jax.ShapeDtypeStruct(((layers + 1) * frames, rows, channels), jnp.bfloat16)
    sums, first, last = pl.pallas_call(
        begin_kernel,
        out_shape=[spread, brim, brim],
        in_specs=[HBM, HBM],
        out_specs=[VMEM] * 3,
        scratch_shapes=[
            pltpu.VMEM((2, places, LANES), jnp.float32),
            pltpu.VMEM((layers + 1,) + video_span.shape, jnp.bfloat16),
            pltpu.SemaphoreType.DMA((layers + 1,)),
        ],
        compiler_params=pltpu.CompilerParams(vmem_limit_bytes=24 << 20),
        name="begin",
    )(video, caches)
    brims = around(first, last)
    before, after = brims
    members = channels // GROUPS
    same = jnp.asarray(np.kron(np.eye(GROUPS), np.ones((members, members))), jnp.bfloat16)
    stats = gathered(sums)

    def cached_part(layer):
        return pl.pallas_call(
            functools.partial(cached_kernel, layer, chunk),
            out_shape=[
                jax.ShapeDtypeStruct((PLANES, places, LANES), jnp.float32),
                jax.ShapeDtypeStruct((2, channels, tiles), weights.dtype),
            ],
            in_specs=[HBM, VMEM, VMEM, HBM, VMEM],
            out_specs=[VMEM, HBM],
            scratch_shapes=scratch(frames, rows)
            + [
                pltpu.VMEM(video_span.shape, jnp.bfloat16),
                pltpu.VMEM((channels, weights.shape[1]), weights.dtype),
                pltpu.VMEM((3, channels, tiles), weights.dtype),
                pltpu.SemaphoreType.DMA((3,)),
            ],
            compiler_params=pltpu.CompilerParams(vmem_limit_bytes=24 << 20),
            name="cached",
        )(caches, *brims, turned, biases)

    x = video_span
    carried = None
    for layer in range(layers):
        final = layer == layers - 1
        part, ordered = cached_part(layer)
        operands = [x, before, after, stats, norm_gains, shifts, in_hbm(ordered), part, same]
        specs = [VMEM] * 6 + [HBM, VMEM, VMEM]
        aliases = {}
        if layer == 1:
            operands.append(video)
            specs.append(HBM)
        if layer > 0:
            aliases = {len(operands): 1}
            operands.append(carried)
            specs.append(HBM)
        state = jax.ShapeDtypeStruct((PLANES, places, LANES), jnp.float32)
        if final:
            state = jax.ShapeDtypeStruct(video_span.shape, jnp.bfloat16)
        outs = [state, jax.ShapeDtypeStruct(caches.shape, jnp.bfloat16)]
        out_specs = [VMEM, HBM]
        if not final:
            edge = jax.ShapeDtypeStruct((PLANES, rows, LANES), jnp.bfloat16)
            outs += [spread, edge, edge]
            out_specs += [VMEM] * 3
        results = pl.pallas_call(
            functools.partial(active_kernel, layer, chunk, entries, final),
            out_shape=outs,
            in_specs=specs,
            out_specs=out_specs,
            scratch_shapes=scratch(frames, rows)
            + [
                pltpu.VMEM(video_span.shape, jnp.bfloat16),
                pltpu.VMEM(video_span.shape, jnp.bfloat16),
                pltpu.VMEM((2, channels, tiles), weights.dtype),
                pltpu.SemaphoreType.DMA((3,)),
            ],
            compiler_params=pltpu.CompilerParams(vmem_limit_bytes=24 << 20),
            input_output_aliases=aliases,
            name="active",
        )(*operands)
        x, carried = results[:2]
        if not final:
            stats = gathered(results[2])
            before, after = around(results[3], results[4])
    return x, carried


def solution(mesh):
    return jax.shard_map(
        local,
        mesh=mesh,
        in_specs=(
            P(None, "clips", "lon", None),
            P(None, None, "clips", "lon", None),
            P(),
            P(),
            P(),
            P(),
        ),
        out_specs=(P(None, "clips", "lon", None), P(None, None, "clips", "lon", None)),
        check_vma=False,
    )
```

```python
import functools

import jax
import jax.numpy as jnp
import numpy as np
from jax import lax
from jax.experimental import pallas as pl
from jax.experimental.pallas import tpu as pltpu
from jax.sharding import PartitionSpec as P

GROUPS = 32
EPSILON = 1e-06
LANES = 128
HALF = LANES // 2
COLS = 8
SLABS = 10
UNROLL = 11
PLANES = 3
VMEM = pl.BlockSpec(memory_space=pltpu.VMEM)
HBM = pl.BlockSpec(memory_space=pltpu.HBM)


def silu_of_twice(u):
    return u + u * jnp.tanh(u)


def twice(v):
    return jnp.concatenate([v, v], axis=-1)


def halves(value):
    return value[..., :LANES], value[..., LANES:]


def planes(first, second):
    (a, b), (c, d) = halves(first), halves(second)
    return a, c, jnp.concatenate([b, d], axis=-1)


def pair(a, b):
    return jnp.concatenate([a, b], axis=0).astype(jnp.bfloat16)


def build_slabs(rows, row_of, edge_of, slabs, keep=None):
    lane = lax.broadcasted_iota(jnp.int32, (COLS, LANES), 1)
    low = lane < HALF
    column = lax.broadcasted_iota(jnp.int32, (COLS, LANES), 0)
    first, last = column == 0, column == COLS - 1
    zero = jnp.zeros((COLS, LANES), jnp.float32)

    def shifted(h):
        out = []
        for plane, value in enumerate(row_of(h)):
            left, right = edge_of(h, plane)
            out.append(
                (
                    jnp.where(first, left, pltpu.roll(value, 1, 0)),
                    value,
                    jnp.where(last, right, pltpu.roll(value, COLS - 1, 0)),
                )
            )
        rest = out[2]
        swapped = [pltpu.roll(v, HALF, 1) for v in rest]
        if keep is not None:
            keep(h, out[0][1], rest[1], out[1][1], swapped[1])
        mains = out[0] + out[1]
        packed = (jnp.where(low, rest[0], swapped[1]), jnp.where(low, swapped[0], rest[1]))
        return mains, packed, (rest[2], swapped[2])

    def put(frame, index, k, value):
        start = k * 16 if isinstance(k, int) else pl.multiple_of(k * 16, 16)
        slabs[frame][index, pl.ds(start, 16), :] = value

    def around(frame, upper, lower):
        return jnp.where(low, upper[frame], lower[1 - frame])

    def step(k, carry):
        before, older, oldest = carry
        one, two = shifted(2 * k), shifted(2 * k + 1)
        for frame in range(2):
            for r in range(3):
                put(frame, r, k, pair(one[0][3 * frame + r], two[0][3 * frame + r]))
                put(frame, 3 + r, k, pair(before[0][3 * frame + r], one[0][3 * frame + r]))
            put(frame, 6, k, pair(one[1][frame], two[1][frame]))
            put(frame, 7, k, pair(before[1][frame], one[1][frame]))
            put(frame, 9, k, pair(one[2][frame], two[2][frame]))
            if older is not None:
                upper = around(frame, oldest, before[2])
                put(frame, 8, k - 1, pair(upper, around(frame, older, one[2])))
        return two, one[2], before[2]

    count = rows // 2
    carry = step(0, (((zero,) * 6, (zero,) * 2, (zero,) * 2), None, None))
    before, older, oldest = lax.fori_loop(1, count, step, carry, unroll=UNROLL)
    for frame in range(2):
        for r in range(3):
            put(frame, 3 + r, count, pair(before[0][3 * frame + r], zero))
        put(frame, 7, count, pair(before[1][frame], zero))
        upper = around(frame, oldest, before[2])
        put(frame, 8, count - 1, pair(upper, around(frame, older, (zero, zero))))


def slab_rows(slab, start, size):
    def at(index, step=0):
        return slab[index, pl.ds(start + step, size), :]

    tiles = [at(3 + r) for r in range(3)] + [at(r) for r in range(3)]
    tiles += [at(3 + r, 16) for r in range(3)]
    return tiles + [at(7), at(6), at(7, 16), at(8), at(9)]


def tap_lanes(weight, origin, channels):
    def at(q, r, start, size):
        return weight[:, pl.ds(origin + (q * 3 + r) * channels + start, size)]

    tiles = [at(q, r, 0, LANES) for q in range(3) for r in range(3)]
    for q in range(3):
        tiles += [at(q, 0, LANES, HALF), at(q, 1, LANES, HALF)]
    tiles += [at(0, 2, LANES, HALF), at(2, 2, LANES, HALF), at(1, 2, LANES, HALF)]
    tiles.append(jnp.zeros((weight.shape[0], HALF), weight.dtype))
    return jnp.concatenate(tiles, axis=1)


def product(pairs, start, size):
    left = [tile for slab, _ in pairs for tile in slab_rows(slab, start, size)]
    right = [taps for _, taps in pairs]
    return lax.dot_general(
        jnp.concatenate(left, axis=1),
        jnp.concatenate(right, axis=1),
        (((1,), (1,)), ((), ())),
        preferred_element_type=jnp.float32,
    )


def put_planes(out, t, here, value):
    main, rest = halves(value)
    out[t, here, :] = main
    out[2, here, HALF * t : HALF * (t + 1)] = rest


def get_planes(held, t, here):
    rest = held[2, here, HALF * t : HALF * (t + 1)]
    return jnp.concatenate([held[t, here, :], rest], axis=1)


def group_sums(pieces, same):
    total = jnp.concatenate([jnp.sum(v, axis=0, keepdims=True) for v in pieces], axis=0)
    high = total.astype(jnp.bfloat16)
    left = total - high.astype(jnp.float32)
    middle = left.astype(jnp.bfloat16)
    low = (left - middle.astype(jnp.float32)).astype(jnp.bfloat16)
    split = jnp.concatenate([high, middle, low], axis=0)
    sums = jnp.dot(split, same, preferred_element_type=jnp.float32)
    return sums[0:2] + sums[2:4] + sums[4:6]


def begin_kernel(video, caches, same, sums, first, last, wide, held, alike, sem):
    layers, frames, rows, cols, channels = caches.shape
    copies = [pltpu.make_async_copy(video, held.at[0], sem.at[0])]
    for layer in range(layers):
        copies.append(
            pltpu.make_async_copy(caches.at[layer], held.at[layer + 1], sem.at[layer + 1])
        )
    fetch = pltpu.make_async_copy(same, alike, sem.at[layers + 1])
    for copy in copies + [fetch]:
        copy.start()
    half, places = channels - LANES, rows * cols
    total = [jnp.zeros((COLS, LANES), jnp.float32), jnp.zeros((COLS, half), jnp.float32)]
    square = list(total)
    for group, copy in enumerate(copies):
        copy.wait()
        for frame in range(frames):
            value = held[group, frame].astype(jnp.float32)
            parts = halves(value)
            if group == 0:
                for i in range(2):
                    total[i] = total[i] + jnp.sum(parts[i], axis=0)
                    square[i] = square[i] + jnp.sum(parts[i] * parts[i], axis=0)
            wide[frame] = parts[0].reshape(places, LANES)
            wide[2, :, HALF * frame : HALF * (frame + 1)] = parts[1].reshape(places, half)
        for out, column in ((first, 0), (last, cols - 1)):
            for plane in range(PLANES):
                edge = wide[plane, pl.ds(column, rows, stride=cols), :]
                out[group * PLANES + plane] = edge.astype(jnp.bfloat16)
    fetch.wait()
    both = group_sums([jnp.concatenate(v, axis=1) for v in (total, square)], alike[...])
    sums[...] = jnp.broadcast_to(both[None], sums.shape)


def cached_kernel(layer, chunk, far, caches, before, after, weights, bias, *refs):
    out, ordered, edges, *slabs, cache, weight, taps, sem = refs
    if far:
        away, out, *slabs = out, slabs[0], *slabs[1:]
    _, _, rows, cols, channels = caches.shape
    places = rows * cols
    begun = pltpu.make_async_copy(caches.at[layer], cache, sem.at[0])
    fetch = pltpu.make_async_copy(weights.at[layer], weight, sem.at[1])
    begun.start()
    fetch.start()
    begun.wait()
    for side, ref in enumerate((before, after)):
        for plane in range(PLANES):
            edges[side, plane] = ref[(layer + 1) * PLANES + plane].astype(jnp.float32)

    def row_of(h):
        return planes(*(cache[frame, h].astype(jnp.float32) for frame in range(2)))

    def edge_of(h, plane):
        return [edges[side, plane, pl.ds(h, COLS, stride=0), :] for side in (0, 1)]

    build_slabs(rows, row_of, edge_of, slabs)
    fetch.wait()
    for p in (1, 2, 0):
        taps[p] = tap_lanes(weight, p * 9 * channels, channels)
    store = pltpu.make_async_copy(taps.at[pl.ds(1, 2)], ordered, sem.at[2])
    store.start()
    constant = bias[layer : layer + 1, :]
    tables = [taps[p] for p in range(2)]
    value = product([(slabs[1], tables[0])], 0, places)
    put_planes(out, 1, pl.ds(0, places), value + constant)
    for start in range(0, places, chunk):
        value = product([(slabs[0], tables[0]), (slabs[1], tables[1])], start, chunk)
        put_planes(out, 0, pl.ds(start, chunk), value + constant)
    if far:
        leave = pltpu.make_async_copy(out, away, sem.at[3])
        leave.start()
        leave.wait()
    store.wait()


def active_kernel(layer, chunk, far, entries, final, *refs):
    x, before, after, stats, gain, shift, ordered, part, same = refs[:9]
    rest = refs[9:]
    residual = None
    if layer == 1:
        residual, *rest = rest
    if layer > 0:
        _, *rest = rest
    if final:
        y, carried, *rest = rest
    else:
        y, carried, sums, first, last, *rest = rest
    edges, *slabs, kept, held, taps, alike, sem = rest
    away = None
    if far:
        away, part, *slabs = part, *slabs
    frames, rows, cols, channels = kept.shape
    places = rows * cols
    fetch = [pltpu.make_async_copy(ordered, taps, sem.at[1])]
    if not final:
        fetch.append(pltpu.make_async_copy(same, alike, sem.at[4]))
    if far:
        fetch.append(pltpu.make_async_copy(away, part, sem.at[3]))
    if residual is not None:
        fetch.append(pltpu.make_async_copy(residual, held, sem.at[2]))
    for copy in fetch:
        copy.start()

    means = jnp.sum(stats[...], axis=0) / entries
    average = means[0:1]
    variance = means[1:2] - average * average
    scale = lax.rsqrt(variance + EPSILON) * gain[layer : layer + 1, :]
    offset = shift[layer : layer + 1, :] - average * scale
    scale, offset = 0.5 * scale, 0.5 * offset
    scales = [scale[:, :LANES]] * 2 + [twice(scale[:, LANES:])]
    offsets = [offset[:, :LANES]] * 2 + [twice(offset[:, LANES:])]

    def act(values):
        return [silu_of_twice(v * a + b) for v, a, b in zip(values, scales, offsets)]

    for side, ref in enumerate((before, after)):
        values = [ref[plane].astype(jnp.float32) for plane in range(PLANES)]
        for plane, value in enumerate(act(values)):
            edges[side, plane] = value

    def row_of(h):
        if layer:
            start = h * COLS if isinstance(h, int) else pl.multiple_of(h * COLS, COLS)
            return act([x[plane, pl.ds(start, COLS), :] for plane in range(PLANES)])
        return act(planes(*(x[frame, h].astype(jnp.float32) for frame in range(2))))

    def edge_of(h, plane):
        return [edges[side, plane, pl.ds(h, COLS, stride=0), :] for side in (0, 1)]

    def keep(h, *values):
        for frame in range(2):
            main, other = values[2 * frame : 2 * frame + 2]
            whole = jnp.concatenate([main, other[:, : channels - LANES]], axis=1)
            kept[frame, h] = whole.astype(jnp.bfloat16)

    build_slabs(rows, row_of, edge_of, slabs, keep)
    copy = pltpu.make_async_copy(kept, carried.at[layer], sem.at[0])
    copy.start()
    for one in fetch:
        one.wait()
    tables = [taps[p] for p in range(2)]
    moments = [jnp.zeros((COLS, channels), jnp.float32)] * 2

    def finish(t, start, size, value, moments):
        here, span = pl.ds(start, size), pl.ds(start // COLS, size // COLS)
        shape = (size // COLS, COLS, channels)
        value = value + get_planes(part, t, here)
        if final:
            value = value + get_planes(x, t, here)
            y[t, span] = value.reshape(shape).astype(jnp.bfloat16)
            return moments
        if residual is not None:
            value = value + held[t, span].astype(jnp.float32).reshape(size, channels)
        put_planes(y, t, here, value)
        folded = value.reshape(shape)
        return [
            moments[0] + jnp.sum(folded, axis=0),
            moments[1] + jnp.sum(folded * folded, axis=0),
        ]

    value = product([(slabs[0], tables[1])], 0, places)
    moments = finish(0, 0, places, value, moments)
    for start in range(0, places, chunk):
        value = product([(slabs[0], tables[0]), (slabs[1], tables[1])], start, chunk)
        moments = finish(1, start, chunk, value, moments)
    if not final:
        both = group_sums(moments, alike[...])
        sums[...] = jnp.broadcast_to(both[None], sums.shape)
        for plane in range(PLANES):
            for out, column in ((first, 0), (last, cols - 1)):
                edge = y[plane, pl.ds(column, rows, stride=cols), :]
                out[plane] = edge.astype(jnp.bfloat16)
    copy.wait()


def scratch(frames, rows, room):
    slab = pltpu.VMEM((SLABS, rows * COLS + 16, LANES), jnp.bfloat16)
    return [pltpu.VMEM((2, PLANES, rows, LANES), jnp.float32)] + room + [slab] * frames


def local(video_span, caches, norm_gains, shifts, weights, biases):
    peers = lax.axis_size("lon")
    frames, rows, cols, channels = video_span.shape
    layers = caches.shape[0]
    places = rows * cols
    entries = frames * places * peers * (channels // GROUPS)
    up = [(i, (i + 1) % peers) for i in range(peers)]
    down = [(j, i) for i, j in up]
    chunk = 720
    tiles = 14 * LANES

    def around(first, last):
        return lax.ppermute(last, "lon", up), lax.ppermute(first, "lon", down)

    def gathered(sums):
        return lax.all_to_all(sums, "lon", 0, 0)

    def in_hbm(value):
        return pltpu.with_memory_space_constraint(value, pltpu.HBM)

    turned = in_hbm(jnp.swapaxes(weights, 1, 2))
    caches, video = in_hbm(caches), in_hbm(video_span)
    members = channels // GROUPS
    alike = np.kron(np.eye(GROUPS), np.ones((members, members)))
    same = in_hbm(jnp.asarray(alike, jnp.bfloat16))
    spread = jax.ShapeDtypeStruct((peers, 2, channels), jnp.float32)
    brim = jax.ShapeDtypeStruct(((layers + 1) * PLANES, rows, LANES), jnp.bfloat16)
    sums, first, last = pl.pallas_call(
        begin_kernel,
        out_shape=[spread, brim, brim],
        in_specs=[HBM] * 3,
        out_specs=[VMEM] * 3,
        scratch_shapes=[
            pltpu.VMEM((PLANES, places, LANES), jnp.float32),
            pltpu.VMEM((layers + 1,) + video_span.shape, jnp.bfloat16),
            pltpu.VMEM(same.shape, same.dtype),
            pltpu.SemaphoreType.DMA((layers + 2,)),
        ],
        compiler_params=pltpu.CompilerParams(vmem_limit_bytes=24 << 20),
        name="begin",
    )(video, caches, same)
    brims = around(first, last)
    before, after = brims
    stats = gathered(sums)

    def room(far):
        return [pltpu.VMEM((PLANES, places, LANES), jnp.float32)] if far else []

    def cached_part(layer, far):
        planar = pltpu.HBM if far else jax.ShapeDtypeStruct
        return pl.pallas_call(
            functools.partial(cached_kernel, layer, chunk, far),
            out_shape=[
                planar((PLANES, places, LANES), jnp.float32),
                pltpu.HBM((2, channels, tiles), weights.dtype),
            ],
            in_specs=[HBM, VMEM, VMEM, HBM, VMEM],
            out_specs=[HBM if far else VMEM, HBM],
            scratch_shapes=scratch(frames, rows, room(far))
            + [
                pltpu.VMEM(video_span.shape, jnp.bfloat16),
                pltpu.VMEM((channels, weights.shape[1]), weights.dtype),
                pltpu.VMEM((3, channels, tiles), weights.dtype),
                pltpu.SemaphoreType.DMA((4,)),
            ],
            compiler_params=pltpu.CompilerParams(vmem_limit_bytes=24 << 20),
            name="cached",
        )(caches, *brims, turned, biases)

    x = video_span
    carried = None
    for layer in range(layers):
        final = layer == layers - 1
        far = 0 < layer < layers - 1
        part, ordered = cached_part(layer, far)
        if far:
            part = in_hbm(part)
        operands = [x, before, after, stats, norm_gains, shifts, in_hbm(ordered), part, same]
        specs = [VMEM] * 6 + [HBM, HBM if far else VMEM, HBM]
        aliases = {}
        if layer == 1:
            operands.append(video)
            specs.append(HBM)
        if layer > 0:
            aliases = {len(operands): 1}
            operands.append(carried)
            specs.append(HBM)
        state = jax.ShapeDtypeStruct((PLANES, places, LANES), jnp.float32)
        if final:
            state = jax.ShapeDtypeStruct(video_span.shape, jnp.bfloat16)
        outs = [state, jax.ShapeDtypeStruct(caches.shape, jnp.bfloat16)]
        out_specs = [VMEM, HBM]
        if not final:
            edge = jax.ShapeDtypeStruct((PLANES, rows, LANES), jnp.bfloat16)
            outs += [spread, edge, edge]
            out_specs += [VMEM] * 3
        results = pl.pallas_call(
            functools.partial(active_kernel, layer, chunk, far, entries, final),
            out_shape=outs,
            in_specs=specs,
            out_specs=out_specs,
            scratch_shapes=scratch(frames, rows, room(far))
            + [
                pltpu.VMEM(video_span.shape, jnp.bfloat16),
                pltpu.VMEM(video_span.shape, jnp.bfloat16),
                pltpu.VMEM((2, channels, tiles), weights.dtype),
                pltpu.VMEM(same.shape, same.dtype),
                pltpu.SemaphoreType.DMA((5,)),
            ],
            compiler_params=pltpu.CompilerParams(vmem_limit_bytes=24 << 20),
            input_output_aliases=aliases,
            name="active",
        )(*operands)
        x, carried = results[:2]
        if not final:
            stats = gathered(results[2])
            before, after = around(results[3], results[4])
    return x, carried


def solution(mesh):
    return jax.shard_map(
        local,
        mesh=mesh,
        in_specs=(
            P(None, "clips", "lon", None),
            P(None, None, "clips", "lon", None),
            P(),
            P(),
            P(),
            P(),
        ),
        out_specs=(P(None, "clips", "lon", None), P(None, None, "clips", "lon", None)),
        check_vma=False,
    )
```

```python
import functools

import jax
import jax.numpy as jnp
import numpy as np
from jax import lax
from jax.experimental import pallas as pl
from jax.experimental.pallas import tpu as pltpu
from jax.sharding import PartitionSpec as P

GROUPS = 32
EPSILON = 1e-06
LANES = 128
HALF = LANES // 2
COLS = 8
SLABS = 10
UNROLL = 11
PLANES = 3
VMEM = pl.BlockSpec(memory_space=pltpu.VMEM)
HBM = pl.BlockSpec(memory_space=pltpu.HBM)


def silu_of_twice(u):
    return u + u * jnp.tanh(u)


def twice(v):
    return jnp.concatenate([v, v], axis=-1)


def halves(value):
    return value[..., :LANES], value[..., LANES:]


def planes(first, second):
    (a, b), (c, d) = halves(first), halves(second)
    return a, c, jnp.concatenate([b, d], axis=-1)


def pair(a, b):
    return jnp.concatenate([a, b], axis=0).astype(jnp.bfloat16)


def build_slabs(rows, row_of, edge_of, slabs, keep=None):
    lane = lax.broadcasted_iota(jnp.int32, (COLS, LANES), 1)
    low = lane < HALF
    column = lax.broadcasted_iota(jnp.int32, (COLS, LANES), 0)
    first, last = column == 0, column == COLS - 1
    zero = jnp.zeros((COLS, LANES), jnp.float32)

    def shifted(h):
        out = []
        for plane, value in enumerate(row_of(h)):
            left, right = edge_of(h, plane)
            out.append(
                (
                    jnp.where(first, left, pltpu.roll(value, 1, 0)),
                    value,
                    jnp.where(last, right, pltpu.roll(value, COLS - 1, 0)),
                )
            )
        rest = out[2]
        swapped = [pltpu.roll(v, HALF, 1) for v in rest]
        if keep is not None:
            keep(h, out[0][1], rest[1], out[1][1], swapped[1])
        mains = out[0] + out[1]
        packed = (jnp.where(low, rest[0], swapped[1]), jnp.where(low, swapped[0], rest[1]))
        return mains, packed, (rest[2], swapped[2])

    def put(frame, index, k, value):
        start = k * 16 if isinstance(k, int) else pl.multiple_of(k * 16, 16)
        slabs[frame][index, pl.ds(start, 16), :] = value

    def around(frame, upper, lower):
        return jnp.where(low, upper[frame], lower[1 - frame])

    def step(k, carry):
        before, older, oldest = carry
        one, two = shifted(2 * k), shifted(2 * k + 1)
        for frame in range(2):
            for r in range(3):
                put(frame, r, k, pair(one[0][3 * frame + r], two[0][3 * frame + r]))
                put(frame, 3 + r, k, pair(before[0][3 * frame + r], one[0][3 * frame + r]))
            put(frame, 6, k, pair(one[1][frame], two[1][frame]))
            put(frame, 7, k, pair(before[1][frame], one[1][frame]))
            put(frame, 9, k, pair(one[2][frame], two[2][frame]))
            if older is not None:
                upper = around(frame, oldest, before[2])
                put(frame, 8, k - 1, pair(upper, around(frame, older, one[2])))
        return two, one[2], before[2]

    count = rows // 2
    carry = step(0, (((zero,) * 6, (zero,) * 2, (zero,) * 2), None, None))
    before, older, oldest = lax.fori_loop(1, count, step, carry, unroll=UNROLL)
    for frame in range(2):
        for r in range(3):
            put(frame, 3 + r, count, pair(before[0][3 * frame + r], zero))
        put(frame, 7, count, pair(before[1][frame], zero))
        upper = around(frame, oldest, before[2])
        put(frame, 8, count - 1, pair(upper, around(frame, older, (zero, zero))))


def slab_rows(slab, start, size):
    def at(index, step=0):
        return slab[index, pl.ds(start + step, size), :]

    tiles = [at(3 + r) for r in range(3)] + [at(r) for r in range(3)]
    tiles += [at(3 + r, 16) for r in range(3)]
    return tiles + [at(7), at(6), at(7, 16), at(8), at(9)]


def tap_lanes(weight, origin, channels):
    def at(q, r, start, size):
        return weight[:, pl.ds(origin + (q * 3 + r) * channels + start, size)]

    tiles = [at(q, r, 0, LANES) for q in range(3) for r in range(3)]
    for q in range(3):
        tiles += [at(q, 0, LANES, HALF), at(q, 1, LANES, HALF)]
    tiles += [at(0, 2, LANES, HALF), at(2, 2, LANES, HALF), at(1, 2, LANES, HALF)]
    tiles.append(jnp.zeros((weight.shape[0], HALF), weight.dtype))
    return jnp.concatenate(tiles, axis=1)


def product(pairs, start, size):
    left = [tile for slab, _ in pairs for tile in slab_rows(slab, start, size)]
    right = [taps for _, taps in pairs]
    return lax.dot_general(
        jnp.concatenate(left, axis=1),
        jnp.concatenate(right, axis=1),
        (((1,), (1,)), ((), ())),
        preferred_element_type=jnp.float32,
    )


def put_planes(out, t, here, value):
    main, rest = halves(value)
    out[t, here, :] = main
    out[2, here, HALF * t : HALF * (t + 1)] = rest


def get_planes(held, t, here):
    rest = held[2, here, HALF * t : HALF * (t + 1)]
    return jnp.concatenate([held[t, here, :], rest], axis=1)


def group_sums(pieces, same):
    total = jnp.concatenate([jnp.sum(v, axis=0, keepdims=True) for v in pieces], axis=0)
    high = total.astype(jnp.bfloat16)
    left = total - high.astype(jnp.float32)
    middle = left.astype(jnp.bfloat16)
    low = (left - middle.astype(jnp.float32)).astype(jnp.bfloat16)
    split = jnp.concatenate([high, middle, low], axis=0)
    sums = jnp.dot(split, same, preferred_element_type=jnp.float32)
    sums = sums[0:2] + sums[2:4] + sums[4:6]
    rest = twice(sums[:, LANES:])
    return jnp.concatenate([sums[:, :LANES], rest, rest, rest], axis=0)


def begin_kernel(video, caches, same, sums, first, last, wide, held, alike, sem):
    layers, frames, rows, cols, channels = caches.shape
    copies = [pltpu.make_async_copy(video, held.at[0], sem.at[0])]
    for layer in range(layers):
        copies.append(
            pltpu.make_async_copy(caches.at[layer], held.at[layer + 1], sem.at[layer + 1])
        )
    fetch = pltpu.make_async_copy(same, alike, sem.at[layers + 1])
    for copy in copies + [fetch]:
        copy.start()
    half, places = channels - LANES, rows * cols
    total = [jnp.zeros((COLS, LANES), jnp.float32), jnp.zeros((COLS, half), jnp.float32)]
    square = list(total)
    for group, copy in enumerate(copies):
        copy.wait()
        for frame in range(frames):
            value = held[group, frame].astype(jnp.float32)
            parts = halves(value)
            if group == 0:
                for i in range(2):
                    total[i] = total[i] + jnp.sum(parts[i], axis=0)
                    square[i] = square[i] + jnp.sum(parts[i] * parts[i], axis=0)
            wide[frame] = parts[0].reshape(places, LANES)
            wide[2, :, HALF * frame : HALF * (frame + 1)] = parts[1].reshape(places, half)
        for out, column in ((first, 0), (last, cols - 1)):
            for plane in range(PLANES):
                edge = wide[plane, pl.ds(column, rows, stride=cols), :]
                out[group * PLANES + plane] = edge.astype(jnp.bfloat16)
    fetch.wait()
    both = group_sums([jnp.concatenate(v, axis=1) for v in (total, square)], alike[...])
    sums[...] = jnp.broadcast_to(both[None], sums.shape)


def cached_kernel(layer, chunk, far, caches, before, after, weights, bias, *refs):
    out, ordered, edges, *slabs, cache, weight, taps, sem = refs
    if far:
        away, out, *slabs = out, slabs[0], *slabs[1:]
    _, _, rows, cols, channels = caches.shape
    places = rows * cols
    begun = pltpu.make_async_copy(caches.at[layer], cache, sem.at[0])
    fetch = pltpu.make_async_copy(weights.at[layer], weight, sem.at[1])
    begun.start()
    fetch.start()
    begun.wait()
    for side, ref in enumerate((before, after)):
        for plane in range(PLANES):
            edges[side, plane] = ref[(layer + 1) * PLANES + plane].astype(jnp.float32)

    def row_of(h):
        return planes(*(cache[frame, h].astype(jnp.float32) for frame in range(2)))

    def edge_of(h, plane):
        return [edges[side, plane, pl.ds(h, COLS, stride=0), :] for side in (0, 1)]

    build_slabs(rows, row_of, edge_of, slabs)
    fetch.wait()
    for p in (1, 2, 0):
        taps[p] = tap_lanes(weight, p * 9 * channels, channels)
    store = pltpu.make_async_copy(taps.at[pl.ds(1, 2)], ordered, sem.at[2])
    store.start()
    constant = bias[layer : layer + 1, :]
    tables = [taps[p] for p in range(2)]
    value = product([(slabs[1], tables[0])], 0, places)
    put_planes(out, 1, pl.ds(0, places), value + constant)
    for start in range(0, places, chunk):
        value = product([(slabs[0], tables[0]), (slabs[1], tables[1])], start, chunk)
        put_planes(out, 0, pl.ds(start, chunk), value + constant)
    if far:
        leave = pltpu.make_async_copy(out, away, sem.at[3])
        leave.start()
        leave.wait()
    store.wait()


def active_kernel(layer, chunk, far, entries, final, *refs):
    x, before, after, stats, gain, shift, ordered, part, same = refs[:9]
    rest = refs[9:]
    residual = None
    if layer == 1:
        residual, *rest = rest
    if layer > 0:
        _, *rest = rest
    if final:
        y, carried, *rest = rest
    else:
        y, carried, sums, first, last, *rest = rest
    edges, *slabs, kept, held, taps, alike, sem = rest
    away = None
    if far:
        away, part, *slabs = part, *slabs
    frames, rows, cols, channels = kept.shape
    places = rows * cols
    fetch = [pltpu.make_async_copy(ordered, taps, sem.at[1])]
    if not final:
        fetch.append(pltpu.make_async_copy(same, alike, sem.at[4]))
    if far:
        fetch.append(pltpu.make_async_copy(away, part, sem.at[3]))
    if residual is not None:
        fetch.append(pltpu.make_async_copy(residual, held, sem.at[2]))
    for copy in fetch:
        copy.start()

    means = jnp.sum(stats[...], axis=0) / entries
    scales, offsets = [], []
    for index, lift in enumerate((lambda v: v, twice)):
        average = means[2 * index : 2 * index + 1]
        variance = means[2 * index + 1 : 2 * index + 2] - average * average
        scale = lax.rsqrt(variance + EPSILON) * lift(halves(gain[layer : layer + 1, :])[index])
        offset = lift(halves(shift[layer : layer + 1, :])[index]) - average * scale
        scales.append(0.5 * scale)
        offsets.append(0.5 * offset)
    scales, offsets = [[v[0], v[0], v[1]] for v in (scales, offsets)]

    def act(values):
        return [silu_of_twice(v * a + b) for v, a, b in zip(values, scales, offsets)]

    for side, ref in enumerate((before, after)):
        values = [ref[plane].astype(jnp.float32) for plane in range(PLANES)]
        for plane, value in enumerate(act(values)):
            edges[side, plane] = value

    def row_of(h):
        if layer:
            start = h * COLS if isinstance(h, int) else pl.multiple_of(h * COLS, COLS)
            return act([x[plane, pl.ds(start, COLS), :] for plane in range(PLANES)])
        return act(planes(*(x[frame, h].astype(jnp.float32) for frame in range(2))))

    def edge_of(h, plane):
        return [edges[side, plane, pl.ds(h, COLS, stride=0), :] for side in (0, 1)]

    def keep(h, *values):
        for frame in range(2):
            main, other = values[2 * frame : 2 * frame + 2]
            whole = jnp.concatenate([main, other[:, : channels - LANES]], axis=1)
            kept[frame, h] = whole.astype(jnp.bfloat16)

    build_slabs(rows, row_of, edge_of, slabs, keep)
    copy = pltpu.make_async_copy(kept, carried.at[layer], sem.at[0])
    copy.start()
    for one in fetch:
        one.wait()
    tables = [taps[p] for p in range(2)]
    moments = [jnp.zeros((COLS, channels), jnp.float32)] * 2

    def finish(t, start, size, value, moments):
        here, span = pl.ds(start, size), pl.ds(start // COLS, size // COLS)
        shape = (size // COLS, COLS, channels)
        value = value + get_planes(part, t, here)
        if final:
            value = value + get_planes(x, t, here)
            y[t, span] = value.reshape(shape).astype(jnp.bfloat16)
            return moments
        if residual is not None:
            value = value + held[t, span].astype(jnp.float32).reshape(size, channels)
        put_planes(y, t, here, value)
        folded = value.reshape(shape)
        return [
            moments[0] + jnp.sum(folded, axis=0),
            moments[1] + jnp.sum(folded * folded, axis=0),
        ]

    value = product([(slabs[0], tables[1])], 0, places)
    moments = finish(0, 0, places, value, moments)
    for start in range(0, places, chunk):
        value = product([(slabs[0], tables[0]), (slabs[1], tables[1])], start, chunk)
        moments = finish(1, start, chunk, value, moments)
    if not final:
        both = group_sums(moments, alike[...])
        sums[...] = jnp.broadcast_to(both[None], sums.shape)
        for plane in range(PLANES):
            for out, column in ((first, 0), (last, cols - 1)):
                edge = y[plane, pl.ds(column, rows, stride=cols), :]
                out[plane] = edge.astype(jnp.bfloat16)
    copy.wait()


def scratch(frames, rows, room):
    slab = pltpu.VMEM((SLABS, rows * COLS + 16, LANES), jnp.bfloat16)
    return [pltpu.VMEM((2, PLANES, rows, LANES), jnp.float32)] + room + [slab] * frames


def local(video_span, caches, norm_gains, shifts, weights, biases):
    peers = lax.axis_size("lon")
    frames, rows, cols, channels = video_span.shape
    layers = caches.shape[0]
    places = rows * cols
    entries = frames * places * peers * (channels // GROUPS)
    up = [(i, (i + 1) % peers) for i in range(peers)]
    down = [(j, i) for i, j in up]
    chunk = 720
    tiles = 14 * LANES

    def around(first, last):
        return lax.ppermute(last, "lon", up), lax.ppermute(first, "lon", down)

    def gathered(sums):
        return lax.all_to_all(sums, "lon", 0, 0)

    def in_hbm(value):
        return pltpu.with_memory_space_constraint(value, pltpu.HBM)

    turned = in_hbm(jnp.swapaxes(weights, 1, 2))
    caches, video = in_hbm(caches), in_hbm(video_span)
    members = channels // GROUPS
    alike = np.kron(np.eye(GROUPS), np.ones((members, members)))
    same = in_hbm(jnp.asarray(alike, jnp.bfloat16))
    spread = jax.ShapeDtypeStruct((peers, COLS, LANES), jnp.float32)
    brim = jax.ShapeDtypeStruct(((layers + 1) * PLANES, rows, LANES), jnp.bfloat16)
    sums, first, last = pl.pallas_call(
        begin_kernel,
        out_shape=[spread, brim, brim],
        in_specs=[HBM] * 3,
        out_specs=[VMEM] * 3,
        scratch_shapes=[
            pltpu.VMEM((PLANES, places, LANES), jnp.float32),
            pltpu.VMEM((layers + 1,) + video_span.shape, jnp.bfloat16),
            pltpu.VMEM(same.shape, same.dtype),
            pltpu.SemaphoreType.DMA((layers + 2,)),
        ],
        compiler_params=pltpu.CompilerParams(vmem_limit_bytes=24 << 20),
        name="begin",
    )(video, caches, same)
    brims = around(first, last)
    before, after = brims
    stats = gathered(sums)

    def room(far):
        return [pltpu.VMEM((PLANES, places, LANES), jnp.float32)] if far else []

    def cached_part(layer, far):
        planar = pltpu.HBM if far else jax.ShapeDtypeStruct
        return pl.pallas_call(
            functools.partial(cached_kernel, layer, chunk, far),
            out_shape=[
                planar((PLANES, places, LANES), jnp.float32),
                pltpu.HBM((2, channels, tiles), weights.dtype),
            ],
            in_specs=[HBM, VMEM, VMEM, HBM, VMEM],
            out_specs=[HBM if far else VMEM, HBM],
            scratch_shapes=scratch(frames, rows, room(far))
            + [
                pltpu.VMEM(video_span.shape, jnp.bfloat16),
                pltpu.VMEM((channels, weights.shape[1]), weights.dtype),
                pltpu.VMEM((3, channels, tiles), weights.dtype),
                pltpu.SemaphoreType.DMA((4,)),
            ],
            compiler_params=pltpu.CompilerParams(vmem_limit_bytes=24 << 20),
            name="cached",
        )(caches, *brims, turned, biases)

    x = video_span
    carried = None
    for layer in range(layers):
        final = layer == layers - 1
        far = 0 < layer < layers - 1
        part, ordered = cached_part(layer, far)
        if far:
            part = in_hbm(part)
        operands = [x, before, after, stats, norm_gains, shifts, in_hbm(ordered), part, same]
        specs = [VMEM] * 6 + [HBM, HBM if far else VMEM, HBM]
        aliases = {}
        if layer == 1:
            operands.append(video)
            specs.append(HBM)
        if layer > 0:
            aliases = {len(operands): 1}
            operands.append(carried)
            specs.append(HBM)
        state = jax.ShapeDtypeStruct((PLANES, places, LANES), jnp.float32)
        if final:
            state = jax.ShapeDtypeStruct(video_span.shape, jnp.bfloat16)
        outs = [state, jax.ShapeDtypeStruct(caches.shape, jnp.bfloat16)]
        out_specs = [VMEM, HBM]
        if not final:
            edge = jax.ShapeDtypeStruct((PLANES, rows, LANES), jnp.bfloat16)
            outs += [spread, edge, edge]
            out_specs += [VMEM] * 3
        results = pl.pallas_call(
            functools.partial(active_kernel, layer, chunk, far, entries, final),
            out_shape=outs,
            in_specs=specs,
            out_specs=out_specs,
            scratch_shapes=scratch(frames, rows, room(far))
            + [
                pltpu.VMEM(video_span.shape, jnp.bfloat16),
                pltpu.VMEM(video_span.shape, jnp.bfloat16),
                pltpu.VMEM((2, channels, tiles), weights.dtype),
                pltpu.VMEM(same.shape, same.dtype),
                pltpu.SemaphoreType.DMA((5,)),
            ],
            compiler_params=pltpu.CompilerParams(vmem_limit_bytes=24 << 20),
            input_output_aliases=aliases,
            name="active",
        )(*operands)
        x, carried = results[:2]
        if not final:
            stats = gathered(results[2])
            before, after = around(results[3], results[4])
    return x, carried


def solution(mesh):
    return jax.shard_map(
        local,
        mesh=mesh,
        in_specs=(
            P(None, "clips", "lon", None),
            P(None, None, "clips", "lon", None),
            P(),
            P(),
            P(),
            P(),
        ),
        out_specs=(P(None, "clips", "lon", None), P(None, None, "clips", "lon", None)),
        check_vma=False,
    )
```

```python
import functools

import jax
import jax.numpy as jnp
import numpy as np
from jax import lax
from jax.experimental import pallas as pl
from jax.experimental.pallas import tpu as pltpu
from jax.sharding import PartitionSpec as P

GROUPS = 32
EPSILON = 1e-06
LANES = 128
HALF = LANES // 2
COLS = 8
SLABS = 10
UNROLL = 11
PLANES = 3
VMEM = pl.BlockSpec(memory_space=pltpu.VMEM)
HBM = pl.BlockSpec(memory_space=pltpu.HBM)


def silu_of_twice(u):
    return u + u * jnp.tanh(u)


def twice(v):
    return jnp.concatenate([v, v], axis=-1)


def halves(value):
    return value[..., :LANES], value[..., LANES:]


def planes(first, second):
    (a, b), (c, d) = halves(first), halves(second)
    return a, c, jnp.concatenate([b, d], axis=-1)


def pair(a, b):
    return jnp.concatenate([a, b], axis=0).astype(jnp.bfloat16)


def build_slabs(rows, row_of, edge_of, slabs, keep=None):
    lane = lax.broadcasted_iota(jnp.int32, (COLS, LANES), 1)
    low = lane < HALF
    column = lax.broadcasted_iota(jnp.int32, (COLS, LANES), 0)
    first, last = column == 0, column == COLS - 1
    zero = jnp.zeros((COLS, LANES), jnp.float32)

    def shifted(h):
        out = []
        for plane, value in enumerate(row_of(h)):
            left, right = edge_of(h, plane)
            out.append(
                (
                    jnp.where(first, left, pltpu.roll(value, 1, 0)),
                    value,
                    jnp.where(last, right, pltpu.roll(value, COLS - 1, 0)),
                )
            )
        rest = out[2]
        swapped = [pltpu.roll(v, HALF, 1) for v in rest]
        if keep is not None:
            keep(h, out[0][1], rest[1], out[1][1], swapped[1])
        mains = out[0] + out[1]
        packed = (jnp.where(low, rest[0], swapped[1]), jnp.where(low, swapped[0], rest[1]))
        return mains, packed, (rest[2], swapped[2])

    def put(frame, index, k, value):
        start = k * 16 if isinstance(k, int) else pl.multiple_of(k * 16, 16)
        slabs[frame][index, pl.ds(start, 16), :] = value

    def around(frame, upper, lower):
        return jnp.where(low, upper[frame], lower[1 - frame])

    def step(k, carry):
        before, older, oldest = carry
        one, two = shifted(2 * k), shifted(2 * k + 1)
        for frame in range(2):
            for r in range(3):
                put(frame, r, k, pair(one[0][3 * frame + r], two[0][3 * frame + r]))
                put(frame, 3 + r, k, pair(before[0][3 * frame + r], one[0][3 * frame + r]))
            put(frame, 6, k, pair(one[1][frame], two[1][frame]))
            put(frame, 7, k, pair(before[1][frame], one[1][frame]))
            put(frame, 9, k, pair(one[2][frame], two[2][frame]))
            if older is not None:
                upper = around(frame, oldest, before[2])
                put(frame, 8, k - 1, pair(upper, around(frame, older, one[2])))
        return two, one[2], before[2]

    count = rows // 2
    carry = step(0, (((zero,) * 6, (zero,) * 2, (zero,) * 2), None, None))
    before, older, oldest = lax.fori_loop(1, count, step, carry, unroll=UNROLL)
    for frame in range(2):
        for r in range(3):
            put(frame, 3 + r, count, pair(before[0][3 * frame + r], zero))
        put(frame, 7, count, pair(before[1][frame], zero))
        upper = around(frame, oldest, before[2])
        put(frame, 8, count - 1, pair(upper, around(frame, older, (zero, zero))))


def slab_rows(slab, start, size):
    def at(index, step=0):
        return slab[index, pl.ds(start + step, size), :]

    tiles = [at(3 + r) for r in range(3)] + [at(r) for r in range(3)]
    tiles += [at(3 + r, 16) for r in range(3)]
    return tiles + [at(7), at(6), at(7, 16), at(8), at(9)]


def tap_lanes(weight, origin, channels):
    def at(q, r, start, size):
        return weight[:, pl.ds(origin + (q * 3 + r) * channels + start, size)]

    tiles = [at(q, r, 0, LANES) for q in range(3) for r in range(3)]
    for q in range(3):
        tiles += [at(q, 0, LANES, HALF), at(q, 1, LANES, HALF)]
    tiles += [at(0, 2, LANES, HALF), at(2, 2, LANES, HALF), at(1, 2, LANES, HALF)]
    tiles.append(jnp.zeros((weight.shape[0], HALF), weight.dtype))
    return jnp.concatenate(tiles, axis=1)


def product(pairs, start, size):
    left = [tile for slab, _ in pairs for tile in slab_rows(slab, start, size)]
    right = [taps for _, taps in pairs]
    return lax.dot_general(
        jnp.concatenate(left, axis=1),
        jnp.concatenate(right, axis=1),
        (((1,), (1,)), ((), ())),
        preferred_element_type=jnp.float32,
    )


def put_planes(out, t, here, value):
    main, rest = halves(value)
    out[t, here, :] = main
    out[2, here, HALF * t : HALF * (t + 1)] = rest


def get_planes(held, t, here):
    rest = held[2, here, HALF * t : HALF * (t + 1)]
    return jnp.concatenate([held[t, here, :], rest], axis=1)


def group_sums(pieces, same):
    total = jnp.concatenate([jnp.sum(v, axis=0, keepdims=True) for v in pieces], axis=0)
    high = total.astype(jnp.bfloat16)
    left = total - high.astype(jnp.float32)
    middle = left.astype(jnp.bfloat16)
    low = (left - middle.astype(jnp.float32)).astype(jnp.bfloat16)
    split = jnp.concatenate([high, middle, low], axis=0)
    sums = jnp.dot(split, same, preferred_element_type=jnp.float32)
    return sums[0:2] + sums[2:4] + sums[4:6]


def begin_kernel(video, caches, same, sums, first, last, wide, held, alike, sem):
    layers, frames, rows, cols, channels = caches.shape
    copies = [pltpu.make_async_copy(video, held.at[0], sem.at[0])]
    for layer in range(layers):
        copies.append(
            pltpu.make_async_copy(caches.at[layer], held.at[layer + 1], sem.at[layer + 1])
        )
    fetch = pltpu.make_async_copy(same, alike, sem.at[layers + 1])
    for copy in copies + [fetch]:
        copy.start()
    half, places = channels - LANES, rows * cols
    total = [jnp.zeros((COLS, LANES), jnp.float32), jnp.zeros((COLS, half), jnp.float32)]
    square = list(total)
    for group, copy in enumerate(copies):
        copy.wait()
        for frame in range(frames):
            value = held[group, frame].astype(jnp.float32)
            parts = halves(value)
            if group == 0:
                for i in range(2):
                    total[i] = total[i] + jnp.sum(parts[i], axis=0)
                    square[i] = square[i] + jnp.sum(parts[i] * parts[i], axis=0)
            wide[frame] = parts[0].reshape(places, LANES)
            wide[2, :, HALF * frame : HALF * (frame + 1)] = parts[1].reshape(places, half)
        for out, column in ((first, 0), (last, cols - 1)):
            for plane in range(PLANES):
                edge = wide[plane, pl.ds(column, rows, stride=cols), :]
                out[group * PLANES + plane] = edge.astype(jnp.bfloat16)
    fetch.wait()
    both = group_sums([jnp.concatenate(v, axis=1) for v in (total, square)], alike[...])
    sums[...] = jnp.broadcast_to(both[None], sums.shape)


def cached_kernel(layer, chunk, far, caches, before, after, weights, bias, *refs):
    out, ordered, edges, *slabs, cache, weight, taps, sem = refs
    if far:
        away, out, *slabs = out, slabs[0], *slabs[1:]
    _, _, rows, cols, channels = caches.shape
    places = rows * cols
    begun = pltpu.make_async_copy(caches.at[layer], cache, sem.at[0])
    fetch = pltpu.make_async_copy(weights.at[layer], weight, sem.at[1])
    begun.start()
    fetch.start()
    begun.wait()
    for side, ref in enumerate((before, after)):
        for plane in range(PLANES):
            edges[side, plane] = ref[(layer + 1) * PLANES + plane].astype(jnp.float32)

    def row_of(h):
        return planes(*(cache[frame, h].astype(jnp.float32) for frame in range(2)))

    def edge_of(h, plane):
        return [edges[side, plane, pl.ds(h, COLS, stride=0), :] for side in (0, 1)]

    build_slabs(rows, row_of, edge_of, slabs)
    fetch.wait()
    for p in (1, 2, 0):
        taps[p] = tap_lanes(weight, p * 9 * channels, channels)
    store = pltpu.make_async_copy(taps.at[pl.ds(1, 2)], ordered, sem.at[2])
    store.start()
    constant = bias[layer : layer + 1, :]
    tables = [taps[p] for p in range(2)]
    value = product([(slabs[1], tables[0])], 0, places)
    put_planes(out, 1, pl.ds(0, places), value + constant)
    for start in range(0, places, chunk):
        value = product([(slabs[0], tables[0]), (slabs[1], tables[1])], start, chunk)
        put_planes(out, 0, pl.ds(start, chunk), value + constant)
    if far:
        leave = pltpu.make_async_copy(out, away, sem.at[3])
        leave.start()
        leave.wait()
    store.wait()


def active_kernel(layer, chunk, far, entries, final, *refs):
    x, before, after, stats, gain, shift, ordered, part, same = refs[:9]
    rest = refs[9:]
    residual = None
    if layer == 1:
        residual, *rest = rest
    if layer > 0:
        _, *rest = rest
    if final:
        y, carried, *rest = rest
    else:
        y, carried, sums, first, last, *rest = rest
    edges, *slabs, kept, held, taps, alike, sem = rest
    away = None
    if far:
        away, part, *slabs = part, *slabs
    frames, rows, cols, channels = kept.shape
    places = rows * cols
    fetch = [pltpu.make_async_copy(ordered, taps, sem.at[1])]
    if not final:
        fetch.append(pltpu.make_async_copy(same, alike, sem.at[4]))
    if far:
        fetch.append(pltpu.make_async_copy(away, part, sem.at[3]))
    if residual is not None:
        fetch.append(pltpu.make_async_copy(residual, held, sem.at[2]))
    if not layer:
        source = pltpu.make_async_copy(x, held, sem.at[2])
        source.start()
    for copy in fetch:
        copy.start()

    means = jnp.sum(stats[...], axis=0) / entries
    average = means[0:1]
    variance = means[1:2] - average * average
    scale = lax.rsqrt(variance + EPSILON) * gain[layer : layer + 1, :]
    offset = shift[layer : layer + 1, :] - average * scale
    scale, offset = 0.5 * scale, 0.5 * offset
    scales = [scale[:, :LANES]] * 2 + [twice(scale[:, LANES:])]
    offsets = [offset[:, :LANES]] * 2 + [twice(offset[:, LANES:])]

    def act(values):
        return [silu_of_twice(v * a + b) for v, a, b in zip(values, scales, offsets)]

    for side, ref in enumerate((before, after)):
        values = [ref[plane].astype(jnp.float32) for plane in range(PLANES)]
        for plane, value in enumerate(act(values)):
            edges[side, plane] = value

    def row_of(h):
        if layer:
            start = h * COLS if isinstance(h, int) else pl.multiple_of(h * COLS, COLS)
            return act([x[plane, pl.ds(start, COLS), :] for plane in range(PLANES)])
        return act(planes(*(held[frame, h].astype(jnp.float32) for frame in range(2))))

    def edge_of(h, plane):
        return [edges[side, plane, pl.ds(h, COLS, stride=0), :] for side in (0, 1)]

    def keep(h, *values):
        for frame in range(2):
            main, other = values[2 * frame : 2 * frame + 2]
            whole = jnp.concatenate([main, other[:, : channels - LANES]], axis=1)
            kept[frame, h] = whole.astype(jnp.bfloat16)

    if not layer:
        source.wait()
    build_slabs(rows, row_of, edge_of, slabs, keep)
    copy = pltpu.make_async_copy(kept, carried.at[layer], sem.at[0])
    copy.start()
    for one in fetch:
        one.wait()
    tables = [taps[p] for p in range(2)]
    moments = [jnp.zeros((COLS, channels), jnp.float32)] * 2

    def finish(t, start, size, value, moments):
        here, span = pl.ds(start, size), pl.ds(start // COLS, size // COLS)
        shape = (size // COLS, COLS, channels)
        value = value + get_planes(part, t, here)
        if final:
            value = value + get_planes(x, t, here)
            y[t, span] = value.reshape(shape).astype(jnp.bfloat16)
            return moments
        if residual is not None:
            value = value + held[t, span].astype(jnp.float32).reshape(size, channels)
        put_planes(y, t, here, value)
        folded = value.reshape(shape)
        return [
            moments[0] + jnp.sum(folded, axis=0),
            moments[1] + jnp.sum(folded * folded, axis=0),
        ]

    value = product([(slabs[0], tables[1])], 0, places)
    moments = finish(0, 0, places, value, moments)
    for start in range(0, places, chunk):
        value = product([(slabs[0], tables[0]), (slabs[1], tables[1])], start, chunk)
        moments = finish(1, start, chunk, value, moments)
    if not final:
        both = group_sums(moments, alike[...])
        sums[...] = jnp.broadcast_to(both[None], sums.shape)
        for plane in range(PLANES):
            for out, column in ((first, 0), (last, cols - 1)):
                edge = y[plane, pl.ds(column, rows, stride=cols), :]
                out[plane] = edge.astype(jnp.bfloat16)
    copy.wait()


def scratch(frames, rows, room):
    slab = pltpu.VMEM((SLABS, rows * COLS + 16, LANES), jnp.bfloat16)
    return [pltpu.VMEM((2, PLANES, rows, LANES), jnp.float32)] + room + [slab] * frames


def local(video_span, caches, norm_gains, shifts, weights, biases):
    peers = lax.axis_size("lon")
    frames, rows, cols, channels = video_span.shape
    layers = caches.shape[0]
    places = rows * cols
    entries = frames * places * peers * (channels // GROUPS)
    up = [(i, (i + 1) % peers) for i in range(peers)]
    down = [(j, i) for i, j in up]
    chunk = 720
    tiles = 14 * LANES

    def around(first, last):
        return lax.ppermute(last, "lon", up), lax.ppermute(first, "lon", down)

    def gathered(sums):
        return lax.all_to_all(sums, "lon", 0, 0)

    def in_hbm(value):
        return pltpu.with_memory_space_constraint(value, pltpu.HBM)

    turned = in_hbm(jnp.swapaxes(weights, 1, 2))
    caches, video = in_hbm(caches), in_hbm(video_span)
    members = channels // GROUPS
    alike = np.kron(np.eye(GROUPS), np.ones((members, members)))
    same = in_hbm(jnp.asarray(alike, jnp.bfloat16))
    spread = jax.ShapeDtypeStruct((peers, 2, channels), jnp.float32)
    brim = jax.ShapeDtypeStruct(((layers + 1) * PLANES, rows, LANES), jnp.bfloat16)
    sums, first, last = pl.pallas_call(
        begin_kernel,
        out_shape=[spread, brim, brim],
        in_specs=[HBM] * 3,
        out_specs=[VMEM] * 3,
        scratch_shapes=[
            pltpu.VMEM((PLANES, places, LANES), jnp.float32),
            pltpu.VMEM((layers + 1,) + video_span.shape, jnp.bfloat16),
            pltpu.VMEM(same.shape, same.dtype),
            pltpu.SemaphoreType.DMA((layers + 2,)),
        ],
        compiler_params=pltpu.CompilerParams(vmem_limit_bytes=24 << 20),
        name="begin",
    )(video, caches, same)
    brims = around(first, last)
    before, after = brims
    stats = gathered(sums)

    def room(far):
        return [pltpu.VMEM((PLANES, places, LANES), jnp.float32)] if far else []

    def cached_part(layer, far):
        planar = pltpu.HBM if far else jax.ShapeDtypeStruct
        return pl.pallas_call(
            functools.partial(cached_kernel, layer, chunk, far),
            out_shape=[
                planar((PLANES, places, LANES), jnp.float32),
                pltpu.HBM((2, channels, tiles), weights.dtype),
            ],
            in_specs=[HBM, VMEM, VMEM, HBM, VMEM],
            out_specs=[HBM if far else VMEM, HBM],
            scratch_shapes=scratch(frames, rows, room(far))
            + [
                pltpu.VMEM(video_span.shape, jnp.bfloat16),
                pltpu.VMEM((channels, weights.shape[1]), weights.dtype),
                pltpu.VMEM((3, channels, tiles), weights.dtype),
                pltpu.SemaphoreType.DMA((4,)),
            ],
            compiler_params=pltpu.CompilerParams(vmem_limit_bytes=24 << 20),
            name="cached",
        )(caches, *brims, turned, biases)

    x = video
    carried = None
    for layer in range(layers):
        final = layer == layers - 1
        far = 0 < layer < layers - 1
        part, ordered = cached_part(layer, far)
        if far:
            part = in_hbm(part)
        operands = [x, before, after, stats, norm_gains, shifts, in_hbm(ordered), part, same]
        specs = [VMEM] * 6 + [HBM, HBM if far else VMEM, HBM]
        aliases = {}
        if not layer:
            specs[0] = HBM
        if layer == 1:
            operands.append(video)
            specs.append(HBM)
        if layer > 0:
            aliases = {len(operands): 1}
            operands.append(carried)
            specs.append(HBM)
        state = jax.ShapeDtypeStruct((PLANES, places, LANES), jnp.float32)
        if final:
            state = jax.ShapeDtypeStruct(video_span.shape, jnp.bfloat16)
        outs = [state, jax.ShapeDtypeStruct(caches.shape, jnp.bfloat16)]
        out_specs = [VMEM, HBM]
        if not final:
            edge = jax.ShapeDtypeStruct((PLANES, rows, LANES), jnp.bfloat16)
            outs += [spread, edge, edge]
            out_specs += [VMEM] * 3
        results = pl.pallas_call(
            functools.partial(active_kernel, layer, chunk, far, entries, final),
            out_shape=outs,
            in_specs=specs,
            out_specs=out_specs,
            scratch_shapes=scratch(frames, rows, room(far))
            + [
                pltpu.VMEM(video_span.shape, jnp.bfloat16),
                pltpu.VMEM(video_span.shape, jnp.bfloat16),
                pltpu.VMEM((2, channels, tiles), weights.dtype),
                pltpu.VMEM(same.shape, same.dtype),
                pltpu.SemaphoreType.DMA((5,)),
            ],
            compiler_params=pltpu.CompilerParams(vmem_limit_bytes=24 << 20),
            input_output_aliases=aliases,
            name="active",
        )(*operands)
        x, carried = results[:2]
        if not final:
            stats = gathered(results[2])
            before, after = around(results[3], results[4])
    return x, carried


def solution(mesh):
    return jax.shard_map(
        local,
        mesh=mesh,
        in_specs=(
            P(None, "clips", "lon", None),
            P(None, None, "clips", "lon", None),
            P(),
            P(),
            P(),
            P(),
        ),
        out_specs=(P(None, "clips", "lon", None), P(None, None, "clips", "lon", None)),
        check_vma=False,
    )
```

```python
import functools

import jax
import jax.numpy as jnp
import numpy as np
from jax import lax
from jax.experimental import pallas as pl
from jax.experimental.pallas import tpu as pltpu
from jax.sharding import PartitionSpec as P

GROUPS = 32
EPSILON = 1e-06
LANES = 128
HALF = LANES // 2
COLS = 8
SLABS = 10
UNROLL = 11
PLANES = 3
VMEM = pl.BlockSpec(memory_space=pltpu.VMEM)
HBM = pl.BlockSpec(memory_space=pltpu.HBM)


def silu_of_twice(u):
    return u + u * jnp.tanh(u)


def twice(v):
    return jnp.concatenate([v, v], axis=-1)


def halves(value):
    return value[..., :LANES], value[..., LANES:]


def planes(first, second):
    (a, b), (c, d) = halves(first), halves(second)
    return a, c, jnp.concatenate([b, d], axis=-1)


def pair(a, b):
    return jnp.concatenate([a, b], axis=0).astype(jnp.bfloat16)


def build_slabs(rows, row_of, edge_of, slabs, keep=None):
    lane = lax.broadcasted_iota(jnp.int32, (COLS, LANES), 1)
    low = lane < HALF
    column = lax.broadcasted_iota(jnp.int32, (COLS, LANES), 0)
    first, last = column == 0, column == COLS - 1
    zero = jnp.zeros((COLS, LANES), jnp.float32)

    def shifted(h):
        out = []
        for plane, value in enumerate(row_of(h)):
            left, right = edge_of(h, plane)
            out.append(
                (
                    jnp.where(first, left, pltpu.roll(value, 1, 0)),
                    value,
                    jnp.where(last, right, pltpu.roll(value, COLS - 1, 0)),
                )
            )
        rest = out[2]
        swapped = [pltpu.roll(v, HALF, 1) for v in rest]
        if keep is not None:
            keep(h, out[0][1], rest[1], out[1][1], swapped[1])
        mains = out[0] + out[1]
        packed = (jnp.where(low, rest[0], swapped[1]), jnp.where(low, swapped[0], rest[1]))
        return mains, packed, (rest[2], swapped[2])

    def put(frame, index, k, value):
        start = k * 16 if isinstance(k, int) else pl.multiple_of(k * 16, 16)
        slabs[frame][index, pl.ds(start, 16), :] = value

    def around(frame, upper, lower):
        return jnp.where(low, upper[frame], lower[1 - frame])

    def step(k, carry):
        before, older, oldest = carry
        one, two = shifted(2 * k), shifted(2 * k + 1)
        for frame in range(2):
            for r in range(3):
                put(frame, r, k, pair(one[0][3 * frame + r], two[0][3 * frame + r]))
                put(frame, 3 + r, k, pair(before[0][3 * frame + r], one[0][3 * frame + r]))
            put(frame, 6, k, pair(one[1][frame], two[1][frame]))
            put(frame, 7, k, pair(before[1][frame], one[1][frame]))
            put(frame, 9, k, pair(one[2][frame], two[2][frame]))
            if older is not None:
                upper = around(frame, oldest, before[2])
                put(frame, 8, k - 1, pair(upper, around(frame, older, one[2])))
        return two, one[2], before[2]

    count = rows // 2
    carry = step(0, (((zero,) * 6, (zero,) * 2, (zero,) * 2), None, None))
    before, older, oldest = lax.fori_loop(1, count, step, carry, unroll=UNROLL)
    for frame in range(2):
        for r in range(3):
            put(frame, 3 + r, count, pair(before[0][3 * frame + r], zero))
        put(frame, 7, count, pair(before[1][frame], zero))
        upper = around(frame, oldest, before[2])
        put(frame, 8, count - 1, pair(upper, around(frame, older, (zero, zero))))


def slab_rows(slab, start, size):
    def at(index, step=0):
        return slab[index, pl.ds(start + step, size), :]

    tiles = [at(3 + r) for r in range(3)] + [at(r) for r in range(3)]
    tiles += [at(3 + r, 16) for r in range(3)]
    return tiles + [at(7), at(6), at(7, 16), at(8), at(9)]


def tap_lanes(weight, origin, channels):
    def at(q, r, start, size):
        return weight[:, pl.ds(origin + (q * 3 + r) * channels + start, size)]

    tiles = [at(q, r, 0, LANES) for q in range(3) for r in range(3)]
    for q in range(3):
        tiles += [at(q, 0, LANES, HALF), at(q, 1, LANES, HALF)]
    tiles += [at(0, 2, LANES, HALF), at(2, 2, LANES, HALF), at(1, 2, LANES, HALF)]
    tiles.append(jnp.zeros((weight.shape[0], HALF), weight.dtype))
    return jnp.concatenate(tiles, axis=1)


def product(pairs, start, size):
    left = [tile for slab, _ in pairs for tile in slab_rows(slab, start, size)]
    right = [taps for _, taps in pairs]
    return lax.dot_general(
        jnp.concatenate(left, axis=1),
        jnp.concatenate(right, axis=1),
        (((1,), (1,)), ((), ())),
        preferred_element_type=jnp.float32,
    )


def put_planes(out, t, here, value):
    main, rest = halves(value)
    out[t, here, :] = main
    out[2, here, HALF * t : HALF * (t + 1)] = rest


def get_planes(held, t, here):
    rest = held[2, here, HALF * t : HALF * (t + 1)]
    return jnp.concatenate([held[t, here, :], rest], axis=1)


def group_sums(pieces, same):
    total = jnp.concatenate([jnp.sum(v, axis=0, keepdims=True) for v in pieces], axis=0)
    high = total.astype(jnp.bfloat16)
    left = total - high.astype(jnp.float32)
    middle = left.astype(jnp.bfloat16)
    low = (left - middle.astype(jnp.float32)).astype(jnp.bfloat16)
    split = jnp.concatenate([high, middle, low], axis=0)
    sums = jnp.dot(split, same, preferred_element_type=jnp.float32)
    return sums[0:2] + sums[2:4] + sums[4:6]


def begin_kernel(video, caches, same, sums, first, last, wide, held, alike, sem):
    layers, frames, rows, cols, channels = caches.shape
    copies = [pltpu.make_async_copy(video, held.at[0], sem.at[0])]
    for layer in range(layers):
        copies.append(
            pltpu.make_async_copy(caches.at[layer], held.at[layer + 1], sem.at[layer + 1])
        )
    fetch = pltpu.make_async_copy(same, alike, sem.at[layers + 1])
    for copy in copies + [fetch]:
        copy.start()
    half, places = channels - LANES, rows * cols
    total = [jnp.zeros((COLS, LANES), jnp.float32), jnp.zeros((COLS, half), jnp.float32)]
    square = list(total)
    for group, copy in enumerate(copies):
        copy.wait()
        for frame in range(frames):
            value = held[group, frame].astype(jnp.float32)
            parts = halves(value)
            if group == 0:
                for i in range(2):
                    total[i] = total[i] + jnp.sum(parts[i], axis=0)
                    square[i] = square[i] + jnp.sum(parts[i] * parts[i], axis=0)
            wide[frame] = parts[0].reshape(places, LANES)
            wide[2, :, HALF * frame : HALF * (frame + 1)] = parts[1].reshape(places, half)
        for out, column in ((first, 0), (last, cols - 1)):
            for plane in range(PLANES):
                edge = wide[plane, pl.ds(column, rows, stride=cols), :]
                out[group * PLANES + plane] = edge.astype(jnp.bfloat16)
    fetch.wait()
    both = group_sums([jnp.concatenate(v, axis=1) for v in (total, square)], alike[...])
    sums[...] = jnp.broadcast_to(both[None], sums.shape)


def cached_kernel(layer, chunk, far, caches, before, after, weights, bias, *refs):
    bring = None
    if layer == 0:
        video, out, ordered, near, *refs = refs
        refs = [out, ordered, *refs]
        bring = pltpu.make_async_copy(video, near, refs[-1].at[4])
    out, ordered, edges, *slabs, cache, weight, taps, sem = refs
    if far:
        away, out, *slabs = out, slabs[0], *slabs[1:]
    _, _, rows, cols, channels = caches.shape
    places = rows * cols
    begun = pltpu.make_async_copy(caches.at[layer], cache, sem.at[0])
    fetch = pltpu.make_async_copy(weights.at[layer], weight, sem.at[1])
    begun.start()
    fetch.start()
    if bring is not None:
        bring.start()
    begun.wait()
    for side, ref in enumerate((before, after)):
        for plane in range(PLANES):
            edges[side, plane] = ref[(layer + 1) * PLANES + plane].astype(jnp.float32)

    def row_of(h):
        return planes(*(cache[frame, h].astype(jnp.float32) for frame in range(2)))

    def edge_of(h, plane):
        return [edges[side, plane, pl.ds(h, COLS, stride=0), :] for side in (0, 1)]

    build_slabs(rows, row_of, edge_of, slabs)
    fetch.wait()
    for p in (1, 2, 0):
        taps[p] = tap_lanes(weight, p * 9 * channels, channels)
    store = pltpu.make_async_copy(taps.at[pl.ds(1, 2)], ordered, sem.at[2])
    store.start()
    constant = bias[layer : layer + 1, :]
    tables = [taps[p] for p in range(2)]
    value = product([(slabs[1], tables[0])], 0, places)
    put_planes(out, 1, pl.ds(0, places), value + constant)
    for start in range(0, places, chunk):
        value = product([(slabs[0], tables[0]), (slabs[1], tables[1])], start, chunk)
        put_planes(out, 0, pl.ds(start, chunk), value + constant)
    if far:
        leave = pltpu.make_async_copy(out, away, sem.at[3])
        leave.start()
        leave.wait()
    store.wait()
    if bring is not None:
        bring.wait()


def active_kernel(layer, chunk, far, entries, final, *refs):
    x, before, after, stats, gain, shift, ordered, part, same = refs[:9]
    rest = refs[9:]
    residual = None
    if layer == 1:
        residual, *rest = rest
    if layer > 0:
        _, *rest = rest
    if final:
        y, carried, *rest = rest
    else:
        y, carried, sums, first, last, *rest = rest
    edges, *slabs, kept, held, taps, alike, sem = rest
    away = None
    if far:
        away, part, *slabs = part, *slabs
    frames, rows, cols, channels = kept.shape
    places = rows * cols
    fetch = [pltpu.make_async_copy(ordered, taps, sem.at[1])]
    if not final:
        fetch.append(pltpu.make_async_copy(same, alike, sem.at[4]))
    if far:
        fetch.append(pltpu.make_async_copy(away, part, sem.at[3]))
    if residual is not None:
        fetch.append(pltpu.make_async_copy(residual, held, sem.at[2]))
    for copy in fetch:
        copy.start()

    means = jnp.sum(stats[...], axis=0) / entries
    average = means[0:1]
    variance = means[1:2] - average * average
    scale = lax.rsqrt(variance + EPSILON) * gain[layer : layer + 1, :]
    offset = shift[layer : layer + 1, :] - average * scale
    scale, offset = 0.5 * scale, 0.5 * offset
    scales = [scale[:, :LANES]] * 2 + [twice(scale[:, LANES:])]
    offsets = [offset[:, :LANES]] * 2 + [twice(offset[:, LANES:])]

    def act(values):
        return [silu_of_twice(v * a + b) for v, a, b in zip(values, scales, offsets)]

    for side, ref in enumerate((before, after)):
        values = [ref[plane].astype(jnp.float32) for plane in range(PLANES)]
        for plane, value in enumerate(act(values)):
            edges[side, plane] = value

    def row_of(h):
        if layer:
            start = h * COLS if isinstance(h, int) else pl.multiple_of(h * COLS, COLS)
            return act([x[plane, pl.ds(start, COLS), :] for plane in range(PLANES)])
        return act(planes(*(x[frame, h].astype(jnp.float32) for frame in range(2))))

    def edge_of(h, plane):
        return [edges[side, plane, pl.ds(h, COLS, stride=0), :] for side in (0, 1)]

    def keep(h, *values):
        for frame in range(2):
            main, other = values[2 * frame : 2 * frame + 2]
            whole = jnp.concatenate([main, other[:, : channels - LANES]], axis=1)
            kept[frame, h] = whole.astype(jnp.bfloat16)

    build_slabs(rows, row_of, edge_of, slabs, keep)
    copy = pltpu.make_async_copy(kept, carried.at[layer], sem.at[0])
    copy.start()
    for one in fetch:
        one.wait()
    tables = [taps[p] for p in range(2)]
    moments = [jnp.zeros((COLS, channels), jnp.float32)] * 2

    def finish(t, start, size, value, moments):
        here, span = pl.ds(start, size), pl.ds(start // COLS, size // COLS)
        shape = (size // COLS, COLS, channels)
        value = value + get_planes(part, t, here)
        if final:
            value = value + get_planes(x, t, here)
            y[t, span] = value.reshape(shape).astype(jnp.bfloat16)
            return moments
        if residual is not None:
            value = value + held[t, span].astype(jnp.float32).reshape(size, channels)
        put_planes(y, t, here, value)
        folded = value.reshape(shape)
        return [
            moments[0] + jnp.sum(folded, axis=0),
            moments[1] + jnp.sum(folded * folded, axis=0),
        ]

    value = product([(slabs[0], tables[1])], 0, places)
    moments = finish(0, 0, places, value, moments)
    for start in range(0, places, chunk):
        value = product([(slabs[0], tables[0]), (slabs[1], tables[1])], start, chunk)
        moments = finish(1, start, chunk, value, moments)
    if not final:
        both = group_sums(moments, alike[...])
        sums[...] = jnp.broadcast_to(both[None], sums.shape)
        for plane in range(PLANES):
            for out, column in ((first, 0), (last, cols - 1)):
                edge = y[plane, pl.ds(column, rows, stride=cols), :]
                out[plane] = edge.astype(jnp.bfloat16)
    copy.wait()


def scratch(frames, rows, room):
    slab = pltpu.VMEM((SLABS, rows * COLS + 16, LANES), jnp.bfloat16)
    return [pltpu.VMEM((2, PLANES, rows, LANES), jnp.float32)] + room + [slab] * frames


def local(video_span, caches, norm_gains, shifts, weights, biases):
    peers = lax.axis_size("lon")
    frames, rows, cols, channels = video_span.shape
    layers = caches.shape[0]
    places = rows * cols
    entries = frames * places * peers * (channels // GROUPS)
    up = [(i, (i + 1) % peers) for i in range(peers)]
    down = [(j, i) for i, j in up]
    chunk = 720
    tiles = 14 * LANES

    def around(first, last):
        return lax.ppermute(last, "lon", up), lax.ppermute(first, "lon", down)

    def gathered(sums):
        return lax.all_to_all(sums, "lon", 0, 0)

    def in_hbm(value):
        return pltpu.with_memory_space_constraint(value, pltpu.HBM)

    turned = in_hbm(jnp.swapaxes(weights, 1, 2))
    caches, video = in_hbm(caches), in_hbm(video_span)
    members = channels // GROUPS
    alike = np.kron(np.eye(GROUPS), np.ones((members, members)))
    same = in_hbm(jnp.asarray(alike, jnp.bfloat16))
    spread = jax.ShapeDtypeStruct((peers, 2, channels), jnp.float32)
    brim = jax.ShapeDtypeStruct(((layers + 1) * PLANES, rows, LANES), jnp.bfloat16)
    sums, first, last = pl.pallas_call(
        begin_kernel,
        out_shape=[spread, brim, brim],
        in_specs=[HBM] * 3,
        out_specs=[VMEM] * 3,
        scratch_shapes=[
            pltpu.VMEM((PLANES, places, LANES), jnp.float32),
            pltpu.VMEM((layers + 1,) + video_span.shape, jnp.bfloat16),
            pltpu.VMEM(same.shape, same.dtype),
            pltpu.SemaphoreType.DMA((layers + 2,)),
        ],
        compiler_params=pltpu.CompilerParams(vmem_limit_bytes=24 << 20),
        name="begin",
    )(video, caches, same)
    brims = around(first, last)
    before, after = brims
    stats = gathered(sums)

    def room(far):
        return [pltpu.VMEM((PLANES, places, LANES), jnp.float32)] if far else []

    def cached_part(layer, far):
        planar = pltpu.HBM if far else jax.ShapeDtypeStruct
        return pl.pallas_call(
            functools.partial(cached_kernel, layer, chunk, far),
            out_shape=[
                planar((PLANES, places, LANES), jnp.float32),
                pltpu.HBM((2, channels, tiles), weights.dtype),
            ]
            + ([] if layer else [jax.ShapeDtypeStruct(video_span.shape, video_span.dtype)]),
            in_specs=[HBM, VMEM, VMEM, HBM, VMEM] + ([] if layer else [HBM]),
            out_specs=[HBM if far else VMEM, HBM] + ([] if layer else [VMEM]),
            scratch_shapes=scratch(frames, rows, room(far))
            + [
                pltpu.VMEM(video_span.shape, jnp.bfloat16),
                pltpu.VMEM((channels, weights.shape[1]), weights.dtype),
                pltpu.VMEM((3, channels, tiles), weights.dtype),
                pltpu.SemaphoreType.DMA((5,)),
            ],
            compiler_params=pltpu.CompilerParams(vmem_limit_bytes=24 << 20),
            name="cached",
        )(caches, *brims, turned, biases, *([] if layer else [video]))

    x = None
    carried = None
    for layer in range(layers):
        final = layer == layers - 1
        far = layer < layers - 1
        part, ordered, *near = cached_part(layer, far)
        if near:
            x = near[0]
        if far:
            part = in_hbm(part)
        operands = [x, before, after, stats, norm_gains, shifts, in_hbm(ordered), part, same]
        specs = [VMEM] * 6 + [HBM, HBM if far else VMEM, HBM]
        aliases = {}
        if layer == 1:
            operands.append(video)
            specs.append(HBM)
        if layer > 0:
            aliases = {len(operands): 1}
            operands.append(carried)
            specs.append(HBM)
        state = jax.ShapeDtypeStruct((PLANES, places, LANES), jnp.float32)
        if final:
            state = jax.ShapeDtypeStruct(video_span.shape, jnp.bfloat16)
        outs = [state, jax.ShapeDtypeStruct(caches.shape, jnp.bfloat16)]
        out_specs = [VMEM, HBM]
        if not final:
            edge = jax.ShapeDtypeStruct((PLANES, rows, LANES), jnp.bfloat16)
            outs += [spread, edge, edge]
            out_specs += [VMEM] * 3
        results = pl.pallas_call(
            functools.partial(active_kernel, layer, chunk, far, entries, final),
            out_shape=outs,
            in_specs=specs,
            out_specs=out_specs,
            scratch_shapes=scratch(frames, rows, room(far))
            + [
                pltpu.VMEM(video_span.shape, jnp.bfloat16),
                pltpu.VMEM(video_span.shape, jnp.bfloat16),
                pltpu.VMEM((2, channels, tiles), weights.dtype),
                pltpu.VMEM(same.shape, same.dtype),
                pltpu.SemaphoreType.DMA((5,)),
            ],
            compiler_params=pltpu.CompilerParams(vmem_limit_bytes=24 << 20),
            input_output_aliases=aliases,
            name="active",
        )(*operands)
        x, carried = results[:2]
        if not final:
            stats = gathered(results[2])
            before, after = around(results[3], results[4])
    return x, carried


def solution(mesh):
    return jax.shard_map(
        local,
        mesh=mesh,
        in_specs=(
            P(None, "clips", "lon", None),
            P(None, None, "clips", "lon", None),
            P(),
            P(),
            P(),
            P(),
        ),
        out_specs=(P(None, "clips", "lon", None), P(None, None, "clips", "lon", None)),
        check_vma=False,
    )
```

```python
import functools

import jax
import jax.numpy as jnp
import numpy as np
from jax import lax
from jax.experimental import pallas as pl
from jax.experimental.pallas import tpu as pltpu
from jax.sharding import PartitionSpec as P

GROUPS = 32
EPSILON = 1e-06
LANES = 128
HALF = LANES // 2
COLS = 8
SLABS = 10
UNROLL = 11
PLANES = 3
VMEM = pl.BlockSpec(memory_space=pltpu.VMEM)
HBM = pl.BlockSpec(memory_space=pltpu.HBM)


def silu_of_twice(u):
    return u + u * jnp.tanh(u)


def twice(v):
    return jnp.concatenate([v, v], axis=-1)


def halves(value):
    return value[..., :LANES], value[..., LANES:]


def planes(first, second):
    (a, b), (c, d) = halves(first), halves(second)
    return a, c, jnp.concatenate([b, d], axis=-1)


def pair(a, b):
    return jnp.concatenate([a, b], axis=0).astype(jnp.bfloat16)


def build_slabs(rows, row_of, edge_of, slabs, keep=None):
    lane = lax.broadcasted_iota(jnp.int32, (COLS, LANES), 1)
    low = lane < HALF
    column = lax.broadcasted_iota(jnp.int32, (COLS, LANES), 0)
    first, last = column == 0, column == COLS - 1
    zero = jnp.zeros((COLS, LANES), jnp.float32)

    def shifted(h):
        out = []
        for plane, value in enumerate(row_of(h)):
            left, right = edge_of(h, plane)
            out.append(
                (
                    jnp.where(first, left, pltpu.roll(value, 1, 0)),
                    value,
                    jnp.where(last, right, pltpu.roll(value, COLS - 1, 0)),
                )
            )
        rest = out[2]
        swapped = [pltpu.roll(v, HALF, 1) for v in rest]
        if keep is not None:
            keep(h, out[0][1], rest[1], out[1][1], swapped[1])
        mains = out[0] + out[1]
        packed = (jnp.where(low, rest[0], swapped[1]), jnp.where(low, swapped[0], rest[1]))
        return mains, packed, (rest[2], swapped[2])

    def put(frame, index, k, value):
        start = k * 16 if isinstance(k, int) else pl.multiple_of(k * 16, 16)
        slabs[frame][index, pl.ds(start, 16), :] = value

    def around(frame, upper, lower):
        return jnp.where(low, upper[frame], lower[1 - frame])

    def step(k, carry):
        before, older, oldest = carry
        one, two = shifted(2 * k), shifted(2 * k + 1)
        for frame in range(2):
            for r in range(3):
                put(frame, r, k, pair(one[0][3 * frame + r], two[0][3 * frame + r]))
                put(frame, 3 + r, k, pair(before[0][3 * frame + r], one[0][3 * frame + r]))
            put(frame, 6, k, pair(one[1][frame], two[1][frame]))
            put(frame, 7, k, pair(before[1][frame], one[1][frame]))
            put(frame, 9, k, pair(one[2][frame], two[2][frame]))
            if older is not None:
                upper = around(frame, oldest, before[2])
                put(frame, 8, k - 1, pair(upper, around(frame, older, one[2])))
        return two, one[2], before[2]

    count = rows // 2
    carry = step(0, (((zero,) * 6, (zero,) * 2, (zero,) * 2), None, None))
    before, older, oldest = lax.fori_loop(1, count, step, carry, unroll=UNROLL)
    for frame in range(2):
        for r in range(3):
            put(frame, 3 + r, count, pair(before[0][3 * frame + r], zero))
        put(frame, 7, count, pair(before[1][frame], zero))
        upper = around(frame, oldest, before[2])
        put(frame, 8, count - 1, pair(upper, around(frame, older, (zero, zero))))


def slab_rows(slab, start, size):
    def at(index, step=0):
        return slab[index, pl.ds(start + step, size), :]

    tiles = [at(3 + r) for r in range(3)] + [at(r) for r in range(3)]
    tiles += [at(3 + r, 16) for r in range(3)]
    return tiles + [at(7), at(6), at(7, 16), at(8), at(9)]


def tap_lanes(weight, origin, channels):
    def at(q, r, start, size):
        return weight[:, pl.ds(origin + (q * 3 + r) * channels + start, size)]

    tiles = [at(q, r, 0, LANES) for q in range(3) for r in range(3)]
    for q in range(3):
        tiles += [at(q, 0, LANES, HALF), at(q, 1, LANES, HALF)]
    tiles += [at(0, 2, LANES, HALF), at(2, 2, LANES, HALF), at(1, 2, LANES, HALF)]
    tiles.append(jnp.zeros((weight.shape[0], HALF), weight.dtype))
    return jnp.concatenate(tiles, axis=1)


def product(pairs, start, size):
    left = [tile for slab, _ in pairs for tile in slab_rows(slab, start, size)]
    right = [taps for _, taps in pairs]
    return lax.dot_general(
        jnp.concatenate(left, axis=1),
        jnp.concatenate(right, axis=1),
        (((1,), (1,)), ((), ())),
        preferred_element_type=jnp.float32,
    )


def put_planes(out, t, here, value):
    main, rest = halves(value)
    out[t, here, :] = main
    out[2, here, HALF * t : HALF * (t + 1)] = rest


def get_planes(held, t, here):
    rest = held[2, here, HALF * t : HALF * (t + 1)]
    return jnp.concatenate([held[t, here, :], rest], axis=1)


def group_sums(pieces, same):
    total = jnp.concatenate([jnp.sum(v, axis=0, keepdims=True) for v in pieces], axis=0)
    high = total.astype(jnp.bfloat16)
    left = total - high.astype(jnp.float32)
    middle = left.astype(jnp.bfloat16)
    low = (left - middle.astype(jnp.float32)).astype(jnp.bfloat16)
    split = jnp.concatenate([high, middle, low], axis=0)
    sums = jnp.dot(split, same, preferred_element_type=jnp.float32)
    return sums[0:2] + sums[2:4] + sums[4:6]


def begin_kernel(video, caches, same, sums, first, last, near, wide, held, alike, sem):
    layers, frames, rows, cols, channels = caches.shape
    copies = [pltpu.make_async_copy(video, held.at[0], sem.at[0])]
    for layer in range(layers):
        target = held.at[layer + 1] if layer else near
        copies.append(pltpu.make_async_copy(caches.at[layer], target, sem.at[layer + 1]))
    fetch = pltpu.make_async_copy(same, alike, sem.at[layers + 1])
    for copy in copies + [fetch]:
        copy.start()
    half, places = channels - LANES, rows * cols
    total = [jnp.zeros((COLS, LANES), jnp.float32), jnp.zeros((COLS, half), jnp.float32)]
    square = list(total)
    for group, copy in enumerate(copies):
        copy.wait()
        for frame in range(frames):
            value = (near[frame] if group == 1 else held[group, frame]).astype(jnp.float32)
            parts = halves(value)
            if group == 0:
                for i in range(2):
                    total[i] = total[i] + jnp.sum(parts[i], axis=0)
                    square[i] = square[i] + jnp.sum(parts[i] * parts[i], axis=0)
            wide[frame] = parts[0].reshape(places, LANES)
            wide[2, :, HALF * frame : HALF * (frame + 1)] = parts[1].reshape(places, half)
        for out, column in ((first, 0), (last, cols - 1)):
            for plane in range(PLANES):
                edge = wide[plane, pl.ds(column, rows, stride=cols), :]
                out[group * PLANES + plane] = edge.astype(jnp.bfloat16)
    fetch.wait()
    both = group_sums([jnp.concatenate(v, axis=1) for v in (total, square)], alike[...])
    sums[...] = jnp.broadcast_to(both[None], sums.shape)


def cached_kernel(layer, chunk, far, distant, cache, before, after, weights, bias, *refs):
    bring = None
    if layer == 0:
        video, out, ordered, near, *refs = refs
        refs = [out, ordered, *refs]
        bring = pltpu.make_async_copy(video, near, refs[-1].at[4])
    if distant:
        caches, out, ordered, cache, *refs = cache, *refs
        refs = [out, ordered, *refs]
    out, ordered, edges, *slabs, weight, taps, sem = refs
    if far:
        away, out, *slabs = out, slabs[0], *slabs[1:]
    rows, cols, channels = cache.shape[-3:]
    places = rows * cols
    fetch = pltpu.make_async_copy(weights.at[layer], weight, sem.at[1])
    if distant:
        begun = pltpu.make_async_copy(caches.at[layer], cache, sem.at[0])
        begun.start()
    fetch.start()
    if bring is not None:
        bring.start()
    if distant:
        begun.wait()
    for side, ref in enumerate((before, after)):
        for plane in range(PLANES):
            edges[side, plane] = ref[(layer + 1) * PLANES + plane].astype(jnp.float32)

    def row_of(h):
        return planes(*(cache[frame, h].astype(jnp.float32) for frame in range(2)))

    def edge_of(h, plane):
        return [edges[side, plane, pl.ds(h, COLS, stride=0), :] for side in (0, 1)]

    build_slabs(rows, row_of, edge_of, slabs)
    fetch.wait()
    for p in (1, 2, 0):
        taps[p] = tap_lanes(weight, p * 9 * channels, channels)
    store = pltpu.make_async_copy(taps.at[pl.ds(1, 2)], ordered, sem.at[2])
    store.start()
    constant = bias[layer : layer + 1, :]
    tables = [taps[p] for p in range(2)]
    value = product([(slabs[1], tables[0])], 0, places)
    put_planes(out, 1, pl.ds(0, places), value + constant)
    for start in range(0, places, chunk):
        value = product([(slabs[0], tables[0]), (slabs[1], tables[1])], start, chunk)
        put_planes(out, 0, pl.ds(start, chunk), value + constant)
    if far:
        leave = pltpu.make_async_copy(out, away, sem.at[3])
        leave.start()
        leave.wait()
    store.wait()
    if bring is not None:
        bring.wait()


def active_kernel(layer, chunk, far, bring, entries, final, *refs):
    x, before, after, stats, gain, shift, ordered, part, same = refs[:9]
    rest = refs[9:]
    residual = None
    if layer == 1:
        residual, *rest = rest
    if layer > 0:
        _, *rest = rest
    if final:
        y, carried, *rest = rest
    else:
        if bring:
            caches, *rest = rest
        y, carried, sums, first, last, *rest = rest
        if bring:
            near, *rest = rest
    edges, *slabs, kept, held, taps, alike, sem = rest
    away = None
    if far:
        away, part, *slabs = part, *slabs
    frames, rows, cols, channels = kept.shape
    places = rows * cols
    fetch, late = [pltpu.make_async_copy(ordered, taps, sem.at[1])], []
    if far:
        fetch.append(pltpu.make_async_copy(away, part, sem.at[3]))
    if residual is not None:
        fetch.append(pltpu.make_async_copy(residual, held, sem.at[2]))
    if not final:
        late.append(pltpu.make_async_copy(same, alike, sem.at[4]))
    if bring:
        late.append(pltpu.make_async_copy(caches.at[layer + 1], near, sem.at[5]))
    for copy in fetch + late:
        copy.start()

    means = jnp.sum(stats[...], axis=0) / entries
    average = means[0:1]
    variance = means[1:2] - average * average
    scale = lax.rsqrt(variance + EPSILON) * gain[layer : layer + 1, :]
    offset = shift[layer : layer + 1, :] - average * scale
    scale, offset = 0.5 * scale, 0.5 * offset
    scales = [scale[:, :LANES]] * 2 + [twice(scale[:, LANES:])]
    offsets = [offset[:, :LANES]] * 2 + [twice(offset[:, LANES:])]

    def act(values):
        return [silu_of_twice(v * a + b) for v, a, b in zip(values, scales, offsets)]

    for side, ref in enumerate((before, after)):
        values = [ref[plane].astype(jnp.float32) for plane in range(PLANES)]
        for plane, value in enumerate(act(values)):
            edges[side, plane] = value

    def row_of(h):
        if layer:
            start = h * COLS if isinstance(h, int) else pl.multiple_of(h * COLS, COLS)
            return act([x[plane, pl.ds(start, COLS), :] for plane in range(PLANES)])
        return act(planes(*(x[frame, h].astype(jnp.float32) for frame in range(2))))

    def edge_of(h, plane):
        return [edges[side, plane, pl.ds(h, COLS, stride=0), :] for side in (0, 1)]

    def keep(h, *values):
        for frame in range(2):
            main, other = values[2 * frame : 2 * frame + 2]
            whole = jnp.concatenate([main, other[:, : channels - LANES]], axis=1)
            kept[frame, h] = whole.astype(jnp.bfloat16)

    build_slabs(rows, row_of, edge_of, slabs, keep)
    copy = pltpu.make_async_copy(kept, carried.at[layer], sem.at[0])
    copy.start()
    for one in fetch:
        one.wait()
    tables = [taps[p] for p in range(2)]
    moments = [jnp.zeros((COLS, channels), jnp.float32)] * 2

    def finish(t, start, size, value, moments):
        here, span = pl.ds(start, size), pl.ds(start // COLS, size // COLS)
        shape = (size // COLS, COLS, channels)
        value = value + get_planes(part, t, here)
        if final:
            value = value + get_planes(x, t, here)
            y[t, span] = value.reshape(shape).astype(jnp.bfloat16)
            return moments
        if residual is not None:
            value = value + held[t, span].astype(jnp.float32).reshape(size, channels)
        put_planes(y, t, here, value)
        folded = value.reshape(shape)
        return [
            moments[0] + jnp.sum(folded, axis=0),
            moments[1] + jnp.sum(folded * folded, axis=0),
        ]

    value = product([(slabs[0], tables[1])], 0, places)
    moments = finish(0, 0, places, value, moments)
    for start in range(0, places, chunk):
        value = product([(slabs[0], tables[0]), (slabs[1], tables[1])], start, chunk)
        moments = finish(1, start, chunk, value, moments)
    if not final:
        for one in late:
            one.wait()
        both = group_sums(moments, alike[...])
        sums[...] = jnp.broadcast_to(both[None], sums.shape)
        for plane in range(PLANES):
            for out, column in ((first, 0), (last, cols - 1)):
                edge = y[plane, pl.ds(column, rows, stride=cols), :]
                out[plane] = edge.astype(jnp.bfloat16)
    copy.wait()


def scratch(frames, rows, room):
    slab = pltpu.VMEM((SLABS, rows * COLS + 16, LANES), jnp.bfloat16)
    return [pltpu.VMEM((2, PLANES, rows, LANES), jnp.float32)] + room + [slab] * frames


def local(video_span, caches, norm_gains, shifts, weights, biases):
    peers = lax.axis_size("lon")
    frames, rows, cols, channels = video_span.shape
    layers = caches.shape[0]
    places = rows * cols
    entries = frames * places * peers * (channels // GROUPS)
    up = [(i, (i + 1) % peers) for i in range(peers)]
    down = [(j, i) for i, j in up]
    chunk = 720
    tiles = 14 * LANES

    def around(first, last):
        return lax.ppermute(last, "lon", up), lax.ppermute(first, "lon", down)

    def gathered(sums):
        return lax.all_to_all(sums, "lon", 0, 0)

    def in_hbm(value):
        return pltpu.with_memory_space_constraint(value, pltpu.HBM)

    turned = in_hbm(jnp.swapaxes(weights, 1, 2))
    caches, video = in_hbm(caches), in_hbm(video_span)
    members = channels // GROUPS
    alike = np.kron(np.eye(GROUPS), np.ones((members, members)))
    same = in_hbm(jnp.asarray(alike, jnp.bfloat16))
    spread = jax.ShapeDtypeStruct((peers, 2, channels), jnp.float32)
    brim = jax.ShapeDtypeStruct(((layers + 1) * PLANES, rows, LANES), jnp.bfloat16)
    block = jax.ShapeDtypeStruct(video_span.shape, video_span.dtype)
    sums, first, last, cache = pl.pallas_call(
        begin_kernel,
        out_shape=[spread, brim, brim, block],
        in_specs=[HBM] * 3,
        out_specs=[VMEM] * 4,
        scratch_shapes=[
            pltpu.VMEM((PLANES, places, LANES), jnp.float32),
            pltpu.VMEM((layers + 1,) + video_span.shape, jnp.bfloat16),
            pltpu.VMEM(same.shape, same.dtype),
            pltpu.SemaphoreType.DMA((layers + 2,)),
        ],
        compiler_params=pltpu.CompilerParams(vmem_limit_bytes=24 << 20),
        name="begin",
    )(video, caches, same)
    brims = around(first, last)
    before, after = brims
    stats = gathered(sums)

    def room(far):
        return [pltpu.VMEM((PLANES, places, LANES), jnp.float32)] if far else []

    def cached_part(layer, far, cache):
        distant = cache is None
        own = [pltpu.VMEM(video_span.shape, jnp.bfloat16)] if distant else []
        planar = pltpu.HBM if far else jax.ShapeDtypeStruct
        return pl.pallas_call(
            functools.partial(cached_kernel, layer, chunk, far, distant),
            out_shape=[
                planar((PLANES, places, LANES), jnp.float32),
                pltpu.HBM((2, channels, tiles), weights.dtype),
            ]
            + ([] if layer else [block]),
            in_specs=[HBM if distant else VMEM, VMEM, VMEM, HBM, VMEM]
            + ([] if layer else [HBM]),
            out_specs=[HBM if far else VMEM, HBM] + ([] if layer else [VMEM]),
            scratch_shapes=own + scratch(frames, rows, room(far))
            + [
                pltpu.VMEM((channels, weights.shape[1]), weights.dtype),
                pltpu.VMEM((3, channels, tiles), weights.dtype),
                pltpu.SemaphoreType.DMA((5,)),
            ],
            compiler_params=pltpu.CompilerParams(vmem_limit_bytes=24 << 20),
            name="cached",
        )(caches if distant else cache, *brims, turned, biases, *([] if layer else [video]))

    x = None
    carried = None
    for layer in range(layers):
        final = layer == layers - 1
        far = layer < layers - 1
        bring = layer < layers - 2
        part, ordered, *near = cached_part(layer, far, cache)
        if near:
            x = near[0]
        if far:
            part = in_hbm(part)
        operands = [x, before, after, stats, norm_gains, shifts, in_hbm(ordered), part, same]
        specs = [VMEM] * 6 + [HBM, HBM if far else VMEM, HBM]
        aliases = {}
        if layer == 1:
            operands.append(video)
            specs.append(HBM)
        if layer > 0:
            aliases = {len(operands): 1}
            operands.append(carried)
            specs.append(HBM)
        state = jax.ShapeDtypeStruct((PLANES, places, LANES), jnp.float32)
        if final:
            state = jax.ShapeDtypeStruct(video_span.shape, jnp.bfloat16)
        outs = [state, jax.ShapeDtypeStruct(caches.shape, jnp.bfloat16)]
        out_specs = [VMEM, HBM]
        if not final:
            edge = jax.ShapeDtypeStruct((PLANES, rows, LANES), jnp.bfloat16)
            outs += [spread, edge, edge]
            out_specs += [VMEM] * 3
        if bring:
            outs.append(block)
            out_specs.append(VMEM)
            operands.append(caches)
            specs.append(HBM)
        results = pl.pallas_call(
            functools.partial(active_kernel, layer, chunk, far, bring, entries, final),
            out_shape=outs,
            in_specs=specs,
            out_specs=out_specs,
            scratch_shapes=scratch(frames, rows, room(far))
            + [
                pltpu.VMEM(video_span.shape, jnp.bfloat16),
                pltpu.VMEM(video_span.shape, jnp.bfloat16),
                pltpu.VMEM((2, channels, tiles), weights.dtype),
                pltpu.VMEM(same.shape, same.dtype),
                pltpu.SemaphoreType.DMA((6,)),
            ],
            compiler_params=pltpu.CompilerParams(vmem_limit_bytes=24 << 20),
            input_output_aliases=aliases,
            name="active",
        )(*operands)
        x, carried = results[:2]
        if not final:
            stats = gathered(results[2])
            before, after = around(results[3], results[4])
            cache = results[5] if bring else None
    return x, carried


def solution(mesh):
    return jax.shard_map(
        local,
        mesh=mesh,
        in_specs=(
            P(None, "clips", "lon", None),
            P(None, None, "clips", "lon", None),
            P(),
            P(),
            P(),
            P(),
        ),
        out_specs=(P(None, "clips", "lon", None), P(None, None, "clips", "lon", None)),
        check_vma=False,
    )
```

```python
import functools

import jax
import jax.numpy as jnp
import numpy as np
from jax import lax
from jax.experimental import pallas as pl
from jax.experimental.pallas import tpu as pltpu
from jax.sharding import PartitionSpec as P

GROUPS = 32
EPSILON = 1e-06
LANES = 128
HALF = LANES // 2
COLS = 8
SLABS = 10
UNROLL = 11
PLANES = 3
VMEM = pl.BlockSpec(memory_space=pltpu.VMEM)
HBM = pl.BlockSpec(memory_space=pltpu.HBM)


def silu_of_twice(u):
    return u + u * jnp.tanh(u)


def twice(v):
    return jnp.concatenate([v, v], axis=-1)


def halves(value):
    return value[..., :LANES], value[..., LANES:]


def planes(first, second):
    (a, b), (c, d) = halves(first), halves(second)
    return a, c, jnp.concatenate([b, d], axis=-1)


def pair(a, b):
    return jnp.concatenate([a, b], axis=0).astype(jnp.bfloat16)


def build_slabs(rows, row_of, edge_of, slabs, keep=None):
    lane = lax.broadcasted_iota(jnp.int32, (COLS, LANES), 1)
    low = lane < HALF
    column = lax.broadcasted_iota(jnp.int32, (COLS, LANES), 0)
    first, last = column == 0, column == COLS - 1
    zero = jnp.zeros((COLS, LANES), jnp.float32)

    def shifted(h):
        out = []
        for plane, value in enumerate(row_of(h)):
            left, right = edge_of(h, plane)
            out.append(
                (
                    jnp.where(first, left, pltpu.roll(value, 1, 0)),
                    value,
                    jnp.where(last, right, pltpu.roll(value, COLS - 1, 0)),
                )
            )
        rest = out[2]
        swapped = [pltpu.roll(v, HALF, 1) for v in rest]
        if keep is not None:
            keep(h, out[0][1], rest[1], out[1][1], swapped[1])
        mains = out[0] + out[1]
        packed = (jnp.where(low, rest[0], swapped[1]), jnp.where(low, swapped[0], rest[1]))
        return mains, packed, (rest[2], swapped[2])

    def put(frame, index, k, value):
        start = k * 16 if isinstance(k, int) else pl.multiple_of(k * 16, 16)
        slabs[frame][index, pl.ds(start, 16), :] = value

    def around(frame, upper, lower):
        return jnp.where(low, upper[frame], lower[1 - frame])

    def step(k, carry):
        before, older, oldest = carry
        one, two = shifted(2 * k), shifted(2 * k + 1)
        for frame in range(2):
            for r in range(3):
                put(frame, r, k, pair(one[0][3 * frame + r], two[0][3 * frame + r]))
                put(frame, 3 + r, k, pair(before[0][3 * frame + r], one[0][3 * frame + r]))
            put(frame, 6, k, pair(one[1][frame], two[1][frame]))
            put(frame, 7, k, pair(before[1][frame], one[1][frame]))
            put(frame, 9, k, pair(one[2][frame], two[2][frame]))
            if older is not None:
                upper = around(frame, oldest, before[2])
                put(frame, 8, k - 1, pair(upper, around(frame, older, one[2])))
        return two, one[2], before[2]

    count = rows // 2
    carry = step(0, (((zero,) * 6, (zero,) * 2, (zero,) * 2), None, None))
    before, older, oldest = lax.fori_loop(1, count, step, carry, unroll=UNROLL)
    for frame in range(2):
        for r in range(3):
            put(frame, 3 + r, count, pair(before[0][3 * frame + r], zero))
        put(frame, 7, count, pair(before[1][frame], zero))
        upper = around(frame, oldest, before[2])
        put(frame, 8, count - 1, pair(upper, around(frame, older, (zero, zero))))


def slab_rows(slab, start, size):
    def at(index, step=0):
        return slab[index, pl.ds(start + step, size), :]

    tiles = [at(3 + r) for r in range(3)] + [at(r) for r in range(3)]
    tiles += [at(3 + r, 16) for r in range(3)]
    return tiles + [at(7), at(6), at(7, 16), at(8), at(9)]


def tap_lanes(weight, origin, channels):
    def at(q, r, start, size):
        return weight[:, pl.ds(origin + (q * 3 + r) * channels + start, size)]

    tiles = [at(q, r, 0, LANES) for q in range(3) for r in range(3)]
    for q in range(3):
        tiles += [at(q, 0, LANES, HALF), at(q, 1, LANES, HALF)]
    tiles += [at(0, 2, LANES, HALF), at(2, 2, LANES, HALF), at(1, 2, LANES, HALF)]
    tiles.append(jnp.zeros((weight.shape[0], HALF), weight.dtype))
    return jnp.concatenate(tiles, axis=1)


def product(pairs, start, size):
    left = [tile for slab, _ in pairs for tile in slab_rows(slab, start, size)]
    right = [taps for _, taps in pairs]
    return lax.dot_general(
        jnp.concatenate(left, axis=1),
        jnp.concatenate(right, axis=1),
        (((1,), (1,)), ((), ())),
        preferred_element_type=jnp.float32,
    )


def put_planes(out, t, here, value):
    main, rest = halves(value)
    out[t, here, :] = main
    out[2, here, HALF * t : HALF * (t + 1)] = rest


def get_planes(held, t, here):
    rest = held[2, here, HALF * t : HALF * (t + 1)]
    return jnp.concatenate([held[t, here, :], rest], axis=1)


def group_sums(pieces, same):
    total = jnp.concatenate([jnp.sum(v, axis=0, keepdims=True) for v in pieces], axis=0)
    high = total.astype(jnp.bfloat16)
    left = total - high.astype(jnp.float32)
    middle = left.astype(jnp.bfloat16)
    low = (left - middle.astype(jnp.float32)).astype(jnp.bfloat16)
    split = jnp.concatenate([high, middle, low], axis=0)
    sums = jnp.dot(split, same, preferred_element_type=jnp.float32)
    return sums[0:2] + sums[2:4] + sums[4:6]


def begin_kernel(video, caches, same, sums, first, last, near, wide, held, alike, sem):
    layers, frames, rows, cols, channels = caches.shape
    copies = [pltpu.make_async_copy(video, held.at[0], sem.at[0])]
    for layer in range(layers):
        target = held.at[layer + 1] if layer else near
        copies.append(pltpu.make_async_copy(caches.at[layer], target, sem.at[layer + 1]))
    fetch = pltpu.make_async_copy(same, alike, sem.at[layers + 1])
    for copy in copies + [fetch]:
        copy.start()
    half, places = channels - LANES, rows * cols
    total = [jnp.zeros((COLS, LANES), jnp.float32), jnp.zeros((COLS, half), jnp.float32)]
    square = list(total)
    for group, copy in enumerate(copies):
        copy.wait()
        for frame in range(frames):
            value = (near[frame] if group == 1 else held[group, frame]).astype(jnp.float32)
            parts = halves(value)
            if group == 0:
                for i in range(2):
                    total[i] = total[i] + jnp.sum(parts[i], axis=0)
                    square[i] = square[i] + jnp.sum(parts[i] * parts[i], axis=0)
            wide[frame] = parts[0].reshape(places, LANES)
            wide[2, :, HALF * frame : HALF * (frame + 1)] = parts[1].reshape(places, half)
        for out, column in ((first, 0), (last, cols - 1)):
            for plane in range(PLANES):
                edge = wide[plane, pl.ds(column, rows, stride=cols), :]
                out[group * PLANES + plane] = edge.astype(jnp.bfloat16)
    fetch.wait()
    both = group_sums([jnp.concatenate(v, axis=1) for v in (total, square)], alike[...])
    sums[...] = jnp.broadcast_to(both[None], sums.shape)


def cached_kernel(layer, chunk, far, distant, cache, before, after, weights, bias, *refs):
    bring = None
    if layer < 2:
        video, out, ordered, *refs = refs
        handed = [refs.pop(0) for _ in range(2 * layer)]
        near, *refs = refs
        refs = [out, ordered, *refs]
        bring = pltpu.make_async_copy(video, near, refs[-1].at[4])
    passed = []
    if layer == 1:
        later = pl.ds((layer + 2) * PLANES, handed[0].shape[0])
        for side, ref in enumerate((before, after)):
            passed.append(pltpu.make_async_copy(ref.at[later], handed[side], refs[-1].at[5 + side]))
    if distant:
        caches, out, ordered, cache, brims, *refs = cache, *refs
        refs = [out, ordered, *refs]
        here = pl.ds((layer - 2) * PLANES, PLANES)
        for side, ref in enumerate((before, after)):
            passed.append(pltpu.make_async_copy(ref.at[here], brims.at[side], refs[-1].at[5 + side]))
    out, ordered, edges, *slabs, weight, taps, sem = refs
    if far:
        away, out, *slabs = out, slabs[0], *slabs[1:]
    rows, cols, channels = cache.shape[-3:]
    places = rows * cols
    fetch = pltpu.make_async_copy(weights.at[layer], weight, sem.at[1])
    if distant:
        begun = pltpu.make_async_copy(caches.at[layer], cache, sem.at[0])
        begun.start()
    fetch.start()
    if bring is not None:
        bring.start()
    for copy in passed:
        copy.start()
    origin = (layer + 1) * PLANES
    if distant:
        begun.wait()
        for copy in passed:
            copy.wait()
        before, after, origin, passed = brims.at[0], brims.at[1], 0, []
    for side, ref in enumerate((before, after)):
        for plane in range(PLANES):
            edges[side, plane] = ref[origin + plane].astype(jnp.float32)

    def row_of(h):
        return planes(*(cache[frame, h].astype(jnp.float32) for frame in range(2)))

    def edge_of(h, plane):
        return [edges[side, plane, pl.ds(h, COLS, stride=0), :] for side in (0, 1)]

    build_slabs(rows, row_of, edge_of, slabs)
    fetch.wait()
    if layer == 1:
        bring.wait()
    for p in (1, 2, 0):
        taps[p] = tap_lanes(weight, p * 9 * channels, channels)
    store = pltpu.make_async_copy(taps.at[pl.ds(1, 2)], ordered, sem.at[2])
    store.start()
    constant = bias[layer : layer + 1, :]
    tables = [taps[p] for p in range(2)]

    def finish(t, value):
        value = value + constant
        if layer == 1:
            value = value + near[t].astype(jnp.float32).reshape(places, channels)
        put_planes(out, t, pl.ds(0, places), value)

    finish(1, product([(slabs[1], tables[0])], 0, places))
    finish(0, product([(slabs[0], tables[0]), (slabs[1], tables[1])], 0, places))
    if far:
        leave = pltpu.make_async_copy(out, away, sem.at[3])
        leave.start()
        leave.wait()
    for copy in [store] + passed:
        copy.wait()
    if layer == 0:
        bring.wait()


def active_kernel(layer, chunk, far, bring, entries, final, *refs):
    x, before, after, stats, gain, shift, ordered, part, same = refs[:9]
    rest = refs[9:]
    if layer > 0:
        _, *rest = rest
    if final:
        y, carried, *rest = rest
    else:
        if bring:
            caches, *rest = rest
        y, carried, sums, first, last, *rest = rest
        if bring:
            near, *rest = rest
    edges, *slabs, kept, taps, alike, sem = rest
    away = None
    if far:
        away, part, *slabs = part, *slabs
    frames, rows, cols, channels = kept.shape
    places = rows * cols
    fetch, late = [pltpu.make_async_copy(ordered, taps, sem.at[1])], []
    if far:
        fetch.append(pltpu.make_async_copy(away, part, sem.at[3]))
    if not final:
        late.append(pltpu.make_async_copy(same, alike, sem.at[4]))
    if bring:
        late.append(pltpu.make_async_copy(caches.at[layer + 1], near, sem.at[5]))
    for copy in fetch + late:
        copy.start()

    means = jnp.sum(stats[...], axis=0) / entries
    average = means[0:1]
    variance = means[1:2] - average * average
    scale = lax.rsqrt(variance + EPSILON) * gain[layer : layer + 1, :]
    offset = shift[layer : layer + 1, :] - average * scale
    scale, offset = 0.5 * scale, 0.5 * offset
    scales = [scale[:, :LANES]] * 2 + [twice(scale[:, LANES:])]
    offsets = [offset[:, :LANES]] * 2 + [twice(offset[:, LANES:])]

    def act(values):
        return [silu_of_twice(v * a + b) for v, a, b in zip(values, scales, offsets)]

    for side, ref in enumerate((before, after)):
        values = [ref[plane].astype(jnp.float32) for plane in range(PLANES)]
        for plane, value in enumerate(act(values)):
            edges[side, plane] = value

    def row_of(h):
        if layer:
            start = h * COLS if isinstance(h, int) else pl.multiple_of(h * COLS, COLS)
            return act([x[plane, pl.ds(start, COLS), :] for plane in range(PLANES)])
        return act(planes(*(x[frame, h].astype(jnp.float32) for frame in range(2))))

    def edge_of(h, plane):
        return [edges[side, plane, pl.ds(h, COLS, stride=0), :] for side in (0, 1)]

    def keep(h, *values):
        for frame in range(2):
            main, other = values[2 * frame : 2 * frame + 2]
            whole = jnp.concatenate([main, other[:, : channels - LANES]], axis=1)
            kept[frame, h] = whole.astype(jnp.bfloat16)

    build_slabs(rows, row_of, edge_of, slabs, keep)
    copy = pltpu.make_async_copy(kept, carried.at[layer], sem.at[0])
    copy.start()
    for one in fetch:
        one.wait()
    tables = [taps[p] for p in range(2)]
    moments = [jnp.zeros((COLS, channels), jnp.float32)] * 2

    def finish(t, start, size, value, moments):
        here, span = pl.ds(start, size), pl.ds(start // COLS, size // COLS)
        shape = (size // COLS, COLS, channels)
        value = value + get_planes(part, t, here)
        if final:
            value = value + get_planes(x, t, here)
            y[t, span] = value.reshape(shape).astype(jnp.bfloat16)
            return moments
        put_planes(y, t, here, value)
        folded = value.reshape(shape)
        return [
            moments[0] + jnp.sum(folded, axis=0),
            moments[1] + jnp.sum(folded * folded, axis=0),
        ]

    value = product([(slabs[0], tables[1])], 0, places)
    moments = finish(0, 0, places, value, moments)
    for start in range(0, places, chunk):
        value = product([(slabs[0], tables[0]), (slabs[1], tables[1])], start, chunk)
        moments = finish(1, start, chunk, value, moments)
    if not final:
        for one in late:
            one.wait()
        both = group_sums(moments, alike[...])
        sums[...] = jnp.broadcast_to(both[None], sums.shape)
        for plane in range(PLANES):
            for out, column in ((first, 0), (last, cols - 1)):
                edge = y[plane, pl.ds(column, rows, stride=cols), :]
                out[plane] = edge.astype(jnp.bfloat16)
    copy.wait()


def scratch(frames, rows, room):
    slab = pltpu.VMEM((SLABS, rows * COLS + 16, LANES), jnp.bfloat16)
    return [pltpu.VMEM((2, PLANES, rows, LANES), jnp.float32)] + room + [slab] * frames


def local(video_span, caches, norm_gains, shifts, weights, biases):
    peers = lax.axis_size("lon")
    frames, rows, cols, channels = video_span.shape
    layers = caches.shape[0]
    places = rows * cols
    entries = frames * places * peers * (channels // GROUPS)
    up = [(i, (i + 1) % peers) for i in range(peers)]
    down = [(j, i) for i, j in up]
    chunk = 720
    tiles = 14 * LANES

    def around(first, last):
        return lax.ppermute(last, "lon", up), lax.ppermute(first, "lon", down)

    def gathered(sums):
        return lax.all_to_all(sums, "lon", 0, 0)

    def in_hbm(value):
        return pltpu.with_memory_space_constraint(value, pltpu.HBM)

    turned = in_hbm(jnp.swapaxes(weights, 1, 2))
    caches, video = in_hbm(caches), in_hbm(video_span)
    members = channels // GROUPS
    alike = np.kron(np.eye(GROUPS), np.ones((members, members)))
    same = in_hbm(jnp.asarray(alike, jnp.bfloat16))
    spread = jax.ShapeDtypeStruct((peers, 2, channels), jnp.float32)
    brim = jax.ShapeDtypeStruct(((layers + 1) * PLANES, rows, LANES), jnp.bfloat16)
    block = jax.ShapeDtypeStruct(video_span.shape, video_span.dtype)
    sums, first, last, cache = pl.pallas_call(
        begin_kernel,
        out_shape=[spread, brim, brim, block],
        in_specs=[HBM] * 3,
        out_specs=[VMEM] * 4,
        scratch_shapes=[
            pltpu.VMEM((PLANES, places, LANES), jnp.float32),
            pltpu.VMEM((layers + 1,) + video_span.shape, jnp.bfloat16),
            pltpu.VMEM(same.shape, same.dtype),
            pltpu.SemaphoreType.DMA((layers + 2,)),
        ],
        compiler_params=pltpu.CompilerParams(vmem_limit_bytes=24 << 20),
        name="begin",
    )(video, caches, same)
    brims = around(first, last)
    before, after = brims
    stats = gathered(sums)

    def room(far):
        return [pltpu.VMEM((PLANES, places, LANES), jnp.float32)] if far else []

    def cached_part(layer, far, cache, brims):
        distant = cache is None
        own = [pltpu.VMEM(video_span.shape, jnp.bfloat16)] if distant or layer == 1 else []
        if distant:
            brims = [in_hbm(brim) for brim in brims]
            own.append(pltpu.VMEM((2, PLANES, rows, LANES), jnp.bfloat16))
        later = pltpu.HBM(((layers - 2) * PLANES, rows, LANES), jnp.bfloat16)
        more = {0: [block], 1: [later] * 2}.get(layer, [])
        planar = pltpu.HBM if far else jax.ShapeDtypeStruct
        return pl.pallas_call(
            functools.partial(cached_kernel, layer, chunk, far, distant),
            out_shape=[
                planar((PLANES, places, LANES), jnp.float32),
                pltpu.HBM((2, channels, tiles), weights.dtype),
            ]
            + more,
            in_specs=[HBM if distant else VMEM] * 3 + [HBM, VMEM]
            + ([HBM] if layer < 2 else []),
            out_specs=[HBM if far else VMEM, HBM] + [HBM if layer else VMEM] * len(more),
            scratch_shapes=own + scratch(frames, rows, room(far))
            + [
                pltpu.VMEM((channels, weights.shape[1]), weights.dtype),
                pltpu.VMEM((3, channels, tiles), weights.dtype),
                pltpu.SemaphoreType.DMA((7,)),
            ],
            compiler_params=pltpu.CompilerParams(vmem_limit_bytes=24 << 20),
            name="cached",
        )(caches if distant else cache, *brims, turned, biases, *([video] if layer < 2 else []))

    x = None
    carried = None
    for layer in range(layers):
        final = layer == layers - 1
        far = layer < layers - 1
        bring = layer < layers - 2
        part, ordered, *more = cached_part(layer, far, cache, brims)
        if layer == 0:
            x = more[0]
        elif more:
            brims = more
        if far:
            part = in_hbm(part)
        operands = [x, before, after, stats, norm_gains, shifts, in_hbm(ordered), part, same]
        specs = [VMEM] * 6 + [HBM, HBM if far else VMEM, HBM]
        aliases = {}
        if layer > 0:
            aliases = {len(operands): 1}
            operands.append(carried)
            specs.append(HBM)
        state = jax.ShapeDtypeStruct((PLANES, places, LANES), jnp.float32)
        if final:
            state = jax.ShapeDtypeStruct(video_span.shape, jnp.bfloat16)
        outs = [state, jax.ShapeDtypeStruct(caches.shape, jnp.bfloat16)]
        out_specs = [VMEM, HBM]
        if not final:
            edge = jax.ShapeDtypeStruct((PLANES, rows, LANES), jnp.bfloat16)
            outs += [spread, edge, edge]
            out_specs += [VMEM] * 3
        if bring:
            outs.append(block)
            out_specs.append(VMEM)
            operands.append(caches)
            specs.append(HBM)
        results = pl.pallas_call(
            functools.partial(active_kernel, layer, chunk, far, bring, entries, final),
            out_shape=outs,
            in_specs=specs,
            out_specs=out_specs,
            scratch_shapes=scratch(frames, rows, room(far))
            + [
                pltpu.VMEM(video_span.shape, jnp.bfloat16),
                pltpu.VMEM((2, channels, tiles), weights.dtype),
                pltpu.VMEM(same.shape, same.dtype),
                pltpu.SemaphoreType.DMA((6,)),
            ],
            compiler_params=pltpu.CompilerParams(vmem_limit_bytes=24 << 20),
            input_output_aliases=aliases,
            name="active",
        )(*operands)
        x, carried = results[:2]
        if not final:
            stats = gathered(results[2])
            before, after = around(results[3], results[4])
            cache = results[5] if bring else None
    return x, carried


def solution(mesh):
    return jax.shard_map(
        local,
        mesh=mesh,
        in_specs=(
            P(None, "clips", "lon", None),
            P(None, None, "clips", "lon", None),
            P(),
            P(),
            P(),
            P(),
        ),
        out_specs=(P(None, "clips", "lon", None), P(None, None, "clips", "lon", None)),
        check_vma=False,
    )
```

```python
import functools

import jax
import jax.numpy as jnp
import numpy as np
from jax import lax
from jax.experimental import pallas as pl
from jax.experimental.pallas import tpu as pltpu
from jax.sharding import PartitionSpec as P

GROUPS = 32
EPSILON = 1e-06
LANES = 128
HALF = LANES // 2
COLS = 8
SLABS = 10
UNROLL = 11
PLANES = 3
VMEM = pl.BlockSpec(memory_space=pltpu.VMEM)
HBM = pl.BlockSpec(memory_space=pltpu.HBM)


def silu_of_twice(u):
    return u + u * jnp.tanh(u)


def twice(v):
    return jnp.concatenate([v, v], axis=-1)


def halves(value):
    return value[..., :LANES], value[..., LANES:]


def planes(first, second):
    (a, b), (c, d) = halves(first), halves(second)
    return a, c, jnp.concatenate([b, d], axis=-1)


def pair(a, b):
    return jnp.concatenate([a, b], axis=0).astype(jnp.bfloat16)


def build_slabs(rows, row_of, edge_of, slabs, keep=None):
    lane = lax.broadcasted_iota(jnp.int32, (COLS, LANES), 1)
    low = lane < HALF
    column = lax.broadcasted_iota(jnp.int32, (COLS, LANES), 0)
    first, last = column == 0, column == COLS - 1
    zero = jnp.zeros((COLS, LANES), jnp.float32)

    def shifted(h):
        out = []
        for plane, value in enumerate(row_of(h)):
            left, right = edge_of(h, plane)
            out.append(
                (
                    jnp.where(first, left, pltpu.roll(value, 1, 0)),
                    value,
                    jnp.where(last, right, pltpu.roll(value, COLS - 1, 0)),
                )
            )
        rest = out[2]
        swapped = [pltpu.roll(v, HALF, 1) for v in rest]
        if keep is not None:
            keep(h, out[0][1], rest[1], out[1][1], swapped[1])
        mains = out[0] + out[1]
        packed = (jnp.where(low, rest[0], swapped[1]), jnp.where(low, swapped[0], rest[1]))
        return mains, packed, (rest[2], swapped[2])

    def put(frame, index, k, value):
        start = k * 16 if isinstance(k, int) else pl.multiple_of(k * 16, 16)
        slabs[frame][index, pl.ds(start, 16), :] = value

    def around(frame, upper, lower):
        return jnp.where(low, upper[frame], lower[1 - frame])

    def step(k, carry):
        before, older, oldest = carry
        one, two = shifted(2 * k), shifted(2 * k + 1)
        for frame in range(2):
            for r in range(3):
                put(frame, r, k, pair(one[0][3 * frame + r], two[0][3 * frame + r]))
                put(frame, 3 + r, k, pair(before[0][3 * frame + r], one[0][3 * frame + r]))
            put(frame, 6, k, pair(one[1][frame], two[1][frame]))
            put(frame, 7, k, pair(before[1][frame], one[1][frame]))
            put(frame, 9, k, pair(one[2][frame], two[2][frame]))
            if older is not None:
                upper = around(frame, oldest, before[2])
                put(frame, 8, k - 1, pair(upper, around(frame, older, one[2])))
        return two, one[2], before[2]

    count = rows // 2
    carry = step(0, (((zero,) * 6, (zero,) * 2, (zero,) * 2), None, None))
    before, older, oldest = lax.fori_loop(1, count, step, carry, unroll=UNROLL)
    for frame in range(2):
        for r in range(3):
            put(frame, 3 + r, count, pair(before[0][3 * frame + r], zero))
        put(frame, 7, count, pair(before[1][frame], zero))
        upper = around(frame, oldest, before[2])
        put(frame, 8, count - 1, pair(upper, around(frame, older, (zero, zero))))


def slab_rows(slab, start, size):
    def at(index, step=0):
        return slab[index, pl.ds(start + step, size), :]

    tiles = [at(3 + r) for r in range(3)] + [at(r) for r in range(3)]
    tiles += [at(3 + r, 16) for r in range(3)]
    return tiles + [at(7), at(6), at(7, 16), at(8), at(9)]


def tap_lanes(weight, origin, channels):
    def at(q, r, start, size):
        return weight[:, pl.ds(origin + (q * 3 + r) * channels + start, size)]

    tiles = [at(q, r, 0, LANES) for q in range(3) for r in range(3)]
    for q in range(3):
        tiles += [at(q, 0, LANES, HALF), at(q, 1, LANES, HALF)]
    tiles += [at(0, 2, LANES, HALF), at(2, 2, LANES, HALF), at(1, 2, LANES, HALF)]
    tiles.append(jnp.zeros((weight.shape[0], HALF), weight.dtype))
    return jnp.concatenate(tiles, axis=1)


def product(pairs, start, size):
    left = [tile for slab, _ in pairs for tile in slab_rows(slab, start, size)]
    right = [taps for _, taps in pairs]
    return lax.dot_general(
        jnp.concatenate(left, axis=1),
        jnp.concatenate(right, axis=1),
        (((1,), (1,)), ((), ())),
        preferred_element_type=jnp.float32,
    )


def put_planes(out, t, here, value):
    main, rest = halves(value)
    out[t, here, :] = main
    out[2, here, HALF * t : HALF * (t + 1)] = rest


def get_planes(held, t, here):
    rest = held[2, here, HALF * t : HALF * (t + 1)]
    return jnp.concatenate([held[t, here, :], rest], axis=1)


def group_sums(pieces, same):
    total = jnp.concatenate([jnp.sum(v, axis=0, keepdims=True) for v in pieces], axis=0)
    high = total.astype(jnp.bfloat16)
    left = total - high.astype(jnp.float32)
    middle = left.astype(jnp.bfloat16)
    low = (left - middle.astype(jnp.float32)).astype(jnp.bfloat16)
    split = jnp.concatenate([high, middle, low], axis=0)
    sums = jnp.dot(split, same, preferred_element_type=jnp.float32)
    return sums[0:2] + sums[2:4] + sums[4:6]


def begin_kernel(video, caches, same, sums, first, last, near, wide, held, alike, sem):
    layers, frames, rows, cols, channels = caches.shape
    copies = [pltpu.make_async_copy(video, held.at[0], sem.at[0])]
    for layer in range(layers):
        target = held.at[layer + 1] if layer else near
        copies.append(pltpu.make_async_copy(caches.at[layer], target, sem.at[layer + 1]))
    fetch = pltpu.make_async_copy(same, alike, sem.at[layers + 1])
    for copy in copies + [fetch]:
        copy.start()
    half, places = channels - LANES, rows * cols
    total = [jnp.zeros((COLS, LANES), jnp.float32), jnp.zeros((COLS, half), jnp.float32)]
    square = list(total)
    for group, copy in enumerate(copies):
        copy.wait()
        for frame in range(frames):
            value = (near[frame] if group == 1 else held[group, frame]).astype(jnp.float32)
            parts = halves(value)
            if group == 0:
                for i in range(2):
                    total[i] = total[i] + jnp.sum(parts[i], axis=0)
                    square[i] = square[i] + jnp.sum(parts[i] * parts[i], axis=0)
            wide[frame] = parts[0].reshape(places, LANES)
            wide[2, :, HALF * frame : HALF * (frame + 1)] = parts[1].reshape(places, half)
        for out, column in ((first, 0), (last, cols - 1)):
            for plane in range(PLANES):
                edge = wide[plane, pl.ds(column, rows, stride=cols), :]
                out[group * PLANES + plane] = edge.astype(jnp.bfloat16)
    fetch.wait()
    both = group_sums([jnp.concatenate(v, axis=1) for v in (total, square)], alike[...])
    sums[...] = jnp.broadcast_to(both[None], sums.shape)


def cached_kernel(layer, chunk, far, cache, before, after, weights, bias, *refs):
    bring = None
    if layer < 2:
        video, out, ordered, *refs = refs
        handed = [refs.pop(0) for _ in range(2 * layer)]
        near, *refs = refs
        if layer == 1:
            caches, cache, *refs = cache, *refs
        refs = [out, ordered, *refs]
        bring = pltpu.make_async_copy(video, near, refs[-1].at[4])
    passed = []
    if layer == 1:
        later = pl.ds((layer + 2) * PLANES, handed[0].shape[0])
        for side, ref in enumerate((before, after)):
            passed.append(pltpu.make_async_copy(ref.at[later], handed[side], refs[-1].at[5 + side]))
    out, ordered, edges, *slabs, weight, taps, sem = refs
    if far:
        away, out, *slabs = out, slabs[0], *slabs[1:]
    rows, cols, channels = cache.shape[-3:]
    places = rows * cols
    fetch = pltpu.make_async_copy(weights.at[layer], weight, sem.at[1])
    if layer == 1:
        begun = pltpu.make_async_copy(caches.at[layer], cache, sem.at[0])
        begun.start()
    fetch.start()
    if bring is not None:
        bring.start()
    for copy in passed:
        copy.start()
    origin = (layer + 1) * PLANES if layer < 2 else (layer - 2) * PLANES
    for side, ref in enumerate((before, after)):
        for plane in range(PLANES):
            edges[side, plane] = ref[origin + plane].astype(jnp.float32)

    def row_of(h):
        return planes(*(cache[frame, h].astype(jnp.float32) for frame in range(2)))

    def edge_of(h, plane):
        return [edges[side, plane, pl.ds(h, COLS, stride=0), :] for side in (0, 1)]

    if layer == 1:
        begun.wait()
    build_slabs(rows, row_of, edge_of, slabs)
    fetch.wait()
    if layer == 1:
        bring.wait()
    for p in (1, 2, 0):
        taps[p] = tap_lanes(weight, p * 9 * channels, channels)
    store = pltpu.make_async_copy(taps.at[pl.ds(1, 2)], ordered, sem.at[2])
    store.start()
    constant = bias[layer : layer + 1, :]
    tables = [taps[p] for p in range(2)]

    def finish(t, value):
        value = value + constant
        if layer == 1:
            value = value + near[t].astype(jnp.float32).reshape(places, channels)
        put_planes(out, t, pl.ds(0, places), value)

    finish(1, product([(slabs[1], tables[0])], 0, places))
    finish(0, product([(slabs[0], tables[0]), (slabs[1], tables[1])], 0, places))
    if far:
        leave = pltpu.make_async_copy(out, away, sem.at[3])
        leave.start()
        leave.wait()
    for copy in [store] + passed:
        copy.wait()
    if layer == 0:
        bring.wait()


def active_kernel(layer, chunk, far, bring, entries, final, *refs):
    x, before, after, stats, gain, shift, ordered, part, same = refs[:9]
    rest = refs[9:]
    if layer > 0:
        _, *rest = rest
    if final:
        y, carried, *rest = rest
    else:
        if bring:
            caches, *rest = rest
        y, carried, sums, first, last, *rest = rest
        if bring:
            near, *rest = rest
    edges, *slabs, kept, taps, alike, sem = rest
    away = None
    if far:
        away, part, *slabs = part, *slabs
    frames, rows, cols, channels = kept.shape
    places = rows * cols
    fetch, late = [pltpu.make_async_copy(ordered, taps, sem.at[1])], []
    if far:
        fetch.append(pltpu.make_async_copy(away, part, sem.at[3]))
    if not final:
        late.append(pltpu.make_async_copy(same, alike, sem.at[4]))
    if bring:
        late.append(pltpu.make_async_copy(caches.at[layer + 1], near, sem.at[5]))
    for copy in fetch + late:
        copy.start()

    means = jnp.sum(stats[...], axis=0) / entries
    average = means[0:1]
    variance = means[1:2] - average * average
    scale = lax.rsqrt(variance + EPSILON) * gain[layer : layer + 1, :]
    offset = shift[layer : layer + 1, :] - average * scale
    scale, offset = 0.5 * scale, 0.5 * offset
    scales = [scale[:, :LANES]] * 2 + [twice(scale[:, LANES:])]
    offsets = [offset[:, :LANES]] * 2 + [twice(offset[:, LANES:])]

    def act(values):
        return [silu_of_twice(v * a + b) for v, a, b in zip(values, scales, offsets)]

    for side, ref in enumerate((before, after)):
        values = [ref[plane].astype(jnp.float32) for plane in range(PLANES)]
        for plane, value in enumerate(act(values)):
            edges[side, plane] = value

    def row_of(h):
        if layer:
            start = h * COLS if isinstance(h, int) else pl.multiple_of(h * COLS, COLS)
            return act([x[plane, pl.ds(start, COLS), :] for plane in range(PLANES)])
        return act(planes(*(x[frame, h].astype(jnp.float32) for frame in range(2))))

    def edge_of(h, plane):
        return [edges[side, plane, pl.ds(h, COLS, stride=0), :] for side in (0, 1)]

    def keep(h, *values):
        for frame in range(2):
            main, other = values[2 * frame : 2 * frame + 2]
            whole = jnp.concatenate([main, other[:, : channels - LANES]], axis=1)
            kept[frame, h] = whole.astype(jnp.bfloat16)

    build_slabs(rows, row_of, edge_of, slabs, keep)
    copy = pltpu.make_async_copy(kept, carried.at[layer], sem.at[0])
    copy.start()
    for one in fetch:
        one.wait()
    tables = [taps[p] for p in range(2)]
    moments = [jnp.zeros((COLS, channels), jnp.float32)] * 2

    def finish(t, start, size, value, moments):
        here, span = pl.ds(start, size), pl.ds(start // COLS, size // COLS)
        shape = (size // COLS, COLS, channels)
        value = value + get_planes(part, t, here)
        if final:
            value = value + get_planes(x, t, here)
            y[t, span] = value.reshape(shape).astype(jnp.bfloat16)
            return moments
        put_planes(y, t, here, value)
        folded = value.reshape(shape)
        return [
            moments[0] + jnp.sum(folded, axis=0),
            moments[1] + jnp.sum(folded * folded, axis=0),
        ]

    value = product([(slabs[0], tables[1])], 0, places)
    moments = finish(0, 0, places, value, moments)
    for start in range(0, places, chunk):
        value = product([(slabs[0], tables[0]), (slabs[1], tables[1])], start, chunk)
        moments = finish(1, start, chunk, value, moments)
    if not final:
        for one in late:
            one.wait()
        both = group_sums(moments, alike[...])
        sums[...] = jnp.broadcast_to(both[None], sums.shape)
        for plane in range(PLANES):
            for out, column in ((first, 0), (last, cols - 1)):
                edge = y[plane, pl.ds(column, rows, stride=cols), :]
                out[plane] = edge.astype(jnp.bfloat16)
    copy.wait()


def scratch(frames, rows, room):
    slab = pltpu.VMEM((SLABS, rows * COLS + 16, LANES), jnp.bfloat16)
    return [pltpu.VMEM((2, PLANES, rows, LANES), jnp.float32)] + room + [slab] * frames


def local(video_span, caches, norm_gains, shifts, weights, biases):
    peers = lax.axis_size("lon")
    frames, rows, cols, channels = video_span.shape
    layers = caches.shape[0]
    places = rows * cols
    entries = frames * places * peers * (channels // GROUPS)
    up = [(i, (i + 1) % peers) for i in range(peers)]
    down = [(j, i) for i, j in up]
    chunk = 720
    tiles = 14 * LANES

    def around(first, last):
        return lax.ppermute(last, "lon", up), lax.ppermute(first, "lon", down)

    def gathered(sums):
        return lax.all_to_all(sums, "lon", 0, 0)

    def in_hbm(value):
        return pltpu.with_memory_space_constraint(value, pltpu.HBM)

    turned = in_hbm(jnp.swapaxes(weights, 1, 2))
    caches, video = in_hbm(caches), in_hbm(video_span)
    members = channels // GROUPS
    alike = np.kron(np.eye(GROUPS), np.ones((members, members)))
    same = in_hbm(jnp.asarray(alike, jnp.bfloat16))
    spread = jax.ShapeDtypeStruct((peers, 2, channels), jnp.float32)
    brim = jax.ShapeDtypeStruct(((layers + 1) * PLANES, rows, LANES), jnp.bfloat16)
    block = jax.ShapeDtypeStruct(video_span.shape, video_span.dtype)
    sums, first, last, cache = pl.pallas_call(
        begin_kernel,
        out_shape=[spread, brim, brim, block],
        in_specs=[HBM] * 3,
        out_specs=[VMEM] * 4,
        scratch_shapes=[
            pltpu.VMEM((PLANES, places, LANES), jnp.float32),
            pltpu.VMEM((layers + 1,) + video_span.shape, jnp.bfloat16),
            pltpu.VMEM(same.shape, same.dtype),
            pltpu.SemaphoreType.DMA((layers + 2,)),
        ],
        compiler_params=pltpu.CompilerParams(vmem_limit_bytes=24 << 20),
        name="begin",
    )(video, caches, same)
    brims = around(first, last)
    before, after = brims
    stats = gathered(sums)

    def room(far):
        return [pltpu.VMEM((PLANES, places, LANES), jnp.float32)] if far else []

    def cached_part(layer, far, cache, brims):
        own = [pltpu.VMEM(video_span.shape, jnp.bfloat16)] * 2 if layer == 1 else []
        later = pltpu.HBM(((layers - 2) * PLANES, rows, LANES), jnp.bfloat16)
        more = {0: [block], 1: [later] * 2}.get(layer, [])
        planar = pltpu.HBM if far else jax.ShapeDtypeStruct
        return pl.pallas_call(
            functools.partial(cached_kernel, layer, chunk, far),
            out_shape=[
                planar((PLANES, places, LANES), jnp.float32),
                pltpu.HBM((2, channels, tiles), weights.dtype),
            ]
            + more,
            in_specs=[HBM if cache is None else VMEM, VMEM, VMEM, HBM, VMEM]
            + ([HBM] if layer < 2 else []),
            out_specs=[HBM if far else VMEM, HBM] + [HBM if layer else VMEM] * len(more),
            scratch_shapes=own + scratch(frames, rows, room(far))
            + [
                pltpu.VMEM((channels, weights.shape[1]), weights.dtype),
                pltpu.VMEM((3, channels, tiles), weights.dtype),
                pltpu.SemaphoreType.DMA((7,)),
            ],
            compiler_params=pltpu.CompilerParams(vmem_limit_bytes=24 << 20),
            name="cached",
        )(caches if cache is None else cache, *brims, turned, biases, *([video] if layer < 2 else []))

    x = None
    carried = None
    for layer in range(layers):
        final = layer == layers - 1
        far = layer < layers - 1
        bring = 0 < layer < layers - 1
        part, ordered, *more = cached_part(layer, far, cache, brims)
        if layer == 0:
            x = more[0]
        elif more:
            brims = more
        if far:
            part = in_hbm(part)
        operands = [x, before, after, stats, norm_gains, shifts, in_hbm(ordered), part, same]
        specs = [VMEM] * 6 + [HBM, HBM if far else VMEM, HBM]
        aliases = {}
        if layer > 0:
            aliases = {len(operands): 1}
            operands.append(carried)
            specs.append(HBM)
        state = jax.ShapeDtypeStruct((PLANES, places, LANES), jnp.float32)
        if final:
            state = jax.ShapeDtypeStruct(video_span.shape, jnp.bfloat16)
        outs = [state, jax.ShapeDtypeStruct(caches.shape, jnp.bfloat16)]
        out_specs = [VMEM, HBM]
        if not final:
            edge = jax.ShapeDtypeStruct((PLANES, rows, LANES), jnp.bfloat16)
            outs += [spread, edge, edge]
            out_specs += [VMEM] * 3
        if bring:
            outs.append(block)
            out_specs.append(VMEM)
            operands.append(caches)
            specs.append(HBM)
        results = pl.pallas_call(
            functools.partial(active_kernel, layer, chunk, far, bring, entries, final),
            out_shape=outs,
            in_specs=specs,
            out_specs=out_specs,
            scratch_shapes=scratch(frames, rows, room(far))
            + [
                pltpu.VMEM(video_span.shape, jnp.bfloat16),
                pltpu.VMEM((2, channels, tiles), weights.dtype),
                pltpu.VMEM(same.shape, same.dtype),
                pltpu.SemaphoreType.DMA((6,)),
            ],
            compiler_params=pltpu.CompilerParams(vmem_limit_bytes=24 << 20),
            input_output_aliases=aliases,
            name="active",
        )(*operands)
        x, carried = results[:2]
        if not final:
            stats = gathered(results[2])
            before, after = around(results[3], results[4])
            cache = results[5] if bring else None
    return x, carried


def solution(mesh):
    return jax.shard_map(
        local,
        mesh=mesh,
        in_specs=(
            P(None, "clips", "lon", None),
            P(None, None, "clips", "lon", None),
            P(),
            P(),
            P(),
            P(),
        ),
        out_specs=(P(None, "clips", "lon", None), P(None, None, "clips", "lon", None)),
        check_vma=False,
    )
```

```python
import functools

import jax
import jax.numpy as jnp
import numpy as np
from jax import lax
from jax.experimental import pallas as pl
from jax.experimental.pallas import tpu as pltpu
from jax.sharding import PartitionSpec as P

GROUPS = 32
EPSILON = 1e-06
LANES = 128
HALF = LANES // 2
COLS = 8
SLABS = 10
UNROLL = 11
PLANES = 3
VMEM = pl.BlockSpec(memory_space=pltpu.VMEM)
HBM = pl.BlockSpec(memory_space=pltpu.HBM)


def silu_of_twice(u):
    return u + u * jnp.tanh(u)


def twice(v):
    return jnp.concatenate([v, v], axis=-1)


def halves(value):
    return value[..., :LANES], value[..., LANES:]


def planes(first, second):
    (a, b), (c, d) = halves(first), halves(second)
    return a, c, jnp.concatenate([b, d], axis=-1)


def pair(a, b):
    return jnp.concatenate([a, b], axis=0).astype(jnp.bfloat16)


def build_slabs(rows, row_of, edge_of, slabs, keep=None):
    lane = lax.broadcasted_iota(jnp.int32, (COLS, LANES), 1)
    low = lane < HALF
    column = lax.broadcasted_iota(jnp.int32, (COLS, LANES), 0)
    first, last = column == 0, column == COLS - 1
    zero = jnp.zeros((COLS, LANES), jnp.float32)

    def shifted(h):
        out = []
        for plane, value in enumerate(row_of(h)):
            left, right = edge_of(h, plane)
            out.append(
                (
                    jnp.where(first, left, pltpu.roll(value, 1, 0)),
                    value,
                    jnp.where(last, right, pltpu.roll(value, COLS - 1, 0)),
                )
            )
        rest = out[2]
        swapped = [pltpu.roll(v, HALF, 1) for v in rest]
        if keep is not None:
            keep(h, out[0][1], rest[1], out[1][1], swapped[1])
        mains = out[0] + out[1]
        packed = (jnp.where(low, rest[0], swapped[1]), jnp.where(low, swapped[0], rest[1]))
        return mains, packed, (rest[2], swapped[2])

    def put(frame, index, k, value):
        start = k * 16 if isinstance(k, int) else pl.multiple_of(k * 16, 16)
        slabs[frame][index, pl.ds(start, 16), :] = value

    def around(frame, upper, lower):
        return jnp.where(low, upper[frame], lower[1 - frame])

    def step(k, carry):
        before, older, oldest = carry
        one, two = shifted(2 * k), shifted(2 * k + 1)
        for frame in range(2):
            for r in range(3):
                put(frame, r, k, pair(one[0][3 * frame + r], two[0][3 * frame + r]))
                put(frame, 3 + r, k, pair(before[0][3 * frame + r], one[0][3 * frame + r]))
            put(frame, 6, k, pair(one[1][frame], two[1][frame]))
            put(frame, 7, k, pair(before[1][frame], one[1][frame]))
            put(frame, 9, k, pair(one[2][frame], two[2][frame]))
            if older is not None:
                upper = around(frame, oldest, before[2])
                put(frame, 8, k - 1, pair(upper, around(frame, older, one[2])))
        return two, one[2], before[2]

    count = rows // 2
    carry = step(0, (((zero,) * 6, (zero,) * 2, (zero,) * 2), None, None))
    before, older, oldest = lax.fori_loop(1, count, step, carry, unroll=UNROLL)
    for frame in range(2):
        for r in range(3):
            put(frame, 3 + r, count, pair(before[0][3 * frame + r], zero))
        put(frame, 7, count, pair(before[1][frame], zero))
        upper = around(frame, oldest, before[2])
        put(frame, 8, count - 1, pair(upper, around(frame, older, (zero, zero))))


def slab_rows(slab, start, size):
    def at(index, step=0):
        return slab[index, pl.ds(start + step, size), :]

    tiles = [at(3 + r) for r in range(3)] + [at(r) for r in range(3)]
    tiles += [at(3 + r, 16) for r in range(3)]
    return tiles + [at(7), at(6), at(7, 16), at(8), at(9)]


def tap_lanes(weight, origin, channels):
    def at(q, r, start, size):
        return weight[:, pl.ds(origin + (q * 3 + r) * channels + start, size)]

    tiles = [at(q, r, 0, LANES) for q in range(3) for r in range(3)]
    for q in range(3):
        tiles += [at(q, 0, LANES, HALF), at(q, 1, LANES, HALF)]
    tiles += [at(0, 2, LANES, HALF), at(2, 2, LANES, HALF), at(1, 2, LANES, HALF)]
    tiles.append(jnp.zeros((weight.shape[0], HALF), weight.dtype))
    return jnp.concatenate(tiles, axis=1)


def product(pairs, start, size):
    left = [tile for slab, _ in pairs for tile in slab_rows(slab, start, size)]
    right = [taps for _, taps in pairs]
    return lax.dot_general(
        jnp.concatenate(left, axis=1),
        jnp.concatenate(right, axis=1),
        (((1,), (1,)), ((), ())),
        preferred_element_type=jnp.float32,
    )


def put_planes(out, t, here, value):
    main, rest = halves(value)
    out[t, here, :] = main
    out[2, here, HALF * t : HALF * (t + 1)] = rest


def get_planes(held, t, here):
    rest = held[2, here, HALF * t : HALF * (t + 1)]
    return jnp.concatenate([held[t, here, :], rest], axis=1)


def group_sums(pieces, same):
    total = jnp.concatenate([jnp.sum(v, axis=0, keepdims=True) for v in pieces], axis=0)
    high = total.astype(jnp.bfloat16)
    left = total - high.astype(jnp.float32)
    middle = left.astype(jnp.bfloat16)
    low = (left - middle.astype(jnp.float32)).astype(jnp.bfloat16)
    split = jnp.concatenate([high, middle, low], axis=0)
    sums = jnp.dot(split, same, preferred_element_type=jnp.float32)
    return sums[0:2] + sums[2:4] + sums[4:6]


def begin_kernel(video, caches, same, sums, first, last, near, state, wide, held, alike, sem):
    layers, frames, rows, cols, channels = caches.shape
    copies = [pltpu.make_async_copy(video, held.at[0], sem.at[0])]
    for layer in range(layers):
        target = held.at[layer + 1] if layer else near
        copies.append(pltpu.make_async_copy(caches.at[layer], target, sem.at[layer + 1]))
    fetch = pltpu.make_async_copy(same, alike, sem.at[layers + 1])
    for copy in copies + [fetch]:
        copy.start()
    half, places = channels - LANES, rows * cols
    total = [jnp.zeros((COLS, LANES), jnp.float32), jnp.zeros((COLS, half), jnp.float32)]
    square = list(total)
    for group, copy in enumerate(copies):
        copy.wait()
        target = wide if group else state
        for frame in range(frames):
            value = (near[frame] if group == 1 else held[group, frame]).astype(jnp.float32)
            parts = halves(value)
            if group == 0:
                for i in range(2):
                    total[i] = total[i] + jnp.sum(parts[i], axis=0)
                    square[i] = square[i] + jnp.sum(parts[i] * parts[i], axis=0)
            target[frame] = parts[0].reshape(places, LANES)
            target[2, :, HALF * frame : HALF * (frame + 1)] = parts[1].reshape(places, half)
        for out, column in ((first, 0), (last, cols - 1)):
            for plane in range(PLANES):
                edge = target[plane, pl.ds(column, rows, stride=cols), :]
                out[group * PLANES + plane] = edge.astype(jnp.bfloat16)
    fetch.wait()
    both = group_sums([jnp.concatenate(v, axis=1) for v in (total, square)], alike[...])
    sums[...] = jnp.broadcast_to(both[None], sums.shape)


def cached_kernel(layer, chunk, far, cache, before, after, weights, bias, *refs):
    bring = None
    if layer == 1:
        video, out, ordered, *handed = refs[:5]
        near, *refs = refs[5:]
        caches, cache, *refs = cache, *refs
        refs = [out, ordered, *refs]
        bring = pltpu.make_async_copy(video, near, refs[-1].at[4])
    passed, middle = [], None
    if layer > 1:
        middle, *refs = refs
    if layer == 1:
        later = pl.ds((layer + 2) * PLANES, handed[0].shape[0])
        for side, ref in enumerate((before, after)):
            passed.append(pltpu.make_async_copy(ref.at[later], handed[side], refs[-1].at[5 + side]))
    out, ordered, edges, *slabs, weight, taps, sem = refs
    if far:
        away, out, *slabs = out, slabs[0], *slabs[1:]
    rows, cols, channels = cache.shape[-3:]
    places = rows * cols
    fetch = pltpu.make_async_copy(weights.at[layer], weight, sem.at[1])
    if layer == 1:
        begun = pltpu.make_async_copy(caches.at[layer], cache, sem.at[0])
        begun.start()
    fetch.start()
    if bring is not None:
        bring.start()
    for copy in passed:
        copy.start()
    origin = (layer + 1) * PLANES if layer < 2 else (layer - 2) * PLANES
    for side, ref in enumerate((before, after)):
        for plane in range(PLANES):
            edges[side, plane] = ref[origin + plane].astype(jnp.float32)

    def row_of(h):
        return planes(*(cache[frame, h].astype(jnp.float32) for frame in range(2)))

    def edge_of(h, plane):
        return [edges[side, plane, pl.ds(h, COLS, stride=0), :] for side in (0, 1)]

    if layer == 1:
        begun.wait()
    build_slabs(rows, row_of, edge_of, slabs)
    fetch.wait()
    if layer == 1:
        bring.wait()
    for p in (1, 2, 0):
        taps[p] = tap_lanes(weight, p * 9 * channels, channels)
    store = pltpu.make_async_copy(taps.at[pl.ds(1, 2)], ordered, sem.at[2])
    store.start()
    constant = bias[layer : layer + 1, :]
    tables = [taps[p] for p in range(2)]

    def finish(t, value):
        value = value + constant
        if layer == 1:
            value = value + near[t].astype(jnp.float32).reshape(places, channels)
        elif middle is not None:
            value = value + get_planes(middle, t, pl.ds(0, places))
        put_planes(out, t, pl.ds(0, places), value)

    finish(1, product([(slabs[1], tables[0])], 0, places))
    finish(0, product([(slabs[0], tables[0]), (slabs[1], tables[1])], 0, places))
    if far:
        leave = pltpu.make_async_copy(out, away, sem.at[3])
        leave.start()
        leave.wait()
    for copy in [store] + passed:
        copy.wait()


def active_kernel(layer, chunk, far, bring, entries, final, *refs):
    x, before, after, stats, gain, shift, ordered, part, same = refs[:9]
    rest = refs[9:]
    if layer > 0:
        _, *rest = rest
    if final:
        y, carried, *rest = rest
    else:
        if bring:
            caches, *rest = rest
        y, carried, sums, first, last, *rest = rest
        if bring:
            near, *rest = rest
    edges, *slabs, kept, taps, alike, sem = rest
    away = None
    if far:
        away, part, *slabs = part, *slabs
    frames, rows, cols, channels = kept.shape
    places = rows * cols
    fetch, late = [pltpu.make_async_copy(ordered, taps, sem.at[1])], []
    if far:
        fetch.append(pltpu.make_async_copy(away, part, sem.at[3]))
    if not final:
        late.append(pltpu.make_async_copy(same, alike, sem.at[4]))
    if bring:
        late.append(pltpu.make_async_copy(caches.at[layer + 1], near, sem.at[5]))
    for copy in fetch + late:
        copy.start()

    means = jnp.sum(stats[...], axis=0) / entries
    average = means[0:1]
    variance = means[1:2] - average * average
    scale = lax.rsqrt(variance + EPSILON) * gain[layer : layer + 1, :]
    offset = shift[layer : layer + 1, :] - average * scale
    scale, offset = 0.5 * scale, 0.5 * offset
    scales = [scale[:, :LANES]] * 2 + [twice(scale[:, LANES:])]
    offsets = [offset[:, :LANES]] * 2 + [twice(offset[:, LANES:])]

    def act(values):
        return [silu_of_twice(v * a + b) for v, a, b in zip(values, scales, offsets)]

    for side, ref in enumerate((before, after)):
        values = [ref[plane].astype(jnp.float32) for plane in range(PLANES)]
        for plane, value in enumerate(act(values)):
            edges[side, plane] = value

    def row_of(h):
        start = h * COLS if isinstance(h, int) else pl.multiple_of(h * COLS, COLS)
        return act([x[plane, pl.ds(start, COLS), :] for plane in range(PLANES)])

    def edge_of(h, plane):
        return [edges[side, plane, pl.ds(h, COLS, stride=0), :] for side in (0, 1)]

    def keep(h, *values):
        for frame in range(2):
            main, other = values[2 * frame : 2 * frame + 2]
            whole = jnp.concatenate([main, other[:, : channels - LANES]], axis=1)
            kept[frame, h] = whole.astype(jnp.bfloat16)

    build_slabs(rows, row_of, edge_of, slabs, keep)
    copy = pltpu.make_async_copy(kept, carried.at[layer], sem.at[0])
    copy.start()
    for one in fetch:
        one.wait()
    tables = [taps[p] for p in range(2)]
    moments = [jnp.zeros((COLS, channels), jnp.float32)] * 2

    def finish(t, start, size, value, moments):
        here, span = pl.ds(start, size), pl.ds(start // COLS, size // COLS)
        shape = (size // COLS, COLS, channels)
        value = value + get_planes(part, t, here)
        if final:
            y[t, span] = value.reshape(shape).astype(jnp.bfloat16)
            return moments
        put_planes(y, t, here, value)
        folded = value.reshape(shape)
        return [
            moments[0] + jnp.sum(folded, axis=0),
            moments[1] + jnp.sum(folded * folded, axis=0),
        ]

    value = product([(slabs[0], tables[1])], 0, places)
    moments = finish(0, 0, places, value, moments)
    for start in range(0, places, chunk):
        value = product([(slabs[0], tables[0]), (slabs[1], tables[1])], start, chunk)
        moments = finish(1, start, chunk, value, moments)
    if not final:
        for one in late:
            one.wait()
        both = group_sums(moments, alike[...])
        sums[...] = jnp.broadcast_to(both[None], sums.shape)
        for plane in range(PLANES):
            for out, column in ((first, 0), (last, cols - 1)):
                edge = y[plane, pl.ds(column, rows, stride=cols), :]
                out[plane] = edge.astype(jnp.bfloat16)
    copy.wait()


def scratch(frames, rows, room):
    slab = pltpu.VMEM((SLABS, rows * COLS + 16, LANES), jnp.bfloat16)
    return [pltpu.VMEM((2, PLANES, rows, LANES), jnp.float32)] + room + [slab] * frames


def local(video_span, caches, norm_gains, shifts, weights, biases):
    peers = lax.axis_size("lon")
    frames, rows, cols, channels = video_span.shape
    layers = caches.shape[0]
    places = rows * cols
    entries = frames * places * peers * (channels // GROUPS)
    up = [(i, (i + 1) % peers) for i in range(peers)]
    down = [(j, i) for i, j in up]
    chunk = 720
    tiles = 14 * LANES

    def around(first, last):
        return lax.ppermute(last, "lon", up), lax.ppermute(first, "lon", down)

    def gathered(sums):
        return lax.all_to_all(sums, "lon", 0, 0)

    def in_hbm(value):
        return pltpu.with_memory_space_constraint(value, pltpu.HBM)

    turned = in_hbm(jnp.swapaxes(weights, 1, 2))
    caches, video = in_hbm(caches), in_hbm(video_span)
    members = channels // GROUPS
    alike = np.kron(np.eye(GROUPS), np.ones((members, members)))
    same = in_hbm(jnp.asarray(alike, jnp.bfloat16))
    spread = jax.ShapeDtypeStruct((peers, 2, channels), jnp.float32)
    brim = jax.ShapeDtypeStruct(((layers + 1) * PLANES, rows, LANES), jnp.bfloat16)
    block = jax.ShapeDtypeStruct(video_span.shape, video_span.dtype)
    planar = jax.ShapeDtypeStruct((PLANES, places, LANES), jnp.float32)
    sums, first, last, cache, x = pl.pallas_call(
        begin_kernel,
        out_shape=[spread, brim, brim, block, planar],
        in_specs=[HBM] * 3,
        out_specs=[VMEM] * 5,
        scratch_shapes=[
            pltpu.VMEM((PLANES, places, LANES), jnp.float32),
            pltpu.VMEM((layers + 1,) + video_span.shape, jnp.bfloat16),
            pltpu.VMEM(same.shape, same.dtype),
            pltpu.SemaphoreType.DMA((layers + 2,)),
        ],
        compiler_params=pltpu.CompilerParams(vmem_limit_bytes=24 << 20),
        name="begin",
    )(video, caches, same)
    brims = around(first, last)
    before, after = brims
    stats = gathered(sums)

    def room(far):
        return [pltpu.VMEM((PLANES, places, LANES), jnp.float32)] if far else []

    def cached_part(layer, far, cache, brims, x):
        own = [pltpu.VMEM(video_span.shape, jnp.bfloat16)] * 2 if layer == 1 else []
        later = pltpu.HBM(((layers - 2) * PLANES, rows, LANES), jnp.bfloat16)
        more = [later] * 2 if layer == 1 else []
        extra = {0: [], 1: [video]}.get(layer, [x])
        planar = pltpu.HBM if far else jax.ShapeDtypeStruct
        return pl.pallas_call(
            functools.partial(cached_kernel, layer, chunk, far),
            out_shape=[
                planar((PLANES, places, LANES), jnp.float32),
                pltpu.HBM((2, channels, tiles), weights.dtype),
            ]
            + more,
            in_specs=[HBM if cache is None else VMEM, VMEM, VMEM, HBM, VMEM]
            + [HBM if layer < 2 else VMEM] * len(extra),
            out_specs=[HBM if far else VMEM, HBM] + [HBM] * len(more),
            scratch_shapes=own + scratch(frames, rows, room(far))
            + [
                pltpu.VMEM((channels, weights.shape[1]), weights.dtype),
                pltpu.VMEM((3, channels, tiles), weights.dtype),
                pltpu.SemaphoreType.DMA((7,)),
            ],
            compiler_params=pltpu.CompilerParams(vmem_limit_bytes=24 << 20),
            name="cached",
        )(caches if cache is None else cache, *brims, turned, biases, *extra)

    carried = None
    for layer in range(layers):
        final = layer == layers - 1
        far = layer < layers - 1
        bring = 0 < layer < layers - 1
        part, ordered, *more = cached_part(layer, far, cache, brims, x)
        if more:
            brims = more
        if far:
            part = in_hbm(part)
        operands = [x, before, after, stats, norm_gains, shifts, in_hbm(ordered), part, same]
        specs = [VMEM] * 6 + [HBM, HBM if far else VMEM, HBM]
        aliases = {}
        if layer > 0:
            aliases = {len(operands): 1}
            operands.append(carried)
            specs.append(HBM)
        state = jax.ShapeDtypeStruct((PLANES, places, LANES), jnp.float32)
        if final:
            state = jax.ShapeDtypeStruct(video_span.shape, jnp.bfloat16)
        outs = [state, jax.ShapeDtypeStruct(caches.shape, jnp.bfloat16)]
        out_specs = [VMEM, HBM]
        if not final:
            edge = jax.ShapeDtypeStruct((PLANES, rows, LANES), jnp.bfloat16)
            outs += [spread, edge, edge]
            out_specs += [VMEM] * 3
        if bring:
            outs.append(block)
            out_specs.append(VMEM)
            operands.append(caches)
            specs.append(HBM)
        results = pl.pallas_call(
            functools.partial(active_kernel, layer, chunk, far, bring, entries, final),
            out_shape=outs,
            in_specs=specs,
            out_specs=out_specs,
            scratch_shapes=scratch(frames, rows, room(far))
            + [
                pltpu.VMEM(video_span.shape, jnp.bfloat16),
                pltpu.VMEM((2, channels, tiles), weights.dtype),
                pltpu.VMEM(same.shape, same.dtype),
                pltpu.SemaphoreType.DMA((6,)),
            ],
            compiler_params=pltpu.CompilerParams(vmem_limit_bytes=24 << 20),
            input_output_aliases=aliases,
            name="active",
        )(*operands)
        x, carried = results[:2]
        if not final:
            stats = gathered(results[2])
            before, after = around(results[3], results[4])
            cache = results[5] if bring else None
    return x, carried


def solution(mesh):
    return jax.shard_map(
        local,
        mesh=mesh,
        in_specs=(
            P(None, "clips", "lon", None),
            P(None, None, "clips", "lon", None),
            P(),
            P(),
            P(),
            P(),
        ),
        out_specs=(P(None, "clips", "lon", None), P(None, None, "clips", "lon", None)),
        check_vma=False,
    )
```

```python
import functools

import jax
import jax.numpy as jnp
import numpy as np
from jax import lax
from jax.experimental import pallas as pl
from jax.experimental.pallas import tpu as pltpu
from jax.sharding import PartitionSpec as P

GROUPS = 32
EPSILON = 1e-06
LANES = 128
HALF = LANES // 2
COLS = 8
SLABS = 10
UNROLL = 11
PLANES = 3
VMEM = pl.BlockSpec(memory_space=pltpu.VMEM)
HBM = pl.BlockSpec(memory_space=pltpu.HBM)


def silu_of_twice(u):
    return u + u * jnp.tanh(u)


def twice(v):
    return jnp.concatenate([v, v], axis=-1)


def halves(value):
    return value[..., :LANES], value[..., LANES:]


def planes(first, second):
    (a, b), (c, d) = halves(first), halves(second)
    return a, c, jnp.concatenate([b, d], axis=-1)


def pair(a, b):
    return jnp.concatenate([a, b], axis=0).astype(jnp.bfloat16)


def build_slabs(rows, row_of, edge_of, slabs, keep=None):
    lane = lax.broadcasted_iota(jnp.int32, (COLS, LANES), 1)
    low = lane < HALF
    column = lax.broadcasted_iota(jnp.int32, (COLS, LANES), 0)
    first, last = column == 0, column == COLS - 1
    zero = jnp.zeros((COLS, LANES), jnp.float32)

    def shifted(h):
        out = []
        for plane, value in enumerate(row_of(h)):
            left, right = edge_of(h, plane)
            out.append(
                (
                    jnp.where(first, left, pltpu.roll(value, 1, 0)),
                    value,
                    jnp.where(last, right, pltpu.roll(value, COLS - 1, 0)),
                )
            )
        rest = out[2]
        swapped = [pltpu.roll(v, HALF, 1) for v in rest]
        if keep is not None:
            keep(h, out[0][1], rest[1], out[1][1], swapped[1])
        mains = out[0] + out[1]
        packed = (jnp.where(low, rest[0], swapped[1]), jnp.where(low, swapped[0], rest[1]))
        return mains, packed, (rest[2], swapped[2])

    def put(frame, index, k, value):
        start = k * 16 if isinstance(k, int) else pl.multiple_of(k * 16, 16)
        slabs[frame][index, pl.ds(start, 16), :] = value

    def around(frame, upper, lower):
        return jnp.where(low, upper[frame], lower[1 - frame])

    def step(k, carry):
        before, older, oldest = carry
        one, two = shifted(2 * k), shifted(2 * k + 1)
        for frame in range(2):
            for r in range(3):
                put(frame, r, k, pair(one[0][3 * frame + r], two[0][3 * frame + r]))
                put(frame, 3 + r, k, pair(before[0][3 * frame + r], one[0][3 * frame + r]))
            put(frame, 6, k, pair(one[1][frame], two[1][frame]))
            put(frame, 7, k, pair(before[1][frame], one[1][frame]))
            put(frame, 9, k, pair(one[2][frame], two[2][frame]))
            if older is not None:
                upper = around(frame, oldest, before[2])
                put(frame, 8, k - 1, pair(upper, around(frame, older, one[2])))
        return two, one[2], before[2]

    count = rows // 2
    carry = step(0, (((zero,) * 6, (zero,) * 2, (zero,) * 2), None, None))
    before, older, oldest = lax.fori_loop(1, count, step, carry, unroll=UNROLL)
    for frame in range(2):
        for r in range(3):
            put(frame, 3 + r, count, pair(before[0][3 * frame + r], zero))
        put(frame, 7, count, pair(before[1][frame], zero))
        upper = around(frame, oldest, before[2])
        put(frame, 8, count - 1, pair(upper, around(frame, older, (zero, zero))))


def slab_rows(slab, start, size):
    def at(index, step=0):
        return slab[index, pl.ds(start + step, size), :]

    tiles = [at(3 + r) for r in range(3)] + [at(r) for r in range(3)]
    tiles += [at(3 + r, 16) for r in range(3)]
    return tiles + [at(7), at(6), at(7, 16), at(8), at(9)]


def tap_lanes(weight, origin, channels):
    def at(q, r, start, size):
        return weight[:, pl.ds(origin + (q * 3 + r) * channels + start, size)]

    tiles = [at(q, r, 0, LANES) for q in range(3) for r in range(3)]
    for q in range(3):
        tiles += [at(q, 0, LANES, HALF), at(q, 1, LANES, HALF)]
    tiles += [at(0, 2, LANES, HALF), at(2, 2, LANES, HALF), at(1, 2, LANES, HALF)]
    tiles.append(jnp.zeros((weight.shape[0], HALF), weight.dtype))
    return jnp.concatenate(tiles, axis=1)


def product(pairs, start, size):
    left = [tile for slab, _ in pairs for tile in slab_rows(slab, start, size)]
    right = [taps for _, taps in pairs]
    return lax.dot_general(
        jnp.concatenate(left, axis=1),
        jnp.concatenate(right, axis=1),
        (((1,), (1,)), ((), ())),
        preferred_element_type=jnp.float32,
    )


def put_planes(out, t, here, value):
    main, rest = halves(value)
    out[t, here, :] = main
    out[2, here, HALF * t : HALF * (t + 1)] = rest


def get_planes(held, t, here):
    rest = held[2, here, HALF * t : HALF * (t + 1)]
    return jnp.concatenate([held[t, here, :], rest], axis=1)


def group_sums(pieces, same):
    total = jnp.concatenate([jnp.sum(v, axis=0, keepdims=True) for v in pieces], axis=0)
    high = total.astype(jnp.bfloat16)
    left = total - high.astype(jnp.float32)
    middle = left.astype(jnp.bfloat16)
    low = (left - middle.astype(jnp.float32)).astype(jnp.bfloat16)
    split = jnp.concatenate([high, middle, low], axis=0)
    sums = jnp.dot(split, same, preferred_element_type=jnp.float32)
    return sums[0:2] + sums[2:4] + sums[4:6]


def pieces(source, target, sem, first, cuts):
    size = source.shape[1] // cuts
    copies = []
    for lead in range(source.shape[0]):
        for cut in range(cuts):
            at = (lead, pl.ds(cut * size, size))
            own = sem.at[first + len(copies)]
            copies.append(pltpu.make_async_copy(source.at[at], target.at[at], own))
    return copies


def begin_kernel(video, caches, same, sums, first, last, near, wide, held, alike, sem):
    layers, frames, rows, cols, channels = caches.shape
    copies = [pltpu.make_async_copy(video, held.at[0], sem.at[0])]
    for layer in range(layers):
        target = held.at[layer + 1] if layer else near
        copies.append(pltpu.make_async_copy(caches.at[layer], target, sem.at[layer + 1]))
    fetch = pltpu.make_async_copy(same, alike, sem.at[layers + 1])
    for copy in copies + [fetch]:
        copy.start()
    half, places = channels - LANES, rows * cols
    total = [jnp.zeros((COLS, LANES), jnp.float32), jnp.zeros((COLS, half), jnp.float32)]
    square = list(total)
    for group, copy in enumerate(copies):
        copy.wait()
        for frame in range(frames):
            value = (near[frame] if group == 1 else held[group, frame]).astype(jnp.float32)
            parts = halves(value)
            if group == 0:
                for i in range(2):
                    total[i] = total[i] + jnp.sum(parts[i], axis=0)
                    square[i] = square[i] + jnp.sum(parts[i] * parts[i], axis=0)
            wide[frame] = parts[0].reshape(places, LANES)
            wide[2, :, HALF * frame : HALF * (frame + 1)] = parts[1].reshape(places, half)
        for out, column in ((first, 0), (last, cols - 1)):
            for plane in range(PLANES):
                edge = wide[plane, pl.ds(column, rows, stride=cols), :]
                out[group * PLANES + plane] = edge.astype(jnp.bfloat16)
    fetch.wait()
    both = group_sums([jnp.concatenate(v, axis=1) for v in (total, square)], alike[...])
    sums[...] = jnp.broadcast_to(both[None], sums.shape)


def cached_kernel(layer, chunk, far, cache, before, after, weights, bias, *refs):
    bring = None
    if layer < 2:
        video, out, ordered, *refs = refs
        handed = [refs.pop(0) for _ in range(2 * layer)]
        near, *refs = refs
        if layer == 1:
            caches, cache, *refs = cache, *refs
        refs = [out, ordered, *refs]
        bring = pltpu.make_async_copy(video, near, refs[-1].at[4])
    passed, middle = [], None
    if layer > 1:
        middle, *refs = refs
    if layer == 1:
        later = pl.ds((layer + 2) * PLANES, handed[0].shape[0])
        for side, ref in enumerate((before, after)):
            passed.append(pltpu.make_async_copy(ref.at[later], handed[side], refs[-1].at[5 + side]))
    out, ordered, edges, *slabs, weight, taps, sem = refs
    if far:
        away, out, *slabs = out, slabs[0], *slabs[1:]
    rows, cols, channels = cache.shape[-3:]
    places = rows * cols
    fetch = pltpu.make_async_copy(weights.at[layer], weight, sem.at[1])
    if layer == 1:
        begun = pieces(caches.at[layer], cache, sem, 12, 3)
        for copy in begun:
            copy.start()
    fetch.start()
    if bring is not None:
        bring.start()
    for copy in passed:
        copy.start()
    origin = (layer + 1) * PLANES if layer < 2 else (layer - 2) * PLANES
    for side, ref in enumerate((before, after)):
        for plane in range(PLANES):
            edges[side, plane] = ref[origin + plane].astype(jnp.float32)

    def row_of(h):
        return planes(*(cache[frame, h].astype(jnp.float32) for frame in range(2)))

    def edge_of(h, plane):
        return [edges[side, plane, pl.ds(h, COLS, stride=0), :] for side in (0, 1)]

    if layer == 1:
        for copy in begun:
            copy.wait()
    build_slabs(rows, row_of, edge_of, slabs)
    fetch.wait()
    if layer == 1:
        bring.wait()
    for p in (1, 2, 0):
        taps[p] = tap_lanes(weight, p * 9 * channels, channels)
    store = pltpu.make_async_copy(taps.at[pl.ds(1, 2)], ordered, sem.at[2])
    store.start()
    constant = bias[layer : layer + 1, :]
    tables = [taps[p] for p in range(2)]

    def finish(t, value):
        value = value + constant
        if layer == 1:
            value = value + near[t].astype(jnp.float32).reshape(places, channels)
        elif middle is not None:
            value = value + get_planes(middle, t, pl.ds(0, places))
        put_planes(out, t, pl.ds(0, places), value)

    finish(1, product([(slabs[1], tables[0])], 0, places))
    finish(0, product([(slabs[0], tables[0]), (slabs[1], tables[1])], 0, places))
    if far:
        leave = pieces(out, away, sem, 8, 1)
        for copy in leave:
            copy.start()
        for copy in leave:
            copy.wait()
    for copy in [store] + passed:
        copy.wait()
    if layer == 0:
        bring.wait()


def active_kernel(layer, chunk, far, bring, entries, final, *refs):
    x, before, after, stats, gain, shift, ordered, part, same = refs[:9]
    rest = refs[9:]
    if layer > 0:
        _, *rest = rest
    if final:
        y, carried, *rest = rest
    else:
        if bring:
            caches, *rest = rest
        y, carried, sums, first, last, *rest = rest
        if bring:
            near, *rest = rest
    edges, *slabs, kept, taps, alike, sem = rest
    away = None
    if far:
        away, part, *slabs = part, *slabs
    frames, rows, cols, channels = kept.shape
    places = rows * cols
    fetch, late = pieces(ordered, taps, sem, 8, 4), []
    if far:
        fetch += pieces(away, part, sem, 16, 1)
    if not final:
        late.append(pltpu.make_async_copy(same, alike, sem.at[4]))
    if bring:
        late.append(pltpu.make_async_copy(caches.at[layer + 1], near, sem.at[5]))
    for copy in fetch + late:
        copy.start()

    means = jnp.sum(stats[...], axis=0) / entries
    average = means[0:1]
    variance = means[1:2] - average * average
    scale = lax.rsqrt(variance + EPSILON) * gain[layer : layer + 1, :]
    offset = shift[layer : layer + 1, :] - average * scale
    scale, offset = 0.5 * scale, 0.5 * offset
    scales = [scale[:, :LANES]] * 2 + [twice(scale[:, LANES:])]
    offsets = [offset[:, :LANES]] * 2 + [twice(offset[:, LANES:])]

    def act(values):
        return [silu_of_twice(v * a + b) for v, a, b in zip(values, scales, offsets)]

    for side, ref in enumerate((before, after)):
        values = [ref[plane].astype(jnp.float32) for plane in range(PLANES)]
        for plane, value in enumerate(act(values)):
            edges[side, plane] = value

    def row_of(h):
        if layer:
            start = h * COLS if isinstance(h, int) else pl.multiple_of(h * COLS, COLS)
            return act([x[plane, pl.ds(start, COLS), :] for plane in range(PLANES)])
        return act(planes(*(x[frame, h].astype(jnp.float32) for frame in range(2))))

    def edge_of(h, plane):
        return [edges[side, plane, pl.ds(h, COLS, stride=0), :] for side in (0, 1)]

    def keep(h, *values):
        for frame in range(2):
            main, other = values[2 * frame : 2 * frame + 2]
            whole = jnp.concatenate([main, other[:, : channels - LANES]], axis=1)
            kept[frame, h] = whole.astype(jnp.bfloat16)

    build_slabs(rows, row_of, edge_of, slabs, keep)
    copy = pltpu.make_async_copy(kept, carried.at[layer], sem.at[0])
    copy.start()
    for one in fetch:
        one.wait()
    tables = [taps[p] for p in range(2)]
    moments = [jnp.zeros((COLS, channels), jnp.float32)] * 2

    def finish(t, start, size, value, moments):
        here, span = pl.ds(start, size), pl.ds(start // COLS, size // COLS)
        shape = (size // COLS, COLS, channels)
        value = value + get_planes(part, t, here)
        if final:
            y[t, span] = value.reshape(shape).astype(jnp.bfloat16)
            return moments
        put_planes(y, t, here, value)
        folded = value.reshape(shape)
        return [
            moments[0] + jnp.sum(folded, axis=0),
            moments[1] + jnp.sum(folded * folded, axis=0),
        ]

    value = product([(slabs[0], tables[1])], 0, places)
    moments = finish(0, 0, places, value, moments)
    for start in range(0, places, chunk):
        value = product([(slabs[0], tables[0]), (slabs[1], tables[1])], start, chunk)
        moments = finish(1, start, chunk, value, moments)
    if not final:
        for one in late:
            one.wait()
        both = group_sums(moments, alike[...])
        sums[...] = jnp.broadcast_to(both[None], sums.shape)
        for plane in range(PLANES):
            for out, column in ((first, 0), (last, cols - 1)):
                edge = y[plane, pl.ds(column, rows, stride=cols), :]
                out[plane] = edge.astype(jnp.bfloat16)
    copy.wait()


def scratch(frames, rows, room):
    slab = pltpu.VMEM((SLABS, rows * COLS + 16, LANES), jnp.bfloat16)
    return [pltpu.VMEM((2, PLANES, rows, LANES), jnp.float32)] + room + [slab] * frames


def local(video_span, caches, norm_gains, shifts, weights, biases):
    peers = lax.axis_size("lon")
    frames, rows, cols, channels = video_span.shape
    layers = caches.shape[0]
    places = rows * cols
    entries = frames * places * peers * (channels // GROUPS)
    up = [(i, (i + 1) % peers) for i in range(peers)]
    down = [(j, i) for i, j in up]
    chunk = 720
    tiles = 14 * LANES

    def around(first, last):
        return lax.ppermute(last, "lon", up), lax.ppermute(first, "lon", down)

    def gathered(sums):
        return lax.all_to_all(sums, "lon", 0, 0)

    def in_hbm(value):
        return pltpu.with_memory_space_constraint(value, pltpu.HBM)

    turned = in_hbm(jnp.swapaxes(weights, 1, 2))
    caches, video = in_hbm(caches), in_hbm(video_span)
    members = channels // GROUPS
    alike = np.kron(np.eye(GROUPS), np.ones((members, members)))
    same = in_hbm(jnp.asarray(alike, jnp.bfloat16))
    spread = jax.ShapeDtypeStruct((peers, 2, channels), jnp.float32)
    brim = jax.ShapeDtypeStruct(((layers + 1) * PLANES, rows, LANES), jnp.bfloat16)
    block = jax.ShapeDtypeStruct(video_span.shape, video_span.dtype)
    sums, first, last, cache = pl.pallas_call(
        begin_kernel,
        out_shape=[spread, brim, brim, block],
        in_specs=[HBM] * 3,
        out_specs=[VMEM] * 4,
        scratch_shapes=[
            pltpu.VMEM((PLANES, places, LANES), jnp.float32),
            pltpu.VMEM((layers + 1,) + video_span.shape, jnp.bfloat16),
            pltpu.VMEM(same.shape, same.dtype),
            pltpu.SemaphoreType.DMA((layers + 2,)),
        ],
        compiler_params=pltpu.CompilerParams(vmem_limit_bytes=24 << 20),
        name="begin",
    )(video, caches, same)
    brims = around(first, last)
    before, after = brims
    stats = gathered(sums)

    def room(far):
        return [pltpu.VMEM((PLANES, places, LANES), jnp.float32)] if far else []

    def cached_part(layer, far, cache, brims, x):
        own = [pltpu.VMEM(video_span.shape, jnp.bfloat16)] * 2 if layer == 1 else []
        later = pltpu.HBM(((layers - 2) * PLANES, rows, LANES), jnp.bfloat16)
        more = {0: [block], 1: [later] * 2}.get(layer, [])
        planar = pltpu.HBM if far else jax.ShapeDtypeStruct
        return pl.pallas_call(
            functools.partial(cached_kernel, layer, chunk, far),
            out_shape=[
                planar((PLANES, places, LANES), jnp.float32),
                pltpu.HBM((2, channels, tiles), weights.dtype),
            ]
            + more,
            in_specs=[HBM if cache is None else VMEM, VMEM, VMEM, HBM, VMEM]
            + [HBM if layer < 2 else VMEM],
            out_specs=[HBM if far else VMEM, HBM] + [HBM if layer else VMEM] * len(more),
            scratch_shapes=own + scratch(frames, rows, room(far))
            + [
                pltpu.VMEM((channels, weights.shape[1]), weights.dtype),
                pltpu.VMEM((3, channels, tiles), weights.dtype),
                pltpu.SemaphoreType.DMA((20,)),
            ],
            compiler_params=pltpu.CompilerParams(vmem_limit_bytes=24 << 20),
            name="cached",
        )(caches if cache is None else cache, *brims, turned, biases, video if layer < 2 else x)

    x = None
    carried = None
    for layer in range(layers):
        final = layer == layers - 1
        far = layer < layers - 1
        bring = 0 < layer < layers - 1
        part, ordered, *more = cached_part(layer, far, cache, brims, x)
        if layer == 0:
            x = more[0]
        elif more:
            brims = more
        if far:
            part = in_hbm(part)
        operands = [x, before, after, stats, norm_gains, shifts, in_hbm(ordered), part, same]
        specs = [VMEM] * 6 + [HBM, HBM if far else VMEM, HBM]
        aliases = {}
        if layer > 0:
            aliases = {len(operands): 1}
            operands.append(carried)
            specs.append(HBM)
        state = jax.ShapeDtypeStruct((PLANES, places, LANES), jnp.float32)
        if final:
            state = jax.ShapeDtypeStruct(video_span.shape, jnp.bfloat16)
        outs = [state, jax.ShapeDtypeStruct(caches.shape, jnp.bfloat16)]
        out_specs = [VMEM, HBM]
        if not final:
            edge = jax.ShapeDtypeStruct((PLANES, rows, LANES), jnp.bfloat16)
            outs += [spread, edge, edge]
            out_specs += [VMEM] * 3
        if bring:
            outs.append(block)
            out_specs.append(VMEM)
            operands.append(caches)
            specs.append(HBM)
        results = pl.pallas_call(
            functools.partial(active_kernel, layer, chunk, far, bring, entries, final),
            out_shape=outs,
            in_specs=specs,
            out_specs=out_specs,
            scratch_shapes=scratch(frames, rows, room(far))
            + [
                pltpu.VMEM(video_span.shape, jnp.bfloat16),
                pltpu.VMEM((2, channels, tiles), weights.dtype),
                pltpu.VMEM(same.shape, same.dtype),
                pltpu.SemaphoreType.DMA((20,)),
            ],
            compiler_params=pltpu.CompilerParams(vmem_limit_bytes=24 << 20),
            input_output_aliases=aliases,
            name="active",
        )(*operands)
        x, carried = results[:2]
        if not final:
            stats = gathered(results[2])
            before, after = around(results[3], results[4])
            cache = results[5] if bring else None
    return x, carried


def solution(mesh):
    return jax.shard_map(
        local,
        mesh=mesh,
        in_specs=(
            P(None, "clips", "lon", None),
            P(None, None, "clips", "lon", None),
            P(),
            P(),
            P(),
            P(),
        ),
        out_specs=(P(None, "clips", "lon", None), P(None, None, "clips", "lon", None)),
        check_vma=False,
    )
```

```python
import functools

import jax
import jax.numpy as jnp
import numpy as np
from jax import lax
from jax.experimental import pallas as pl
from jax.experimental.pallas import tpu as pltpu
from jax.sharding import PartitionSpec as P

GROUPS = 32
EPSILON = 1e-06
LANES = 128
HALF = LANES // 2
COLS = 8
SLABS = 10
UNROLL = 11
PLANES = 3
VMEM = pl.BlockSpec(memory_space=pltpu.VMEM)
HBM = pl.BlockSpec(memory_space=pltpu.HBM)


def silu_of_twice(u):
    return u + u * jnp.tanh(u)


def twice(v):
    return jnp.concatenate([v, v], axis=-1)


def halves(value):
    return value[..., :LANES], value[..., LANES:]


def planes(first, second):
    (a, b), (c, d) = halves(first), halves(second)
    return a, c, jnp.concatenate([b, d], axis=-1)


def pair(a, b):
    return jnp.concatenate([a, b], axis=0).astype(jnp.bfloat16)


def build_slabs(rows, row_of, edge_of, slabs, keep=None):
    lane = lax.broadcasted_iota(jnp.int32, (COLS, LANES), 1)
    low = lane < HALF
    column = lax.broadcasted_iota(jnp.int32, (COLS, LANES), 0)
    first, last = column == 0, column == COLS - 1
    zero = jnp.zeros((COLS, LANES), jnp.float32)

    def shifted(h):
        out = []
        for plane, value in enumerate(row_of(h)):
            left, right = edge_of(h, plane)
            out.append(
                (
                    jnp.where(first, left, pltpu.roll(value, 1, 0)),
                    value,
                    jnp.where(last, right, pltpu.roll(value, COLS - 1, 0)),
                )
            )
        rest = out[2]
        swapped = [pltpu.roll(v, HALF, 1) for v in rest]
        if keep is not None:
            keep(h, out[0][1], rest[1], out[1][1], swapped[1])
        mains = out[0] + out[1]
        packed = (jnp.where(low, rest[0], swapped[1]), jnp.where(low, swapped[0], rest[1]))
        return mains, packed, (rest[2], swapped[2])

    def put(frame, index, k, value):
        start = k * 16 if isinstance(k, int) else pl.multiple_of(k * 16, 16)
        slabs[frame][index, pl.ds(start, 16), :] = value

    def around(frame, upper, lower):
        return jnp.where(low, upper[frame], lower[1 - frame])

    def step(k, carry):
        before, older, oldest = carry
        one, two = shifted(2 * k), shifted(2 * k + 1)
        for frame in range(2):
            for r in range(3):
                put(frame, r, k, pair(one[0][3 * frame + r], two[0][3 * frame + r]))
                put(frame, 3 + r, k, pair(before[0][3 * frame + r], one[0][3 * frame + r]))
            put(frame, 6, k, pair(one[1][frame], two[1][frame]))
            put(frame, 7, k, pair(before[1][frame], one[1][frame]))
            put(frame, 9, k, pair(one[2][frame], two[2][frame]))
            if older is not None:
                upper = around(frame, oldest, before[2])
                put(frame, 8, k - 1, pair(upper, around(frame, older, one[2])))
        return two, one[2], before[2]

    count = rows // 2
    carry = step(0, (((zero,) * 6, (zero,) * 2, (zero,) * 2), None, None))
    before, older, oldest = lax.fori_loop(1, count, step, carry, unroll=UNROLL)
    for frame in range(2):
        for r in range(3):
            put(frame, 3 + r, count, pair(before[0][3 * frame + r], zero))
        put(frame, 7, count, pair(before[1][frame], zero))
        upper = around(frame, oldest, before[2])
        put(frame, 8, count - 1, pair(upper, around(frame, older, (zero, zero))))


def slab_rows(slab, start, size):
    def at(index, step=0):
        return slab[index, pl.ds(start + step, size), :]

    tiles = [at(3 + r) for r in range(3)] + [at(r) for r in range(3)]
    tiles += [at(3 + r, 16) for r in range(3)]
    return tiles + [at(7), at(6), at(7, 16), at(8), at(9)]


def tap_lanes(weight, origin, channels):
    def at(q, r, start, size):
        return weight[:, pl.ds(origin + (q * 3 + r) * channels + start, size)]

    tiles = [at(q, r, 0, LANES) for q in range(3) for r in range(3)]
    for q in range(3):
        tiles += [at(q, 0, LANES, HALF), at(q, 1, LANES, HALF)]
    tiles += [at(0, 2, LANES, HALF), at(2, 2, LANES, HALF), at(1, 2, LANES, HALF)]
    tiles.append(jnp.zeros((weight.shape[0], HALF), weight.dtype))
    return jnp.concatenate(tiles, axis=1)


def product(pairs, start, size):
    left = [tile for slab, _ in pairs for tile in slab_rows(slab, start, size)]
    right = [taps for _, taps in pairs]
    return lax.dot_general(
        jnp.concatenate(left, axis=1),
        jnp.concatenate(right, axis=1),
        (((1,), (1,)), ((), ())),
        preferred_element_type=jnp.float32,
    )


def put_planes(out, t, here, value):
    main, rest = halves(value)
    out[t, here, :] = main
    out[2, here, HALF * t : HALF * (t + 1)] = rest


def get_planes(held, t, here):
    rest = held[2, here, HALF * t : HALF * (t + 1)]
    return jnp.concatenate([held[t, here, :], rest], axis=1)


def group_sums(pieces, same):
    total = jnp.concatenate([jnp.sum(v, axis=0, keepdims=True) for v in pieces], axis=0)
    high = total.astype(jnp.bfloat16)
    left = total - high.astype(jnp.float32)
    middle = left.astype(jnp.bfloat16)
    low = (left - middle.astype(jnp.float32)).astype(jnp.bfloat16)
    split = jnp.concatenate([high, middle, low], axis=0)
    sums = jnp.dot(split, same, preferred_element_type=jnp.float32)
    return sums[0:2] + sums[2:4] + sums[4:6]


def begin_kernel(video, caches, same, sums, first, last, near, wide, held, alike, sem):
    layers, frames, rows, cols, channels = caches.shape
    copies = [pltpu.make_async_copy(video, held.at[0], sem.at[0])]
    for layer in range(layers):
        target = held.at[layer + 1] if layer else near
        copies.append(pltpu.make_async_copy(caches.at[layer], target, sem.at[layer + 1]))
    fetch = pltpu.make_async_copy(same, alike, sem.at[layers + 1])
    for copy in copies + [fetch]:
        copy.start()
    half, places = channels - LANES, rows * cols
    total = [jnp.zeros((COLS, LANES), jnp.float32), jnp.zeros((COLS, half), jnp.float32)]
    square = list(total)
    for group, copy in enumerate(copies):
        copy.wait()
        for frame in range(frames):
            value = (near[frame] if group == 1 else held[group, frame]).astype(jnp.float32)
            parts = halves(value)
            if group == 0:
                for i in range(2):
                    total[i] = total[i] + jnp.sum(parts[i], axis=0)
                    square[i] = square[i] + jnp.sum(parts[i] * parts[i], axis=0)
            wide[frame] = parts[0].reshape(places, LANES)
            wide[2, :, HALF * frame : HALF * (frame + 1)] = parts[1].reshape(places, half)
        for out, column in ((first, 0), (last, cols - 1)):
            for plane in range(PLANES):
                edge = wide[plane, pl.ds(column, rows, stride=cols), :]
                out[group * PLANES + plane] = edge.astype(jnp.bfloat16)
    fetch.wait()
    both = group_sums([jnp.concatenate(v, axis=1) for v in (total, square)], alike[...])
    sums[...] = jnp.broadcast_to(both[None], sums.shape)


def cached_kernel(layer, chunk, far, cache, before, after, weights, bias, *refs):
    bring = None
    if layer < 2:
        video, out, ordered, *refs = refs
        handed = [refs.pop(0) for _ in range(2 * layer)]
        near, *refs = refs
        if layer == 1:
            caches, cache, *refs = cache, *refs
        refs = [out, ordered, *refs]
        bring = pltpu.make_async_copy(video, near, refs[-1].at[4])
    passed = []
    if layer == 1:
        later = pl.ds((layer + 2) * PLANES, handed[0].shape[0])
        for side, ref in enumerate((before, after)):
            passed.append(pltpu.make_async_copy(ref.at[later], handed[side], refs[-1].at[5 + side]))
    out, ordered, edges, *slabs, weight, taps, sem = refs
    if far:
        away, out, *slabs = out, slabs[0], *slabs[1:]
    rows, cols, channels = cache.shape[-3:]
    places = rows * cols
    fetch = pltpu.make_async_copy(weights.at[layer], weight, sem.at[1])
    if layer == 1:
        begun = pltpu.make_async_copy(caches.at[layer], cache, sem.at[0])
        begun.start()
    fetch.start()
    if bring is not None:
        bring.start()
    for copy in passed:
        copy.start()
    origin = (layer + 1) * PLANES if layer < 2 else (layer - 2) * PLANES
    for side, ref in enumerate((before, after)):
        for plane in range(PLANES):
            edges[side, plane] = ref[origin + plane].astype(jnp.float32)

    def row_of(h):
        return planes(*(cache[frame, h].astype(jnp.float32) for frame in range(2)))

    def edge_of(h, plane):
        return [edges[side, plane, pl.ds(h, COLS, stride=0), :] for side in (0, 1)]

    if layer == 1:
        begun.wait()
    build_slabs(rows, row_of, edge_of, slabs)
    fetch.wait()
    if layer == 1:
        bring.wait()
    for p in (1, 2, 0):
        taps[p] = tap_lanes(weight, p * 9 * channels, channels)
    store = pltpu.make_async_copy(taps.at[pl.ds(1, 2)], ordered, sem.at[2])
    store.start()
    constant = bias[layer : layer + 1, :]
    tables = [taps[p] for p in range(2)]

    def finish(t, value):
        value = value + constant
        if layer == 1:
            value = value + near[t].astype(jnp.float32).reshape(places, channels)
        put_planes(out, t, pl.ds(0, places), value)

    finish(1, product([(slabs[1], tables[0])], 0, places))
    finish(0, product([(slabs[0], tables[0]), (slabs[1], tables[1])], 0, places))
    if far:
        leave = pltpu.make_async_copy(out, away, sem.at[3])
        leave.start()
        leave.wait()
    for copy in [store] + passed:
        copy.wait()
    if layer == 0:
        bring.wait()


def active_kernel(layer, chunk, far, bring, entries, final, *refs):
    x, before, after, stats, gain, shift, ordered, part, same = refs[:9]
    rest = refs[9:]
    if layer > 0:
        _, *rest = rest
    if final:
        y, carried, *rest = rest
    else:
        if bring:
            caches, *rest = rest
        y, carried, sums, first, last, *rest = rest
        if bring:
            near, *rest = rest
    edges, *slabs, kept, taps, alike, sem = rest
    away = None
    if far:
        away, part, *slabs = part, *slabs
    frames, rows, cols, channels = kept.shape
    places = rows * cols
    fetch, late = [pltpu.make_async_copy(ordered, taps, sem.at[1])], []
    if far:
        fetch.append(pltpu.make_async_copy(away, part, sem.at[3]))
    if not final:
        late.append(pltpu.make_async_copy(same, alike, sem.at[4]))
    if bring:
        late.append(pltpu.make_async_copy(caches.at[layer + 1], near, sem.at[5]))
    for copy in fetch:
        copy.start()

    means = jnp.sum(stats[...], axis=0) / entries
    average = means[0:1]
    variance = means[1:2] - average * average
    scale = lax.rsqrt(variance + EPSILON) * gain[layer : layer + 1, :]
    offset = shift[layer : layer + 1, :] - average * scale
    scale, offset = 0.5 * scale, 0.5 * offset
    scales = [scale[:, :LANES]] * 2 + [twice(scale[:, LANES:])]
    offsets = [offset[:, :LANES]] * 2 + [twice(offset[:, LANES:])]

    def act(values):
        return [silu_of_twice(v * a + b) for v, a, b in zip(values, scales, offsets)]

    for side, ref in enumerate((before, after)):
        values = [ref[plane].astype(jnp.float32) for plane in range(PLANES)]
        for plane, value in enumerate(act(values)):
            edges[side, plane] = value

    def row_of(h):
        if layer:
            start = h * COLS if isinstance(h, int) else pl.multiple_of(h * COLS, COLS)
            return act([x[plane, pl.ds(start, COLS), :] for plane in range(PLANES)])
        return act(planes(*(x[frame, h].astype(jnp.float32) for frame in range(2))))

    def edge_of(h, plane):
        return [edges[side, plane, pl.ds(h, COLS, stride=0), :] for side in (0, 1)]

    def keep(h, *values):
        for frame in range(2):
            main, other = values[2 * frame : 2 * frame + 2]
            whole = jnp.concatenate([main, other[:, : channels - LANES]], axis=1)
            kept[frame, h] = whole.astype(jnp.bfloat16)

    build_slabs(rows, row_of, edge_of, slabs, keep)
    copy = pltpu.make_async_copy(kept, carried.at[layer], sem.at[0])
    copy.start()
    for one in fetch:
        one.wait()
    for one in late:
        one.start()
    tables = [taps[p] for p in range(2)]
    moments = [jnp.zeros((COLS, channels), jnp.float32)] * 2

    def finish(t, start, size, value, moments):
        here, span = pl.ds(start, size), pl.ds(start // COLS, size // COLS)
        shape = (size // COLS, COLS, channels)
        value = value + get_planes(part, t, here)
        if final:
            value = value + get_planes(x, t, here)
            y[t, span] = value.reshape(shape).astype(jnp.bfloat16)
            return moments
        put_planes(y, t, here, value)
        folded = value.reshape(shape)
        return [
            moments[0] + jnp.sum(folded, axis=0),
            moments[1] + jnp.sum(folded * folded, axis=0),
        ]

    value = product([(slabs[0], tables[1])], 0, places)
    moments = finish(0, 0, places, value, moments)
    for start in range(0, places, chunk):
        value = product([(slabs[0], tables[0]), (slabs[1], tables[1])], start, chunk)
        moments = finish(1, start, chunk, value, moments)
    if not final:
        for one in late:
            one.wait()
        both = group_sums(moments, alike[...])
        sums[...] = jnp.broadcast_to(both[None], sums.shape)
        for plane in range(PLANES):
            for out, column in ((first, 0), (last, cols - 1)):
                edge = y[plane, pl.ds(column, rows, stride=cols), :]
                out[plane] = edge.astype(jnp.bfloat16)
    copy.wait()


def scratch(frames, rows, room):
    slab = pltpu.VMEM((SLABS, rows * COLS + 16, LANES), jnp.bfloat16)
    return [pltpu.VMEM((2, PLANES, rows, LANES), jnp.float32)] + room + [slab] * frames


def local(video_span, caches, norm_gains, shifts, weights, biases):
    peers = lax.axis_size("lon")
    frames, rows, cols, channels = video_span.shape
    layers = caches.shape[0]
    places = rows * cols
    entries = frames * places * peers * (channels // GROUPS)
    up = [(i, (i + 1) % peers) for i in range(peers)]
    down = [(j, i) for i, j in up]
    chunk = 720
    tiles = 14 * LANES

    def around(first, last):
        return lax.ppermute(last, "lon", up), lax.ppermute(first, "lon", down)

    def gathered(sums):
        return lax.all_to_all(sums, "lon", 0, 0)

    def in_hbm(value):
        return pltpu.with_memory_space_constraint(value, pltpu.HBM)

    turned = in_hbm(jnp.swapaxes(weights, 1, 2))
    caches, video = in_hbm(caches), in_hbm(video_span)
    members = channels // GROUPS
    alike = np.kron(np.eye(GROUPS), np.ones((members, members)))
    same = in_hbm(jnp.asarray(alike, jnp.bfloat16))
    spread = jax.ShapeDtypeStruct((peers, 2, channels), jnp.float32)
    brim = jax.ShapeDtypeStruct(((layers + 1) * PLANES, rows, LANES), jnp.bfloat16)
    block = jax.ShapeDtypeStruct(video_span.shape, video_span.dtype)
    sums, first, last, cache = pl.pallas_call(
        begin_kernel,
        out_shape=[spread, brim, brim, block],
        in_specs=[HBM] * 3,
        out_specs=[VMEM] * 4,
        scratch_shapes=[
            pltpu.VMEM((PLANES, places, LANES), jnp.float32),
            pltpu.VMEM((layers + 1,) + video_span.shape, jnp.bfloat16),
            pltpu.VMEM(same.shape, same.dtype),
            pltpu.SemaphoreType.DMA((layers + 2,)),
        ],
        compiler_params=pltpu.CompilerParams(vmem_limit_bytes=24 << 20),
        name="begin",
    )(video, caches, same)
    brims = around(first, last)
    before, after = brims
    stats = gathered(sums)

    def room(far):
        return [pltpu.VMEM((PLANES, places, LANES), jnp.float32)] if far else []

    def cached_part(layer, far, cache, brims):
        own = [pltpu.VMEM(video_span.shape, jnp.bfloat16)] * 2 if layer == 1 else []
        later = pltpu.HBM(((layers - 2) * PLANES, rows, LANES), jnp.bfloat16)
        more = {0: [block], 1: [later] * 2}.get(layer, [])
        planar = pltpu.HBM if far else jax.ShapeDtypeStruct
        return pl.pallas_call(
            functools.partial(cached_kernel, layer, chunk, far),
            out_shape=[
                planar((PLANES, places, LANES), jnp.float32),
                pltpu.HBM((2, channels, tiles), weights.dtype),
            ]
            + more,
            in_specs=[HBM if cache is None else VMEM, VMEM, VMEM, HBM, VMEM]
            + ([HBM] if layer < 2 else []),
            out_specs=[HBM if far else VMEM, HBM] + [HBM if layer else VMEM] * len(more),
            scratch_shapes=own + scratch(frames, rows, room(far))
            + [
                pltpu.VMEM((channels, weights.shape[1]), weights.dtype),
                pltpu.VMEM((3, channels, tiles), weights.dtype),
                pltpu.SemaphoreType.DMA((7,)),
            ],
            compiler_params=pltpu.CompilerParams(vmem_limit_bytes=24 << 20),
            name="cached",
        )(caches if cache is None else cache, *brims, turned, biases, *([video] if layer < 2 else []))

    x = None
    carried = None
    for layer in range(layers):
        final = layer == layers - 1
        far = layer < layers - 1
        bring = 0 < layer < layers - 1
        part, ordered, *more = cached_part(layer, far, cache, brims)
        if layer == 0:
            x = more[0]
        elif more:
            brims = more
        if far:
            part = in_hbm(part)
        operands = [x, before, after, stats, norm_gains, shifts, in_hbm(ordered), part, same]
        specs = [VMEM] * 6 + [HBM, HBM if far else VMEM, HBM]
        aliases = {}
        if layer > 0:
            aliases = {len(operands): 1}
            operands.append(carried)
            specs.append(HBM)
        state = jax.ShapeDtypeStruct((PLANES, places, LANES), jnp.float32)
        if final:
            state = jax.ShapeDtypeStruct(video_span.shape, jnp.bfloat16)
        outs = [state, jax.ShapeDtypeStruct(caches.shape, jnp.bfloat16)]
        out_specs = [VMEM, HBM]
        if not final:
            edge = jax.ShapeDtypeStruct((PLANES, rows, LANES), jnp.bfloat16)
            outs += [spread, edge, edge]
            out_specs += [VMEM] * 3
        if bring:
            outs.append(block)
            out_specs.append(VMEM)
            operands.append(caches)
            specs.append(HBM)
        results = pl.pallas_call(
            functools.partial(active_kernel, layer, chunk, far, bring, entries, final),
            out_shape=outs,
            in_specs=specs,
            out_specs=out_specs,
            scratch_shapes=scratch(frames, rows, room(far))
            + [
                pltpu.VMEM(video_span.shape, jnp.bfloat16),
                pltpu.VMEM((2, channels, tiles), weights.dtype),
                pltpu.VMEM(same.shape, same.dtype),
                pltpu.SemaphoreType.DMA((6,)),
            ],
            compiler_params=pltpu.CompilerParams(vmem_limit_bytes=24 << 20),
            input_output_aliases=aliases,
            name="active",
        )(*operands)
        x, carried = results[:2]
        if not final:
            stats = gathered(results[2])
            before, after = around(results[3], results[4])
            cache = results[5] if bring else None
    return x, carried


def solution(mesh):
    return jax.shard_map(
        local,
        mesh=mesh,
        in_specs=(
            P(None, "clips", "lon", None),
            P(None, None, "clips", "lon", None),
            P(),
            P(),
            P(),
            P(),
        ),
        out_specs=(P(None, "clips", "lon", None), P(None, None, "clips", "lon", None)),
        check_vma=False,
    )
```
